32 devices in a mesh: rep: 4 (over y, x), shard: 8 (over z, core).
Axes of the slice: x: 2, y: 2, z: 4, core: 2. Of those that a mesh axis runs over, the one named last changes fastest.
Arguments:
- tokens: bfloat16 [32768, 768], P(('rep', 'shard')), may hold values from -6 to 6
- cotangent: bfloat16 [32768, 768], P(('rep', 'shard')), may hold values from -6 to 6
- qkv_weight: bfloat16 [768, 2304], P('shard'), may hold values from -0.21875 to 0.21875
- query_value_bias: bfloat16 [2, 768], P(None, 'shard'), may hold values from -3 to 3
- out_weight: bfloat16 [768, 768], P('shard'), may hold values from -0.875 to 0.875
- out_bias: bfloat16 [768], P('shard'), may hold values from -2 to 2
- norm_one_gain: bfloat16 [768], P('shard'), may hold values from 0.099609375 to 1.8984375
- norm_one_shift: bfloat16 [768], P('shard'), may hold values from -2 to 2
- up_weight: bfloat16 [768, 3072], P('shard'), may hold values from -0.21875 to 0.21875
- up_bias: bfloat16 [3072], P('shard'), may hold values from -3 to 3
- down_weight: bfloat16 [3072, 768], P('shard'), may hold values from -0.109375 to 0.109375
- down_bias: bfloat16 [768], P('shard'), may hold values from -2 to 2
- norm_two_gain: bfloat16 [768], P('shard'), may hold values from 0.099609375 to 1.8984375
- norm_two_shift: bfloat16 [768], P('shard'), may hold values from -2 to 2
- segment_ids: int32 [64, 512], P(('rep', 'shard')), may hold values from 0 to 7, never falling along the last dimension, each value on 1 to 256 neighbouring positions
- valid: int32 [64, 512], P(('rep', 'shard')), may hold values from 0 to 1, as said below
Outputs:
- layer_output: bfloat16 [32768, 768], P(('rep', 'shard'))
- input_grad: bfloat16 [32768, 768], P(('rep', 'shard'))
- grad_qkv_weight: float32 [768, 2304], P('shard')
- grad_query_value_bias: float32 [2, 768], P(None, 'shard')
- grad_out_weight: float32 [768, 768], P('shard')
- grad_out_bias: float32 [768], P('shard')
- grad_norm_one_gain: float32 [768], P('shard')
- grad_norm_one_shift: float32 [768], P('shard')
- grad_up_weight: float32 [768, 3072], P('shard')
- grad_up_bias: float32 [3072], P('shard')
- grad_down_weight: float32 [3072, 768], P('shard')
- grad_down_bias: float32 [768], P('shard')
- grad_norm_two_gain: float32 [768], P('shard')
- grad_norm_two_shift: float32 [768], P('shard')
The draws below stay inside these ranges and needn't reach their ends.
Inputs may be any that keep to these rules, and one draw needn't show every extreme that they name: `segment_ids`: within each sequence of 512 positions the numbers never fall; a document covers 1 to 256 positions, and one covers exactly 256. `valid`: in each sequence of 512 positions the tokens come first, followed by 0 to 64 padding positions.
All inputs are finite; a program needn't handle non-finite values.
Results may differ from the reference program's by a relative error of at most 0.015.
Values may be sent and summed in bfloat16 or wider, within the bound.
No kernel may reach another device: no remote copies, remote signals or barrier semaphores. Data moves between devices by JAX's collectives and lax.ppermute only.
A program may use at most 192 MiB of HBM per device.

```python
import math
import jax
import jax.numpy as jnp
import numpy as np
from jax import lax

D = 768
H = 12
HD = 64
FF = 3072
SEQ = 512
SEQS = 64
TOKENS = 32768


def draw_valid(key, part):
    pad_counts = jax.random.randint(key, (SEQS, 1), 0, SEQ // 8 + 1)
    positions = jnp.arange(SEQ, dtype=jnp.int32)[None, :]
    return (positions < SEQ - pad_counts).astype(jnp.int32)


def steps_of(stream_key, shape, pieces, least, high):
    factor_of = 1.0
    for axis_at, blocks in pieces:
        draws = jax.random.uniform(jax.random.fold_in(jax.random.fold_in(stream_key, 6), axis_at), (blocks,), jnp.float32, least / len(pieces), high / len(pieces))
        factor_of = factor_of * jnp.repeat(jnp.exp(draws), shape[axis_at] // blocks).reshape((-1,) + (1,) * (len(shape) - 1 - axis_at))
    return factor_of


def split_up(count, total, bound, slope):
    loads = [(1 << 20) // math.isqrt(grade ** slope) + 1 for grade in range(2, count + 1)]
    rest, counts = total - bound - (count - 1), [1] * (count - 1)
    while rest > 0:
        candidates = [i for i in range(count - 1) if counts[i] < bound]
        mass, budget = sum([loads[i] for i in candidates]), rest
        for i in candidates:
            more = min(bound - counts[i], max(1, budget * loads[i] // mass), rest)
            counts[i] = counts[i] + more
            rest = rest - more
    return np.array([bound] + counts)


def uneven(key, count, total, most, slope):
    if count == 2:
        one = jax.random.randint(key, (), max(1, total - most), min(most, total - 1) + 1)
        return jnp.stack([one, total - one])
    tallies = jnp.asarray(split_up(count, total, most, slope), jnp.int32)
    pairs = (count - 1) // 2
    giver, receiver = tallies[1:1 + 2 * pairs:2], tallies[2:2 + 2 * pairs:2]
    slack = jnp.minimum(giver - 1, most - receiver)
    passed = jax.random.randint(jax.random.fold_in(key, 1), (pairs,), 0, 1 << 20) % (slack + 1)
    tallies = tallies.at[1:1 + 2 * pairs:2].set(giver - passed).at[2:2 + 2 * pairs:2].set(receiver + passed)
    return tallies[jax.random.permutation(jax.random.fold_in(key, 2), count)]


def noise(stream_key, dims, width, bound, pieces=(), kind=jnp.bfloat16):
    drawn = width * jax.random.normal(stream_key, dims, jnp.float32)
    if pieces:
        drawn = drawn * steps_of(stream_key, dims, pieces, -0.22, 0.18)
    return jnp.clip(drawn, -bound, bound).astype(kind)


def setup_inputs(seed: int = 0) -> dict:
    key_of = jax.random.split(jax.random.key(seed), 17)
    return {
        "tokens": noise(key_of[0], (TOKENS, D), 1.0, 6.0, ((0, 32),)),
        "cotangent": noise(key_of[1], (TOKENS, D), 1.0, 6.0, ((0, 32),)),
        "qkv_weight": noise(key_of[2], (D, 3 * D), D ** -0.5, 0.21875, ((0, 8),)),
        "query_value_bias": noise(key_of[3], (2, D), 0.5, 3.0, ((1, 8),)),
        "out_weight": noise(key_of[4], (D, D), (D // 16) ** -0.5, 0.875, ((0, 8),)),
        "out_bias": noise(key_of[5], (D,), 0.3, 2.0, ((0, 8),)),
        "norm_one_gain": jnp.clip(1.0 + 0.18 * jax.random.normal(key_of[6], (D,), jnp.float32), 0.099609375, 1.8984375).astype(jnp.bfloat16),
        "norm_one_shift": noise(key_of[7], (D,), 0.3, 2.0, ((0, 8),)),
        "up_weight": noise(key_of[8], (D, FF), D ** -0.5, 0.21875, ((0, 8),)),
        "up_bias": noise(key_of[9], (FF,), 0.5, 3.0, ((0, 8),)),
        "down_weight": noise(key_of[10], (FF, D), FF ** -0.5, 0.109375, ((0, 8),)),
        "down_bias": noise(key_of[11], (D,), 0.3, 2.0, ((0, 8),)),
        "norm_two_gain": jnp.clip(1.0 + 0.18 * jax.random.normal(key_of[12], (D,), jnp.float32), 0.099609375, 1.8984375).astype(jnp.bfloat16),
        "norm_two_shift": noise(key_of[13], (D,), 0.3, 2.0, ((0, 8),)),
        "segment_ids": jax.vmap(lambda own: jnp.searchsorted(jnp.cumsum(uneven(own, max(4, SEQ // 64), SEQ, SEQ // 2, 2)), jnp.arange(SEQ), side="right"))(jax.random.split(key_of[14], SEQS)).reshape((SEQS, SEQ)).astype(jnp.int32),
        "valid": draw_valid(jax.random.fold_in(key_of[16], 71), 0),
    }


@jax.custom_vjp
def low(v):
    return lax.optimization_barrier(v.astype(jnp.bfloat16)).astype(jnp.float32)

@jax.custom_vjp
def low_back(v):
    return v

def low_keep(v):
    return (low(v), None)

def low_pass(kept, grad):
    return (grad,)

def back_keep(v):
    return (v, None)

def back_low(kept, grad):
    return (low(grad),)
low.defvjp(low_keep, low_pass)
low_back.defvjp(back_keep, back_low)
precise = lax.Precision.HIGHEST

def layer_norm(values, gain_vec, shift_vec):
    centre = values - lax.optimization_barrier(jnp.mean(values, axis=-1, keepdims=True))
    spread = lax.optimization_barrier(jnp.mean(centre * centre, axis=-1, keepdims=True))
    return centre * lax.rsqrt(spread + 1e-05) * gain_vec + shift_vec

def attend_sequence(packed):
    queries, key_rows, value_rows, seg_row, valid_row = packed
    allowed = (seg_row[:, None] == seg_row[None, :]) & (valid_row[:, None] == valid_row[None, :])
    scores = jnp.einsum('qhd,khd->hqk', queries, key_rows, precision=precise) * 0.125
    scores = low_back(scores)
    scores = jnp.where(allowed[None], scores, -1e+30)
    row_top = lax.optimization_barrier(jnp.max(scores, axis=-1, keepdims=True))
    shifted_exp = jnp.exp(scores - row_top)
    probabilities = shifted_exp / lax.optimization_barrier(jnp.sum(shifted_exp, axis=-1, keepdims=True))
    probabilities = low(probabilities)
    return jnp.einsum('hqk,khd->qhd', probabilities, value_rows, precision=precise)

def forward(inputs, seg_block, valid_block, params):
    qkv_weight, query_value_bias, out_weight, out_bias, norm_one_gain, norm_one_shift, up_weight, up_bias, down_weight, down_bias, norm_two_gain, norm_two_shift = params
    groups, length, model_width = inputs.shape
    bias_all = jnp.concatenate([query_value_bias[0], jnp.zeros((model_width,), jnp.float32), query_value_bias[1]])
    projected = jnp.einsum('gtd,de->gte', inputs, qkv_weight, precision=precise) + bias_all
    projected = low(low_back(projected))
    split_heads = projected.reshape(groups, length, 3, H, HD)
    attended = lax.map(jax.checkpoint(attend_sequence), (split_heads[:, :, 0], split_heads[:, :, 1], split_heads[:, :, 2], seg_block, valid_block))
    context = low(low_back(attended.reshape(groups, length, model_width)))
    branch = low_back(jnp.einsum('gtd,de->gte', context, out_weight, precision=precise) + out_bias)
    normed = layer_norm(inputs + branch, norm_one_gain, norm_one_shift)
    hidden_pre = low_back(jnp.einsum('gtd,df->gtf', low(normed), up_weight, precision=precise) + up_bias)
    hidden = low(jax.nn.gelu(hidden_pre, approximate=False))
    branch_two = low_back(jnp.einsum('gtf,fd->gtd', hidden, down_weight, precision=precise) + down_bias)
    return layer_norm(normed + branch_two, norm_two_gain, norm_two_shift)

def reference(tokens, cotangent, qkv_weight, query_value_bias, out_weight, out_bias, norm_one_gain, norm_one_shift, up_weight, up_bias, down_weight, down_bias, norm_two_gain, norm_two_shift, segment_ids, valid):
    params = tuple((param.astype(jnp.float32) for param in (qkv_weight, query_value_bias, out_weight, out_bias, norm_one_gain, norm_one_shift, up_weight, up_bias, down_weight, down_bias, norm_two_gain, norm_two_shift)))
    group_size = math.gcd(SEQS, max(1, 4096 // SEQ))
    block_count = SEQS // group_size
    token_blocks = tokens.astype(jnp.float32).reshape(block_count, group_size, SEQ, D)
    cot_blocks = cotangent.astype(jnp.float32).reshape(block_count, group_size, SEQ, D)
    seg_blocks = segment_ids.reshape(block_count, group_size, SEQ)
    valid_blocks = valid.reshape(block_count, group_size, SEQ)

    def scan_step(totals, packed):
        token_block, cot_block, seg_block, valid_block = packed

        def apply_layer(inputs, weights):
            return forward(inputs, seg_block, valid_block, weights)
        result, pullback = jax.vjp(apply_layer, token_block, params)
        input_grad, weight_grads = pullback(cot_block)
        totals = tuple((summed + added for summed, added in zip(totals, weight_grads)))
        return (totals, (result.astype(jnp.bfloat16), input_grad.astype(jnp.bfloat16)))
    zero_grads = tuple((jnp.zeros(param.shape, jnp.float32) for param in params))
    totals, (results, input_grads) = lax.scan(scan_step, zero_grads, (token_blocks, cot_blocks, seg_blocks, valid_blocks))
    return (results.reshape(TOKENS, D), input_grads.reshape(TOKENS, D), totals[0], totals[1], totals[2], totals[3], totals[4], totals[5], totals[6], totals[7], totals[8], totals[9], totals[10], totals[11])
```

```python
import jax
import jax.numpy as jnp
from jax import lax
from jax.experimental import pallas as pl
from jax.experimental.pallas import tpu as pltpu
from jax.sharding import PartitionSpec as P

HD = 64
GW = 256
SCALE = 0.125 * 1.4426950408889634
BIG = 1e30
VMEM_LIMIT = 60 * 1024 * 1024
bf16 = jnp.bfloat16
f32 = jnp.float32


def nn(a, b):
    return lax.dot_general(a, b, (((1,), (0,)), ((), ())), preferred_element_type=f32)


def nt(a, b):
    return lax.dot_general(a, b, (((1,), (1,)), ((), ())), preferred_element_type=f32)


def tn(a, b):
    return lax.dot_general(a, b, (((0,), (0,)), ((), ())), preferred_element_type=f32)


def attend_kernel(tok, wq, wk, wv, bq, bv, aq, ak, q_o, k_o, v_o, ctx_o, lse_o):
    x = tok[...]
    q = (nn(x, wq[...]) + bq[...].astype(f32)).astype(bf16)
    k = nn(x, wk[...]).astype(bf16)
    v = (nn(x, wv[...]) + bv[...].astype(f32)).astype(bf16)
    q_o[...] = q
    k_o[...] = k
    v_o[...] = v
    length, width = q.shape
    lane = lax.broadcasted_iota(jnp.int32, (length, width), 1) // HD
    slot = lax.broadcasted_iota(jnp.int32, (length, 128), 1)
    acc = None
    scale = jnp.zeros((length, width), f32)
    stat = jnp.zeros((length, 128), f32)
    for h in range(width // HD):
        mine = lane == h
        qa = jnp.where(mine, q, aq[...])
        ka = jnp.where(mine, k, ak[...])
        va = jnp.where(mine, v, jnp.zeros_like(v))
        t = nt(qa, ka) * SCALE
        m = jnp.max(t, axis=1, keepdims=True)
        p = jnp.exp2(t - m)
        total = jnp.sum(p, axis=1, keepdims=True)
        part = nn(p.astype(bf16), va)
        acc = part if acc is None else acc + part
        scale = jnp.where(mine, 1.0 / total, scale)
        stat = jnp.where(slot == h, m + jnp.log2(total), stat)
    ctx_o[...] = (acc * scale).astype(bf16)
    lse_o[0, 0] = stat.T[:8]


def attend(tokens, w, bias, aq, ak, length):
    rows, width = tokens.shape
    groups = width // GW
    seqs = rows // length
    col = lambda o: pl.BlockSpec((width, GW), lambda g, b: (0, o * groups + g))
    bcol = lambda o: pl.BlockSpec((1, GW), lambda g, b: (0, o * groups + g))
    seq = pl.BlockSpec((length, width), lambda g, b: (b, 0))
    aug = pl.BlockSpec((length, GW), lambda g, b: (b, 0))
    blk = pl.BlockSpec((length, GW), lambda g, b: (b, g))
    act = jax.ShapeDtypeStruct((rows, width), bf16)
    return pl.pallas_call(
        attend_kernel,
        grid=(groups, seqs),
        in_specs=[seq, col(0), col(1), col(2), bcol(0), bcol(1), aug, aug],
        out_specs=[blk, blk, blk, blk, pl.BlockSpec((1, 1, 8, length), lambda g, b: (b, g, 0, 0))],
        out_shape=[act, act, act, act, jax.ShapeDtypeStruct((seqs, groups, 8, length), f32)],
        compiler_params=pltpu.CompilerParams(vmem_limit_bytes=VMEM_LIMIT),
        name="attend",
    )(tokens, w, w, w, bias, bias, aq, ak)


def attend_back_kernel(q_r, k_r, v_r, do_r, ctx_r, lse_r, aq, ak, tok, wq, wk, wv, gb, dw_o, db_o, dx_o, dw_s, dx_s):
    g, b = pl.program_id(0), pl.program_id(1)
    q, k, v, do = q_r[...], k_r[...], v_r[...], do_r[...]
    length, width = q.shape
    lane = lax.broadcasted_iota(jnp.int32, (length, width), 1) // HD
    sel = lax.broadcasted_iota(jnp.int32, (8, width), 1) // HD == lax.broadcasted_iota(jnp.int32, (8, width), 0)
    sel = sel.astype(f32).astype(bf16)
    prod = do.astype(f32) * ctx_r[...].astype(f32)
    hi = prod.astype(bf16)
    lo = (prod - hi.astype(f32)).astype(bf16)
    delta = nt(sel, hi) + nt(sel, lo)
    dq = dk = dv = None
    zero = jnp.zeros_like(q)
    for h in range(width // HD):
        mine = lane == h
        qa = jnp.where(mine, q, aq[...])
        ka = jnp.where(mine, k, ak[...])
        va = jnp.where(mine, v, zero)
        p = jnp.exp2(nt(ka, qa) * SCALE - lse_r[0, 0, h : h + 1, :])
        dp = nt(va, do)
        ds = (p * (dp - delta[h : h + 1, :])).astype(bf16)
        dv_h = nn(p.astype(bf16), jnp.where(mine, do, zero))
        dk_h = nn(ds, jnp.where(mine, q, zero))
        dq_h = tn(ds, jnp.where(mine, k, zero))
        dv = dv_h if dv is None else dv + dv_h
        dk = dk_h if dk is None else dk + dk_h
        dq = dq_h if dq is None else dq + dq_h
    dq = (dq * 0.125).astype(bf16)
    dk = (dk * 0.125).astype(bf16)
    dv = dv.astype(bf16)
    back = jnp.concatenate([dq, dk, dv], axis=1)
    dw = tn(tok[...], back)
    dx = nt(dq, wq[...]) + nt(dk, wk[...]) + nt(dv, wv[...])
    sums = jnp.sum(back.astype(f32), axis=0, keepdims=True)

    @pl.when(b == 0)
    def _():
        dw_s[...] = dw
        db_o[0] = sums

    @pl.when(b > 0)
    def _():
        dw_s[...] += dw
        db_o[0] += sums

    @pl.when(g == 0)
    def _():
        dx_s[b] = dx + gb[...].astype(f32)

    @pl.when(g > 0)
    def _():
        dx_s[b] += dx

    @pl.when(b == pl.num_programs(1) - 1)
    def _():
        for i in range(3):
            dw_o[i] = dw_s[:, i * width : (i + 1) * width].astype(bf16)

    @pl.when(g == pl.num_programs(0) - 1)
    def _():
        dx_o[...] = dx_s[b].astype(bf16)


def attend_back(q, k, v, do, ctx, lse, aq, ak, tokens, w, gb, length):
    rows, width = tokens.shape
    groups = width // GW
    seqs = rows // length
    col = lambda o: pl.BlockSpec((width, GW), lambda g, b: (0, o * groups + g))
    seq = pl.BlockSpec((length, width), lambda g, b: (b, 0))
    aug = pl.BlockSpec((length, GW), lambda g, b: (b, 0))
    blk = pl.BlockSpec((length, GW), lambda g, b: (b, g))
    return pl.pallas_call(
        attend_back_kernel,
        grid=(groups, seqs),
        in_specs=[blk, blk, blk, blk, blk, pl.BlockSpec((1, 1, 8, length), lambda g, b: (b, g, 0, 0)), aug, aug, seq,
                  col(0), col(1), col(2), seq],
        out_specs=[
            pl.BlockSpec((3, width, GW), lambda g, b: (0, 0, g)),
            pl.BlockSpec((1, 1, 3 * GW), lambda g, b: (g, 0, 0)),
            pl.BlockSpec((length, width), lambda g, b: (jnp.where(g == groups - 1, b, 0), 0)),
        ],
        out_shape=[
            jax.ShapeDtypeStruct((3, width, width), bf16),
            jax.ShapeDtypeStruct((groups, 1, 3 * GW), f32),
            jax.ShapeDtypeStruct((rows, width), bf16),
        ],
        scratch_shapes=[pltpu.VMEM((width, 3 * GW), f32), pltpu.VMEM((seqs, length, width), f32)],
        compiler_params=pltpu.CompilerParams(vmem_limit_bytes=VMEM_LIMIT),
        name="attend_back",
    )(q, k, v, do, ctx, lse, aq, ak, tokens, w, w, w, gb)


def masks(segment_ids, valid):
    code = (segment_ids + 8 * valid).reshape(-1, 1)
    lane = lax.broadcasted_iota(jnp.int32, (1, GW), 1) % HD
    same = code == lane
    aq = same.astype(bf16)
    ak = jnp.where((lane < 16) & ~same, -BIG, 0.0).astype(bf16)
    return aq, ak


def phi(x):
    return 0.5 * (1.0 + lax.erf(x * 0.7071067811865476)), jnp.exp(-0.5 * x * x) * 0.3989422804014327


def middle_kernel(tok, ctx, cot, wo, bo, g1, s1, wu, bu, wd, bd, g2, s2,
                  out_o, low_o, hid_o, gd_o, gu_o, gb_o, gc_o, vec_o, bup_o, slope):
    i = pl.program_id(0)
    width = tok.shape[1]
    ff = wu.shape[1]
    step = width
    chunks = ff // step
    row = lambda r: r[...].astype(f32)
    pre = tok[...].astype(f32) + nn(ctx[...], wo[...]) + row(bo)
    mean = lambda v: jnp.mean(v, axis=1, keepdims=True)
    centre = pre - mean(pre)
    r1 = lax.rsqrt(mean(centre * centre) + 1e-05)
    n1 = centre * r1
    normed = n1 * row(g1) + row(s1)
    low = normed.astype(bf16)
    low_o[...] = low
    acc = normed + row(bd)
    for c in range(chunks):
        cols = slice(c * step, (c + 1) * step)
        hp = nn(low, wu[:, cols]) + bu[:, cols].astype(f32)
        cdf, pdf = phi(hp)
        slope[:, cols] = cdf + hp * pdf
        hid = (hp * cdf).astype(bf16)
        hid_o[:, cols] = hid
        acc = acc + nn(hid, wd[cols, :])
    centre = acc - mean(acc)
    r2 = lax.rsqrt(mean(centre * centre) + 1e-05)
    n2 = centre * r2
    out_o[...] = (n2 * row(g2) + row(s2)).astype(bf16)
    ct = cot[...].astype(f32)
    e = ct * row(g2)
    gp2 = r2 * (e - mean(e) - n2 * mean(e * n2))
    gd = gp2.astype(bf16)
    gd_o[...] = gd
    acc = gp2
    total = lambda v: jnp.sum(v, axis=0, keepdims=True)

    def put(ref, at, v):
        @pl.when(i == 0)
        def _():
            ref[at] = v

        @pl.when(i > 0)
        def _():
            ref[at] += v

    for c in range(chunks):
        cols = slice(c * step, (c + 1) * step)
        gu = (nt(gd, wd[cols, :]) * slope[:, cols]).astype(bf16)
        gu_o[:, cols] = gu
        put(bup_o, (slice(0, 1), cols), total(gu.astype(f32)))
        acc = acc + nt(gu, wu[:, cols])
    e = acc * row(g1)
    gp1 = r1 * (e - mean(e) - n1 * mean(e * n1))
    gb = gp1.astype(bf16)
    gb_o[...] = gb
    gc_o[...] = nt(gb, wo[...]).astype(bf16)
    for at, v in enumerate((gb.astype(f32), acc * n1, acc, gd.astype(f32), ct * n2, ct)):
        put(vec_o, (slice(at, at + 1), slice(None)), total(v))


def middle(tokens, ctx, cot, wo, bo, g1, s1, wu, bu, wd, bd, g2, s2, tile=256):
    rows, width = tokens.shape
    ff = wu.shape[1]
    act = pl.BlockSpec((tile, width), lambda i: (i, 0))
    wide = pl.BlockSpec((tile, ff), lambda i: (i, 0))
    whole = lambda a: pl.BlockSpec(a.shape, lambda i: (0, 0), pipeline_mode=pl.Buffered(1))
    S = jax.ShapeDtypeStruct
    return pl.pallas_call(
        middle_kernel,
        grid=(rows // tile,),
        in_specs=[act, act, act] + [whole(a) for a in (wo, bo, g1, s1, wu, bu, wd, bd, g2, s2)],
        out_specs=[act, act, wide, act, wide, act, act, pl.BlockSpec((8, width), lambda i: (0, 0)), pl.BlockSpec((8, ff), lambda i: (0, 0))],
        out_shape=[S((rows, width), bf16), S((rows, width), bf16), S((rows, ff), bf16), S((rows, width), bf16), S((rows, ff), bf16),
                   S((rows, width), bf16), S((rows, width), bf16), S((8, width), f32), S((8, ff), f32)],
        scratch_shapes=[pltpu.VMEM((tile, ff), f32)],
        compiler_params=pltpu.CompilerParams(vmem_limit_bytes=VMEM_LIMIT),
        name="middle",
    )(tokens, ctx, cot, wo, bo, g1, s1, wu, bu, wd, bd, g2, s2)


def spread(args):
    flat = [a.reshape(-1) for a in args]
    packed = jnp.concatenate(flat)
    every = lax.all_gather(packed, "shard", axis=0)
    out, at = [], 0
    for a in args:
        part = every[:, at : at + a.size].reshape((-1,) + a.shape)
        at += a.size
        out.append(jnp.moveaxis(part, 0, -2).reshape(a.shape[:-1] + (-1,)))
    return out


def shards(
    tokens,
    cotangent,
    qkv_weight,
    query_value_bias,
    out_weight,
    out_bias,
    norm_one_gain,
    norm_one_shift,
    up_weight,
    up_bias,
    down_weight,
    down_bias,
    norm_two_gain,
    norm_two_shift,
    segment_ids,
    valid,
):
    length = segment_ids.shape[1]
    width = tokens.shape[1]
    groups = width // GW
    gather = lambda a: lax.all_gather(a, "shard", axis=0, tiled=True)
    bqv, bo, g1, s1, bu, bd, g2, s2 = spread(
        (query_value_bias, out_bias, norm_one_gain, norm_one_shift, up_bias, down_bias, norm_two_gain, norm_two_shift)
    )
    wqkv, wo, wu, wd = gather(qkv_weight), gather(out_weight), gather(up_weight), gather(down_weight)
    bias = bqv.reshape(1, -1)
    aq, ak = masks(segment_ids, valid)
    q, k, v, ctx, lse = attend(tokens, wqkv, bias, aq, ak, length)
    result, low, hid, gd, gu, gb, gc, vec, bup = middle(
        tokens, ctx, cotangent, wo, bo[None], g1[None], s1[None], wu, bu[None], wd, bd[None], g2[None], s2[None]
    )
    dwd = tn(hid, gd).astype(bf16)
    dwu = tn(low, gu).astype(bf16)
    dwo = tn(ctx, gb).astype(bf16)
    dw, db, dx = attend_back(q, k, v, gc, ctx, lse, aq, ak, tokens, wqkv, gb, length)
    dwq = jnp.concatenate([dw[0], dw[1], dw[2]], axis=1)
    db = db.reshape(groups, 3, GW).transpose(1, 0, 2).reshape(3, width)
    small = jnp.concatenate([db[0], db[2], vec[:6].reshape(-1), bup[0]])
    small = lax.psum(small.reshape(-1, 128), ("rep", "shard")).reshape(-1)

    def owned(a):
        part = lax.psum_scatter(a, "shard", scatter_dimension=0, tiled=True)
        return lax.psum(part, "rep").astype(f32)

    rank = lax.axis_index("shard")
    own = lambda at, size: lax.dynamic_slice(small, (at + rank * size,), (size,))
    piece = out_bias.shape[0]
    vecs = [own(width * i, piece) for i in range(8)]
    dbu = own(8 * width, up_bias.shape[0])
    gd_w, gu_w, go_w, gq_w = owned(dwd), owned(dwu), owned(dwo), owned(dwq)
    return (
        result,
        dx,
        gq_w,
        jnp.stack([vecs[0], vecs[1]]),
        go_w,
        vecs[2],
        vecs[3],
        vecs[4],
        gu_w,
        dbu,
        gd_w,
        vecs[5],
        vecs[6],
        vecs[7],
    )


def solution(mesh):
    rows, one = P(("rep", "shard"), None), P("shard")
    mat, two = P("shard", None), P(None, "shard")
    return jax.shard_map(
        shards,
        mesh=mesh,
        in_specs=(rows, rows, mat, two, mat, one, one, one, mat, one, mat, one, one, one, rows, rows),
        out_specs=(rows, rows, mat, two, mat, one, one, one, mat, one, mat, one, one, one),
        check_vma=False,
    )
```

```python
import functools

import jax
import jax.numpy as jnp
from jax import lax
from jax.experimental import pallas as pl
from jax.experimental.pallas import tpu as pltpu
from jax.sharding import PartitionSpec as P

HD = 64
GW = 256
SCALE = 0.125 * 1.4426950408889634
BIG = 1e30
VMEM_LIMIT = 60 * 1024 * 1024
bf16 = jnp.bfloat16
f32 = jnp.float32


def nn(a, b):
    return lax.dot_general(a, b, (((1,), (0,)), ((), ())), preferred_element_type=f32)


def nt(a, b):
    return lax.dot_general(a, b, (((1,), (1,)), ((), ())), preferred_element_type=f32)


def tn(a, b):
    return lax.dot_general(a, b, (((0,), (0,)), ((), ())), preferred_element_type=f32)


def attend_kernel(tok, wq, wk, wv, vecs, aq, ak, q_o, k_o, v_o, ctx_o, lse_o):
    x = tok[...]
    q = (nn(x, wq[...]) + vecs[0:1, :].astype(f32)).astype(bf16)
    k = nn(x, wk[...]).astype(bf16)
    v = (nn(x, wv[...]) + vecs[1:2, :].astype(f32)).astype(bf16)
    q_o[...] = q
    k_o[...] = k
    v_o[...] = v
    length, width = q.shape
    lane = lax.broadcasted_iota(jnp.int32, (length, width), 1) // HD
    slot = lax.broadcasted_iota(jnp.int32, (length, 128), 1)
    acc = None
    scale = jnp.zeros((length, width), f32)
    stat = jnp.zeros((length, 128), f32)
    for h in range(width // HD):
        mine = lane == h
        qa = jnp.where(mine, q, aq[...])
        ka = jnp.where(mine, k, ak[...])
        va = jnp.where(mine, v, jnp.zeros_like(v))
        t = nt(qa, ka) * SCALE
        m = jnp.max(t, axis=1, keepdims=True)
        p = jnp.exp2(t - m)
        total = jnp.sum(p, axis=1, keepdims=True)
        part = nn(p.astype(bf16), va)
        acc = part if acc is None else acc + part
        scale = jnp.where(mine, 1.0 / total, scale)
        stat = jnp.where(slot == h, m + jnp.log2(total), stat)
    ctx_o[...] = (acc * scale).astype(bf16)
    lse_o[0, 0] = stat.T[:8]


def attend(tokens, w, vecs, aq, ak, length):
    rows, width = tokens.shape
    groups = width // GW
    seqs = rows // length
    col = lambda o: pl.BlockSpec((width, GW), lambda g, b: (0, o * groups + g))
    seq = pl.BlockSpec((length, width), lambda g, b: (b, 0))
    aug = pl.BlockSpec((length, GW), lambda g, b: (b, 0))
    blk = pl.BlockSpec((length, GW), lambda g, b: (b, g))
    act = jax.ShapeDtypeStruct((rows, width), bf16)
    return pl.pallas_call(
        attend_kernel,
        grid=(groups, seqs),
        in_specs=[seq, col(0), col(1), col(2), pl.BlockSpec((16, GW), lambda g, b: (0, g)), aug, aug],
        out_specs=[blk, blk, blk, blk, pl.BlockSpec((1, 1, 8, length), lambda g, b: (b, g, 0, 0))],
        out_shape=[act, act, act, act, jax.ShapeDtypeStruct((seqs, groups, 8, length), f32)],
        compiler_params=pltpu.CompilerParams(vmem_limit_bytes=VMEM_LIMIT),
        cost_estimate=pl.CostEstimate(flops=20_000_000_000, bytes_accessed=12_000_000, transcendentals=0),
        name="attend",
    )(tokens, w, w, w, vecs, aq, ak)


def select_lanes(s, piece, width):
    i = lax.broadcasted_iota(jnp.int32, (128, width), 0)
    j = lax.broadcasted_iota(jnp.int32, (128, width), 1)
    return ((j == s * piece + i) & (i < piece)).astype(f32).astype(bf16)


def attend_back_kernel(rel, at_r, q_r, k_r, v_r, do_r, ctx_r, lse_r, aq, ak, tok, wq, wk, wv, gb, tbl, *rest):
    if rel:
        own_o, other_o, dx_o, dw_s, dx_s, db_o = rest
    else:
        dw_o, db_o, dx_o, dw_s, dx_s = rest
    g, b = pl.program_id(0), pl.program_id(1)
    q, k, v, do = q_r[...], k_r[...], v_r[...], do_r[...]
    length, width = q.shape
    lane = lax.broadcasted_iota(jnp.int32, (length, width), 1) // HD
    sel = lax.broadcasted_iota(jnp.int32, (8, width), 1) // HD == lax.broadcasted_iota(jnp.int32, (8, width), 0)
    sel = sel.astype(f32).astype(bf16)
    prod = do.astype(f32) * ctx_r[...].astype(f32)
    hi = prod.astype(bf16)
    lo = (prod - hi.astype(f32)).astype(bf16)
    delta = nt(sel, hi) + nt(sel, lo)
    dq = dk = dv = None
    zero = jnp.zeros_like(q)
    for h in range(width // HD):
        mine = lane == h
        qa = jnp.where(mine, q, aq[...])
        ka = jnp.where(mine, k, ak[...])
        va = jnp.where(mine, v, zero)
        p = jnp.exp2(nt(ka, qa) * SCALE - lse_r[0, 0, h : h + 1, :])
        dp = nt(va, do)
        ds = (p * (dp - delta[h : h + 1, :])).astype(bf16)
        dv_h = nn(p.astype(bf16), jnp.where(mine, do, zero))
        dk_h = nn(ds, jnp.where(mine, q, zero))
        dq_h = tn(ds, jnp.where(mine, k, zero))
        dv = dv_h if dv is None else dv + dv_h
        dk = dk_h if dk is None else dk + dk_h
        dq = dq_h if dq is None else dq + dq_h
    dq = (dq * 0.125).astype(bf16)
    dk = (dk * 0.125).astype(bf16)
    dv = dv.astype(bf16)
    back = jnp.concatenate([dq, dk, dv], axis=1)
    dw = tn(tok[...], back)
    dx = nt(dq, wq[...]) + nt(dk, wk[...]) + nt(dv, wv[...])
    sums = jnp.sum(back.astype(f32), axis=0, keepdims=True)

    @pl.when(b == 0)
    def _():
        dw_s[...] = dw
        db_o[pl.ds(0 if not rel else g, 1)] = sums[None]

    @pl.when(b > 0)
    def _():
        dw_s[...] += dw
        db_o[pl.ds(0 if not rel else g, 1)] += sums[None]

    @pl.when(g == 0)
    def _():
        dx_s[b] = dx + gb[...].astype(f32)

    @pl.when(g > 0)
    def _():
        dx_s[b] += dx

    @pl.when(b == pl.num_programs(1) - 1)
    def _():
        if not rel:
            for i in range(3):
                dw_o[i] = dw_s[:, i * width : (i + 1) * width].astype(bf16)
        else:
            scatter_rows(dw_s[...].astype(bf16), at_r, own_o, other_o, g * 48, 0, 0, 2 * 384)

    if rel:

        @pl.when((b == pl.num_programs(1) - 1) & (g == pl.num_programs(0) - 1))
        def _():
            x, z, c = at_r[1], at_r[2], at_r[3]
            dbq = jnp.concatenate([db_o[i, :, :width] for i in range(3)], axis=1)
            dbv = jnp.concatenate([db_o[i, :, 2 * width :] for i in range(3)], axis=1)
            table = jnp.concatenate([dbq, dbv, tbl[...]], axis=0).astype(bf16)
            zero16 = jnp.zeros((4, 16, 384), bf16)
            for ab in range(2):
                for h in range(2):
                    own_o[ab, h, :, 144:160, :] = zero16
                    other_o[ab, h, :, 144:160, :] = zero16
            for s in range(8):
                blk = nt(table, select_lanes(s, 96, table.shape[1])).astype(bf16)
                kk = lax.rem(s // 2 - z + 4, 4)

                @pl.when(c == s % 2)
                def _(blk=blk, kk=kk):
                    own_o[0, x, kk, 144:160, 0:128] = blk

                @pl.when(c != s % 2)
                def _(blk=blk, kk=kk):
                    other_o[0, x, kk, 144:160, 0:128] = blk

    @pl.when(g == pl.num_programs(0) - 1)
    def _():
        dx_o[...] = dx_s[b].astype(bf16)


def scatter_rows(res, at_r, own_o, other_o, row, col, lo, hi):
    y, x, z, c = at_r[0], at_r[1], at_r[2], at_r[3]
    piece = res.shape[0] // 8
    half = piece // 2
    wide = (hi - lo) // 2
    for s in range(8):
        kk = lax.rem(s // 2 - z + 4, 4)
        for ab, turn in ((0, x), (1, y)):
            part = res[s * piece + ab * half : s * piece + (ab + 1) * half]
            for h in range(2):
                val = part[:, h * wide : (h + 1) * wide]
                rel_h = lax.rem(h + turn, 2)

                @pl.when(c == s % 2)
                def _(val=val, rel_h=rel_h, kk=kk, ab=ab):
                    own_o[ab, rel_h, kk, pl.ds(row, half), pl.ds(col, wide)] = val

                @pl.when(c != s % 2)
                def _(val=val, rel_h=rel_h, kk=kk, ab=ab):
                    other_o[ab, rel_h, kk, pl.ds(row, half), pl.ds(col, wide)] = val


def attend_back(at, q, k, v, do, ctx, lse, aq, ak, tokens, w, gb, table, length, rel):
    rows, width = tokens.shape
    groups = width // GW
    seqs = rows // length
    col = lambda o: pl.BlockSpec((width, GW), lambda g, b: (0, o * groups + g))
    seq = pl.BlockSpec((length, width), lambda g, b: (b, 0))
    aug = pl.BlockSpec((length, GW), lambda g, b: (b, 0))
    blk = pl.BlockSpec((length, GW), lambda g, b: (b, g))
    dx_spec = pl.BlockSpec((length, width), lambda g, b: (jnp.where(g == groups - 1, b, 0), 0))
    dx_shape = jax.ShapeDtypeStruct((rows, width), bf16)
    scratch = [pltpu.VMEM((width, 3 * GW), f32), pltpu.VMEM((seqs, length, width), f32)]
    if rel:
        part = (2, 2, 4, 160, 384)
        out_specs = [pl.BlockSpec(part, lambda g, b: (0, 0, 0, 0, 0))] * 2 + [dx_spec]
        out_shape = [jax.ShapeDtypeStruct(part, bf16)] * 2 + [dx_shape]
        scratch = scratch + [pltpu.VMEM((groups, 1, 3 * GW), f32)]
    else:
        out_specs = [
            pl.BlockSpec((3, width, GW), lambda g, b: (0, 0, g)),
            pl.BlockSpec((1, 1, 3 * GW), lambda g, b: (g, 0, 0)),
            dx_spec,
        ]
        out_shape = [jax.ShapeDtypeStruct((3, width, width), bf16), jax.ShapeDtypeStruct((groups, 1, 3 * GW), f32), dx_shape]
    return pl.pallas_call(
        functools.partial(attend_back_kernel, rel),
        grid=(groups, seqs),
        in_specs=[pl.BlockSpec(memory_space=pltpu.SMEM), blk, blk, blk, blk, blk, pl.BlockSpec((1, 1, 8, length), lambda g, b: (b, g, 0, 0)), aug, aug, seq,
                  col(0), col(1), col(2), seq, pl.BlockSpec(table.shape, lambda g, b: (0, 0))],
        out_specs=out_specs,
        out_shape=out_shape,
        scratch_shapes=scratch,
        compiler_params=pltpu.CompilerParams(vmem_limit_bytes=VMEM_LIMIT),
        cost_estimate=pl.CostEstimate(flops=34_000_000_000, bytes_accessed=16_000_000, transcendentals=0),
        name="attend_back",
    )(at, q, k, v, do, ctx, lse, aq, ak, tokens, w, w, w, gb, table)


def masks(segment_ids, valid):
    code = (segment_ids + 8 * valid).reshape(-1, 1)
    lane = lax.broadcasted_iota(jnp.int32, (1, GW), 1) % HD
    same = code == lane
    aq = same.astype(bf16)
    ak = jnp.where((lane < 16) & ~same, -BIG, 0.0).astype(bf16)
    return aq, ak


def phi(x):
    return 0.5 * (1.0 + lax.erf(x * 0.7071067811865476)), jnp.exp(-0.5 * x * x) * 0.3989422804014327


def middle_kernel(tok, ctx, cot, wou, vecs, bu, wd,
                  out_o, low_o, hid_o, gd_o, gu_o, gb_o, gc_o, vec_o, bup_o, slope):
    i = pl.program_id(0)
    width = tok.shape[1]
    ff = wd.shape[0]
    step = width
    chunks = ff // step
    bo, g1, s1, bd, g2, s2 = (vecs[j : j + 1, :].astype(f32) for j in range(2, 8))
    up = lambda c: wou[:, (c + 1) * step : (c + 2) * step]
    pre = tok[...].astype(f32) + nn(ctx[...], wou[:, :width]) + bo
    mean = lambda v: jnp.mean(v, axis=1, keepdims=True)
    centre = pre - mean(pre)
    r1 = lax.rsqrt(mean(centre * centre) + 1e-05)
    n1 = centre * r1
    normed = n1 * g1 + s1
    low = normed.astype(bf16)
    low_o[...] = low
    acc = normed + bd
    for c in range(chunks):
        cols = slice(c * step, (c + 1) * step)
        hp = nn(low, up(c)) + bu[:, cols].astype(f32)
        cdf, pdf = phi(hp)
        slope[:, cols] = cdf + hp * pdf
        hid = (hp * cdf).astype(bf16)
        hid_o[:, cols] = hid
        acc = acc + nn(hid, wd[cols, :])
    centre = acc - mean(acc)
    r2 = lax.rsqrt(mean(centre * centre) + 1e-05)
    n2 = centre * r2
    out_o[...] = (n2 * g2 + s2).astype(bf16)
    ct = cot[...].astype(f32)
    e = ct * g2
    gp2 = r2 * (e - mean(e) - n2 * mean(e * n2))
    gd = gp2.astype(bf16)
    gd_o[...] = gd
    acc = gp2
    total = lambda v: jnp.sum(v, axis=0, keepdims=True)

    def put(ref, at, v):
        @pl.when(i == 0)
        def _():
            ref[at] = v

        @pl.when(i > 0)
        def _():
            ref[at] += v

    for c in range(chunks):
        cols = slice(c * step, (c + 1) * step)
        gu = (nt(gd, wd[cols, :]) * slope[:, cols]).astype(bf16)
        gu_o[:, cols] = gu
        put(bup_o, (slice(0, 1), cols), total(gu.astype(f32)))
        acc = acc + nt(gu, up(c))
    e = acc * g1
    gp1 = r1 * (e - mean(e) - n1 * mean(e * n1))
    gb = gp1.astype(bf16)
    gb_o[...] = gb
    gc_o[...] = nt(gb, wou[:, :width]).astype(bf16)
    for at, v in enumerate((gb.astype(f32), acc * n1, acc, gd.astype(f32), ct * n2, ct)):
        put(vec_o, (slice(at, at + 1), slice(None)), total(v))


def middle(tokens, ctx, cot, wou, vecs, bu, wd, tile=256):
    rows, width = tokens.shape
    ff = wd.shape[0]
    act = pl.BlockSpec((tile, width), lambda i: (i, 0))
    wide = pl.BlockSpec((tile, ff), lambda i: (i, 0))
    whole = lambda a: pl.BlockSpec(a.shape, lambda i: (0, 0), pipeline_mode=pl.Buffered(1))
    S = jax.ShapeDtypeStruct
    return pl.pallas_call(
        middle_kernel,
        grid=(rows // tile,),
        in_specs=[act, act, act] + [whole(a) for a in (wou, vecs, bu, wd)],
        out_specs=[act, act, wide, act, wide, act, act, pl.BlockSpec((8, width), lambda i: (0, 0)), pl.BlockSpec((8, ff), lambda i: (0, 0))],
        out_shape=[S((rows, width), bf16), S((rows, width), bf16), S((rows, ff), bf16), S((rows, width), bf16), S((rows, ff), bf16),
                   S((rows, width), bf16), S((rows, width), bf16), S((8, width), f32), S((8, ff), f32)],
        scratch_shapes=[pltpu.VMEM((tile, ff), f32)],
        compiler_params=pltpu.CompilerParams(vmem_limit_bytes=VMEM_LIMIT),
        cost_estimate=pl.CostEstimate(flops=43_000_000_000, bytes_accessed=30_000_000, transcendentals=0),
        name="middle",
    )(tokens, ctx, cot, wou, vecs, bu, wd)


def assemble_kernel(at_r, own, ring, across, along, own2, ring2, across2, along2, out):
    y, x, z, c = at_r[0], at_r[1], at_r[2], at_r[3]
    rows, cols = own.shape
    half, wide = rows // 2, cols // 2
    for turn, parts in ((c, (own, ring, across, along)), (1 - c, (own2, ring2, across2, along2))):
        mine, ringed, xs, ys = parts
        base = (2 * z + turn) * rows
        out[pl.ds(pl.multiple_of(base, 16), rows), :] = mine[...]
        for k in range(1, 4):
            base = (2 * lax.rem(z - k + 4, 4) + turn) * rows
            for ab, flip, far in ((0, x, xs), (1, y, ys)):
                at = pl.ds(pl.multiple_of(base + ab * half, 16), half)
                near = pl.multiple_of(flip * wide, 128)
                away = pl.multiple_of((1 - flip) * wide, 128)
                out[at, pl.ds(near, wide)] = ringed[k - 1, ab * half : (ab + 1) * half, :]
                out[at, pl.ds(away, wide)] = far[k - 1]


def assemble(at, parts):
    rows, cols = parts[0].shape
    vm = pl.BlockSpec(memory_space=pltpu.VMEM)
    return pl.pallas_call(
        assemble_kernel,
        in_specs=[pl.BlockSpec(memory_space=pltpu.SMEM)] + [vm] * 8,
        out_specs=vm,
        out_shape=jax.ShapeDtypeStruct((8 * rows, cols), bf16),
        compiler_params=pltpu.CompilerParams(vmem_limit_bytes=VMEM_LIMIT),
        cost_estimate=pl.CostEstimate(flops=0, bytes_accessed=32 * rows * cols, transcendentals=0),
        name="assemble",
    )(at, *parts)


def grad_down_kernel(at_r, hid, gd, own_o, other_o):
    p = pl.program_id(0)
    res = tn(hid[...], gd[...]).astype(bf16)
    rows, cols = res.shape
    half, wide = rows // 2, cols // 2
    for ab, turn in ((0, at_r[1]), (1, at_r[0])):
        for h in range(2):
            val = res[ab * half : (ab + 1) * half, h * wide : (h + 1) * wide]
            rel_h = lax.rem(h + turn, 2)

            @pl.when(p < 4)
            def _(val=val, rel_h=rel_h, ab=ab):
                other_o[ab, rel_h, lax.rem(p, 4)] = val

            @pl.when(p >= 4)
            def _(val=val, rel_h=rel_h, ab=ab):
                own_o[ab, rel_h, lax.rem(p, 4)] = val


def grad_down(at, hid, gd):
    rows, ff = hid.shape
    width = gd.shape[1]
    piece = ff // 8
    part = (2, 2, 4, piece // 2, width // 2)

    def owner(p, at_r):
        z = lax.rem(at_r[2] + lax.rem(p, 4), 4)
        return 0, 2 * z + jnp.where(p < 4, 1 - at_r[3], at_r[3])

    whole = pl.BlockSpec(part, lambda p, at_r: (0, 0, 0, 0, 0))
    return pl.pallas_call(
        grad_down_kernel,
        grid_spec=pltpu.PrefetchScalarGridSpec(
            num_scalar_prefetch=1,
            grid=(8,),
            in_specs=[pl.BlockSpec((rows, piece), owner), pl.BlockSpec((rows, width), lambda p, at_r: (0, 0))],
            out_specs=[whole, whole],
        ),
        out_shape=[jax.ShapeDtypeStruct(part, bf16)] * 2,
        compiler_params=pltpu.CompilerParams(vmem_limit_bytes=VMEM_LIMIT),
        cost_estimate=pl.CostEstimate(flops=9_000_000_000, bytes_accessed=14_000_000, transcendentals=0),
        name="grad_down",
    )(at, hid, gd)


def grad_up_kernel(at_r, ctx, gb, low, gu, own_o, other_o, turned):
    j = pl.program_id(0)
    step = gb.shape[1]
    half = pl.num_programs(0) // 2
    first = 2 * ctx.shape[1] // (2 * step)
    y, x, z, c = at_r[0], at_r[1], at_r[2], at_r[3]

    @pl.when(j == 0)
    def _():
        turned[...] = ctx[...].T

    @pl.when(j == first)
    def _():
        turned[...] = low[...].T

    def emit(rhs):
        res = nn(turned[...], rhs[...]).astype(bf16)
        piece = res.shape[0] // 8
        rows = piece // 2
        h = j // half
        col = pl.multiple_of(lax.rem(j, half) * step, 128)
        for s in range(8):
            kk = lax.rem(s // 2 - z + 4, 4)
            for ab, turn in ((0, x), (1, y)):
                val = res[s * piece + ab * rows : s * piece + (ab + 1) * rows]
                rel_h = lax.rem(h + turn, 2)

                @pl.when(c == s % 2)
                def _(val=val, rel_h=rel_h, kk=kk, ab=ab):
                    own_o[ab, rel_h, kk, :, pl.ds(col, step)] = val

                @pl.when(c != s % 2)
                def _(val=val, rel_h=rel_h, kk=kk, ab=ab):
                    other_o[ab, rel_h, kk, :, pl.ds(col, step)] = val

    @pl.when(j < first)
    def _():
        emit(gb)

    @pl.when(j >= first)
    def _():
        emit(gu)


def grad_up(at, ctx, gb, low, gu):
    rows, width = gb.shape
    ff = gu.shape[1]
    step = width // 2
    steps = (width + ff) // step
    part = (2, 2, 4, width // 16, (width + ff) // 2)
    act = pl.BlockSpec((rows, width), lambda j: (0, 0))
    whole = pl.BlockSpec(part, lambda j: (0, 0, 0, 0, 0))
    return pl.pallas_call(
        grad_up_kernel,
        grid=(steps,),
        in_specs=[
            pl.BlockSpec(memory_space=pltpu.SMEM),
            act,
            pl.BlockSpec((rows, step), lambda j: (0, jnp.minimum(j, 1))),
            act,
            pl.BlockSpec((rows, step), lambda j: (0, jnp.maximum(j - 2, 0))),
        ],
        out_specs=[whole, whole],
        out_shape=[jax.ShapeDtypeStruct(part, bf16)] * 2,
        scratch_shapes=[pltpu.VMEM((width, rows), bf16)],
        compiler_params=pltpu.CompilerParams(vmem_limit_bytes=VMEM_LIMIT),
        cost_estimate=pl.CostEstimate(flops=11_000_000_000, bytes_accessed=16_000_000, transcendentals=0),
        name="grad_up",
    )(at, ctx, gb, low, gu)


AXES = ("rep", "shard")


def pairs(move):
    found = []
    for y in range(2):
        for x in range(2):
            for z in range(4):
                for c in range(2):
                    j, i, k, d = move(y, x, z, c)
                    found.append(((y * 2 + x) * 8 + z * 2 + c, (j * 2 + i) * 8 + k * 2 + d))
    return found


CORE = pairs(lambda y, x, z, c: (y, x, z, 1 - c))
ACROSS = pairs(lambda y, x, z, c: (y, 1 - x, z, c))
ALONG = pairs(lambda y, x, z, c: (1 - y, x, z, c))
RING = pairs(lambda y, x, z, c: (y, x, (z + 1) % 4, c))


def send(a, where):
    return lax.ppermute(a, AXES, where)


def fetch(w, x, y):
    rows, cols = w.shape
    half, wide = rows // 2, cols // 2
    a = lax.dynamic_slice(w[:half], (0, x * wide), (half, wide))
    b = lax.dynamic_slice(w[half:], (0, y * wide), (half, wide))
    held = jnp.concatenate([a, b], axis=0)
    ring = []
    for _ in range(3):
        held = send(held, RING)
        ring.append(held)
    ring = jnp.stack(ring)
    far_x = send(ring[:, :half], ACROSS)
    far_y = send(ring[:, half:], ALONG)
    return [w, ring, far_x, far_y] + [send(t, CORE) for t in (w, ring, far_x, far_y)]


def total(*terms):
    out = terms[0].astype(f32)
    for t in terms[1:]:
        out = out + t.astype(f32)
    return out.astype(bf16)


def reduce(own, other):
    got = send(other, CORE)
    far_x = send(total(own[0, 1], got[0, 1]), ACROSS)
    far_y = send(total(own[1, 1], got[1, 1]), ALONG)
    a = total(own[0, 0], got[0, 0], far_x)
    b = total(own[1, 0], got[1, 0], far_y)
    held = jnp.stack([a[3], b[3]])
    for k in (2, 1, 0):
        held = send(held, RING)
        held = total(held, jnp.stack([a[k], b[k]]))
    a, b = held[0], held[1]
    a = total(a, send(a, ALONG))
    b = total(b, send(b, ACROSS))
    return a, send(a, ACROSS), b, send(b, ALONG)


def finish_kernel(kind, at_r, a, a2, b, b2, *outs):
    y, x = at_r[0], at_r[1]
    for ab, turn, near, far in ((0, x, a, a2), (1, y, b, b2)):
        one, two = near[...].astype(f32), far[...].astype(f32)
        left = jnp.where(turn == 0, one, two)
        right = jnp.where(turn == 0, two, one)
        if kind == "down":
            half = left.shape[0]
            outs[0][ab * half : (ab + 1) * half, :] = jnp.concatenate([left, right], axis=1)
        elif kind == "up":
            half = left.shape[0]
            at = slice(ab * half, (ab + 1) * half)
            both = jnp.concatenate([left, right], axis=1)
            width = outs[0].shape[1]
            outs[0][at, :] = both[:, :width]
            outs[1][at, :] = both[:, width:]
        else:
            half = outs[0].shape[0] // 2
            at = slice(ab * half, (ab + 1) * half)
            width = outs[0].shape[1] // 3
            for g in range(width // GW):
                both = jnp.concatenate([left[g * half : (g + 1) * half], right[g * half : (g + 1) * half]], axis=1)
                for i in range(3):
                    outs[0][at, i * width + g * GW : i * width + (g + 1) * GW] = both[:, i * GW : (i + 1) * GW]
            if ab == 0:
                outs[1][...] = left[3 * half :, :128]


def finish(at, kind, blocks, shapes):
    vm = pl.BlockSpec(memory_space=pltpu.VMEM)
    return pl.pallas_call(
        functools.partial(finish_kernel, kind),
        in_specs=[pl.BlockSpec(memory_space=pltpu.SMEM)] + [vm] * 4,
        out_specs=[vm] * len(shapes),
        out_shape=[jax.ShapeDtypeStruct(s, f32) for s in shapes],
        compiler_params=pltpu.CompilerParams(vmem_limit_bytes=VMEM_LIMIT),
        cost_estimate=pl.CostEstimate(flops=0, bytes_accessed=4_000_000, transcendentals=0),
        name="finish_" + kind,
    )(at, *blocks)


def pack(vectors, wide):
    block = jnp.concatenate([v.reshape(-1, vectors[1].shape[0]) for v in vectors] + [wide.reshape(4, -1)], axis=0)
    return jnp.pad(block, ((0, 16 - block.shape[0]), (0, 128 - block.shape[1])))


def fetch_vectors(block, z, c):
    piece = 96
    ring = [block]
    for _ in range(3):
        ring.append(send(ring[-1], RING))
    ring = jnp.stack(ring)
    every = jnp.stack([ring, send(ring, CORE)])
    k = lax.broadcasted_iota(jnp.int32, (2, 4, 8), 1)
    d = lax.broadcasted_iota(jnp.int32, (2, 4, 8), 0)
    s = lax.broadcasted_iota(jnp.int32, (2, 4, 8), 2)
    pick = (s == 2 * ((z - k) % 4) + (c + d) % 2).astype(bf16)
    table = jnp.einsum("dks,dkrl->srl", pick, every, preferred_element_type=f32).astype(bf16)
    table = table[:, :, :piece]
    wide = table[:, 8:12].reshape(1, -1)
    return table.transpose(1, 0, 2).reshape(16, -1), wide


def shards_near(
    tokens,
    cotangent,
    qkv_weight,
    query_value_bias,
    out_weight,
    out_bias,
    norm_one_gain,
    norm_one_shift,
    up_weight,
    up_bias,
    down_weight,
    down_bias,
    norm_two_gain,
    norm_two_shift,
    segment_ids,
    valid,
):
    length = segment_ids.shape[1]
    width = tokens.shape[1]
    r, s = lax.axis_index("rep"), lax.axis_index("shard")
    y, x, z, c = r // 2, r % 2, s // 2, s % 2
    at = jnp.stack([y, x, z, c]).astype(jnp.int32)
    block = pack(
        (query_value_bias, out_bias, norm_one_gain, norm_one_shift, down_bias, norm_two_gain, norm_two_shift), up_bias
    )
    vecs, bu = fetch_vectors(block, z, c)
    wqkv = assemble(at, fetch(qkv_weight, x, y))
    aq, ak = masks(segment_ids, valid)
    q, k, v, ctx, lse = attend(tokens, wqkv, vecs, aq, ak, length)
    wou = assemble(at, fetch(jnp.concatenate([out_weight, up_weight], axis=1), x, y))
    wd = assemble(at, fetch(down_weight, x, y))
    result, low, hid, gd, gu, gb, gc, vec, bup = middle(tokens, ctx, cotangent, wou, vecs, bu, wd)
    down = reduce(*grad_down(at, hid, gd))
    up = reduce(*grad_up(at, ctx, gb, low, gu))
    wide = bup[0].reshape(8, 4, 96).transpose(1, 0, 2).reshape(4, width)
    table = jnp.concatenate([vec[:6], wide, jnp.zeros((4, width), f32)], axis=0)
    own, other, dx = attend_back(at, q, k, v, gc, ctx, lse, aq, ak, tokens, wqkv, gb, table, length, True)
    qkv = reduce(own, other)
    (dwd,) = finish(at, "down", down, [down_weight.shape])
    dwo, dwu = finish(at, "up", up, [out_weight.shape, up_weight.shape])
    dwq, small = finish(at, "qkv", qkv, [qkv_weight.shape, (16, 128)])
    piece = out_bias.shape[0]
    one = lambda i: small[i, :piece]
    return (
        result,
        dx,
        dwq,
        small[:2, :piece],
        dwo,
        one(2),
        one(3),
        one(4),
        dwu,
        small[8:12, :piece].reshape(-1),
        dwd,
        one(5),
        one(6),
        one(7),
    )


def spread(args):
    flat = [a.reshape(-1) for a in args]
    packed = jnp.concatenate(flat)
    every = lax.all_gather(packed, "shard", axis=0)
    out, at = [], 0
    for a in args:
        part = every[:, at : at + a.size].reshape((-1,) + a.shape)
        at += a.size
        out.append(jnp.moveaxis(part, 0, -2).reshape(a.shape[:-1] + (-1,)))
    return out


def shards(
    tokens,
    cotangent,
    qkv_weight,
    query_value_bias,
    out_weight,
    out_bias,
    norm_one_gain,
    norm_one_shift,
    up_weight,
    up_bias,
    down_weight,
    down_bias,
    norm_two_gain,
    norm_two_shift,
    segment_ids,
    valid,
):
    length = segment_ids.shape[1]
    width = tokens.shape[1]
    groups = width // GW
    gather = lambda a: lax.all_gather(a, "shard", axis=0, tiled=True)
    *rest, bu = spread(
        (query_value_bias, out_bias, norm_one_gain, norm_one_shift, down_bias, norm_two_gain, norm_two_shift, up_bias)
    )
    vecs = jnp.concatenate([v.reshape(-1, width) for v in rest] + [jnp.zeros((8, width), bf16)], axis=0)
    wqkv, wd = gather(qkv_weight), gather(down_weight)
    wou = jnp.concatenate([gather(out_weight), gather(up_weight)], axis=1)
    at = jnp.zeros((4,), jnp.int32)
    aq, ak = masks(segment_ids, valid)
    q, k, v, ctx, lse = attend(tokens, wqkv, vecs, aq, ak, length)
    result, low, hid, gd, gu, gb, gc, vec, bup = middle(tokens, ctx, cotangent, wou, vecs, bu[None], wd)
    dwd = tn(hid, gd).astype(bf16)
    dwu = tn(low, gu).astype(bf16)
    dwo = tn(ctx, gb).astype(bf16)
    dw, db, dx = attend_back(at, q, k, v, gc, ctx, lse, aq, ak, tokens, wqkv, gb, vec, length, False)
    dwq = jnp.concatenate([dw[0], dw[1], dw[2]], axis=1)
    db = db.reshape(groups, 3, GW).transpose(1, 0, 2).reshape(3, width)
    small = jnp.concatenate([db[0], db[2], vec[:6].reshape(-1), bup[0]])
    small = lax.psum(small.reshape(-1, 128), ("rep", "shard")).reshape(-1)

    def owned(a):
        part = lax.psum_scatter(a, "shard", scatter_dimension=0, tiled=True)
        return lax.psum(part, "rep").astype(f32)

    rank = lax.axis_index("shard")
    own = lambda at, size: lax.dynamic_slice(small, (at + rank * size,), (size,))
    piece = out_bias.shape[0]
    vs = [own(width * i, piece) for i in range(8)]
    dbu = own(8 * width, up_bias.shape[0])
    gd_w, gu_w, go_w, gq_w = owned(dwd), owned(dwu), owned(dwo), owned(dwq)
    return result, dx, gq_w, jnp.stack(vs[:2]), go_w, vs[2], vs[3], vs[4], gu_w, dbu, gd_w, vs[5], vs[6], vs[7]


def solution(mesh):
    rows, one = P(("rep", "shard"), None), P("shard")
    mat, two = P("shard", None), P(None, "shard")
    near = mesh.shape["rep"] == 4 and mesh.shape["shard"] == 8
    return jax.shard_map(
        shards_near if near else shards,
        mesh=mesh,
        in_specs=(rows, rows, mat, two, mat, one, one, one, mat, one, mat, one, one, one, rows, rows),
        out_specs=(rows, rows, mat, two, mat, one, one, one, mat, one, mat, one, one, one),
        check_vma=False,
    )
```

```python
import functools

import jax
import jax.numpy as jnp
from jax import lax
from jax.experimental import pallas as pl
from jax.experimental.pallas import tpu as pltpu
from jax.sharding import PartitionSpec as P

HD = 64
GW = 256
SCALE = 0.125 * 1.4426950408889634
BIG = 1e30
VMEM_LIMIT = 60 * 1024 * 1024
bf16 = jnp.bfloat16
f32 = jnp.float32
SMEM = pl.BlockSpec(memory_space=pltpu.SMEM)
VMEM = pl.BlockSpec(memory_space=pltpu.VMEM)


def nn(a, b):
    return lax.dot_general(a, b, (((1,), (0,)), ((), ())), preferred_element_type=f32)


def nt(a, b):
    return lax.dot_general(a, b, (((1,), (1,)), ((), ())), preferred_element_type=f32)


def tn(a, b):
    return lax.dot_general(a, b, (((0,), (0,)), ((), ())), preferred_element_type=f32)


def params(**more):
    return pltpu.CompilerParams(vmem_limit_bytes=VMEM_LIMIT, **more)


def cost(flops, moved):
    return pl.CostEstimate(flops=flops, bytes_accessed=moved, transcendentals=0)


def attend_kernel(tok, wq, wk, wv, vecs, aq, ak, q_o, k_o, v_o, ctx_o, lse_o):
    x = tok[...]
    q = (nn(x, wq[...]) + vecs[0:1, :].astype(f32)).astype(bf16)
    k = nn(x, wk[...]).astype(bf16)
    v = (nn(x, wv[...]) + vecs[1:2, :].astype(f32)).astype(bf16)
    q_o[...] = q
    k_o[...] = k
    v_o[...] = v
    length, width = q.shape
    lane = lax.broadcasted_iota(jnp.int32, (length, width), 1) // HD
    slot = lax.broadcasted_iota(jnp.int32, (length, 128), 1)
    acc = None
    scale = jnp.zeros((length, width), f32)
    stat = jnp.zeros((length, 128), f32)
    for h in range(width // HD):
        mine = lane == h
        qa = jnp.where(mine, q, aq[...])
        ka = jnp.where(mine, k, ak[...])
        va = jnp.where(mine, v, jnp.zeros_like(v))
        t = nt(qa, ka) * SCALE
        m = jnp.max(t, axis=1, keepdims=True)
        p = jnp.exp2(t - m)
        total = jnp.sum(p, axis=1, keepdims=True)
        part = nn(p.astype(bf16), va)
        acc = part if acc is None else acc + part
        scale = jnp.where(mine, 1.0 / total, scale)
        stat = jnp.where(slot == h, m + jnp.log2(total), stat)
    ctx_o[...] = (acc * scale).astype(bf16)
    lse_o[0] = stat.T[:8]


def attend(g, tokens, w, vecs, aq, ak, length):
    rows, width = tokens.shape
    groups = width // GW
    seqs = rows // length
    col = lambda o: pl.BlockSpec((width, GW), lambda b: (0, o * groups + g))
    seq = pl.BlockSpec((length, width), lambda b: (b, 0))
    blk = pl.BlockSpec((length, GW), lambda b: (b, 0))
    act = jax.ShapeDtypeStruct((rows, GW), bf16)
    return pl.pallas_call(
        attend_kernel,
        grid=(seqs,),
        in_specs=[seq, col(0), col(1), col(2), pl.BlockSpec((16, GW), lambda b: (0, g)), blk, blk],
        out_specs=[blk, blk, blk, blk, pl.BlockSpec((1, 8, length), lambda b: (b, 0, 0))],
        out_shape=[act, act, act, act, jax.ShapeDtypeStruct((seqs, 8, length), f32)],
        compiler_params=params(),
        cost_estimate=cost(4_000_000_000, 5_000_000),
        name="attend",
    )(tokens, w, w, w, vecs, aq, ak)


def owner_of(s, at_r):
    return lax.rem(s // 2 - at_r[2] + 4, 4), at_r[3] != s % 2


def select_lanes(s, piece, width):
    i = lax.broadcasted_iota(jnp.int32, (128, width), 0)
    j = lax.broadcasted_iota(jnp.int32, (128, width), 1)
    return ((j == s * piece + i) & (i < piece)).astype(f32).astype(bf16)


def attend_back_kernel(mode, at_r, q_r, k_r, v_r, do_r, ctx_r, lse_r, aq, ak, tok, wq, wk, wv, dx_i, *rest):
    b = pl.program_id(0)
    last = b == pl.num_programs(0) - 1
    if mode == "plain":
        dw_o, dx_o, db_o, dw_s = rest
    elif mode == "first":
        own_o, other_o, dx_o, db_o, dw_s = rest
    elif mode == "second":
        _, _, own_o, other_o, dx_o, db_o, dw_s = rest
    else:
        db0, db1, tbl, own_o, other_o, dx_o, db_o, dw_s = rest
    q, k, v, do = q_r[...], k_r[...], v_r[...], do_r[...]
    length, width = q.shape
    lane = lax.broadcasted_iota(jnp.int32, (length, width), 1) // HD
    sel = lax.broadcasted_iota(jnp.int32, (8, width), 1) // HD == lax.broadcasted_iota(jnp.int32, (8, width), 0)
    sel = sel.astype(f32).astype(bf16)
    prod = do.astype(f32) * ctx_r[...].astype(f32)
    hi = prod.astype(bf16)
    lo = (prod - hi.astype(f32)).astype(bf16)
    delta = nt(sel, hi) + nt(sel, lo)
    dq = dk = dv = None
    zero = jnp.zeros_like(q)
    for h in range(width // HD):
        mine = lane == h
        qa = jnp.where(mine, q, aq[...])
        ka = jnp.where(mine, k, ak[...])
        va = jnp.where(mine, v, zero)
        p = jnp.exp2(nt(ka, qa) * SCALE - lse_r[0, h : h + 1, :])
        dp = nt(va, do)
        ds = (p * (dp - delta[h : h + 1, :])).astype(bf16)
        dv_h = nn(p.astype(bf16), jnp.where(mine, do, zero))
        dk_h = nn(ds, jnp.where(mine, q, zero))
        dq_h = tn(ds, jnp.where(mine, k, zero))
        dv = dv_h if dv is None else dv + dv_h
        dk = dk_h if dk is None else dk + dk_h
        dq = dq_h if dq is None else dq + dq_h
    dq = (dq * 0.125).astype(bf16)
    dk = (dk * 0.125).astype(bf16)
    dv = dv.astype(bf16)
    back = jnp.concatenate([dq, dk, dv], axis=1)
    dw = tn(tok[...], back)
    dx = nt(dq, wq[...]) + nt(dk, wk[...]) + nt(dv, wv[...])
    dx_o[...] = (dx_i[...].astype(f32) + dx).astype(dx_o.dtype)
    sums = jnp.sum(back.astype(f32), axis=0, keepdims=True)

    @pl.when(b == 0)
    def _():
        dw_s[...] = dw
        db_o[...] = sums

    @pl.when(b > 0)
    def _():
        dw_s[...] += dw
        db_o[...] += sums

    @pl.when(last)
    def _():
        if mode == "plain":
            for i in range(3):
                dw_o[i] = dw_s[:, i * width : (i + 1) * width].astype(bf16)
            return
        res = dw_s[...].astype(bf16)
        piece = res.shape[0] // 8
        half, wide = piece // 2, res.shape[1] // 2
        for s in range(8):
            kk, far = owner_of(s, at_r)
            for ab, turn in ((0, at_r[1]), (1, at_r[0])):
                for h in range(2):
                    val = res[s * piece + ab * half : s * piece + (ab + 1) * half, h * wide : (h + 1) * wide]
                    rel = lax.rem(h + turn, 2)
                    for ref, cond in ((other_o, far), (own_o, ~far)):

                        @pl.when(cond)
                        def _(val=val, rel=rel, kk=kk, ab=ab, ref=ref):
                            ref[ab, rel, kk, 0:half] = val

        if mode == "third":
            sums = [r[...] for r in (db0, db1, db_o)]
            dbq = jnp.concatenate([r[:, :width] for r in sums], axis=1)
            dbv = jnp.concatenate([r[:, 2 * width :] for r in sums], axis=1)
            table = jnp.concatenate([dbq, dbv, tbl[...]], axis=0).astype(bf16)
            extra = jnp.zeros((4, 16, wide), bf16)
            for ab in range(2):
                for h in range(2):
                    own_o[ab, h, :, half : half + 16, :] = extra
                    other_o[ab, h, :, half : half + 16, :] = extra
            for s in range(8):
                blk = nt(table, select_lanes(s, piece, table.shape[1])).astype(bf16)
                kk, far = owner_of(s, at_r)
                for ref, cond in ((other_o, far), (own_o, ~far)):

                    @pl.when(cond)
                    def _(blk=blk, kk=kk, ref=ref):
                        ref[0, at_r[1], kk, half : half + 16, 0:128] = blk


def attend_back(mode, g, at, saved, gc, aq, ak, tokens, w, dx, length, extra=()):
    rows, width = tokens.shape
    groups = width // GW
    seqs = rows // length
    half = width // 16
    col = lambda o: pl.BlockSpec((width, GW), lambda b: (0, o * groups + g))
    seq = pl.BlockSpec((length, width), lambda b: (b, 0))
    blk = pl.BlockSpec((length, GW), lambda b: (b, 0))
    whole = lambda s: pl.BlockSpec(s, lambda b: (0,) * len(s))
    S = jax.ShapeDtypeStruct
    tall = {"first": 2 * half, "second": 2 * half, "third": half + 16, "plain": 0}[mode]
    at_row = 1 if mode == "second" else 0
    block = half + 16 if mode == "third" else half
    part = pl.BlockSpec((2, 2, 4, block, 3 * GW // 2), lambda b: (0, 0, 0, at_row, 0))
    if mode == "plain":
        out_specs, out_shape = [whole((3, width, GW))], [S((3, width, GW), bf16)]
    else:
        out_specs, out_shape = [part, part], [S((2, 2, 4, tall, 3 * GW // 2), bf16)] * 2
    out_specs += [seq, whole((1, 3 * GW))]
    out_shape += [S((rows, width), bf16 if mode == "third" or g == groups - 1 else f32), S((1, 3 * GW), f32)]
    in_specs = [SMEM, blk, blk, blk, pl.BlockSpec((length, GW), lambda b: (b, g)), blk]
    in_specs += [pl.BlockSpec((1, 8, length), lambda b: (b, 0, 0)), blk, blk, seq, col(0), col(1), col(2), seq]
    aliases = {}
    if mode == "second":
        in_specs += [pl.BlockSpec(memory_space=pl.ANY)] * 2
        aliases = {len(in_specs) - 2: 0, len(in_specs) - 1: 1}
    elif mode == "third":
        in_specs += [whole(e.shape) for e in extra]
    q, k, v, ctx, lse = saved
    return pl.pallas_call(
        functools.partial(attend_back_kernel, mode),
        grid=(seqs,),
        in_specs=in_specs,
        out_specs=out_specs,
        out_shape=out_shape,
        scratch_shapes=[pltpu.VMEM((width, 3 * GW), f32)],
        input_output_aliases=aliases,
        compiler_params=params(),
        cost_estimate=cost(8_000_000_000, 8_000_000),
        name="attend_back",
    )(at, q, k, v, gc, ctx, lse, aq, ak, tokens, w, w, w, dx, *extra)


def masks(segment_ids, valid):
    code = (segment_ids + 8 * valid).reshape(-1, 1)
    lane = lax.broadcasted_iota(jnp.int32, (1, GW), 1) % HD
    same = code == lane
    aq = same.astype(bf16)
    ak = jnp.where((lane < 16) & ~same, -BIG, 0.0).astype(bf16)
    return aq, ak


def phi(x):
    return 0.5 * (1.0 + lax.erf(x * 0.7071067811865476)), jnp.exp(-0.5 * x * x) * 0.3989422804014327


def middle_kernel(groups, tok, *refs):
    ctx_r = refs[:groups]
    cot, wo, vecs, wu, bu, wd, out_o, low_o, hid_o, gd_o, gu_o, gb_o, gc_o, vec_o, bup_o, slope = refs[groups:]
    i = pl.program_id(0)
    width = tok.shape[1]
    ff = wd.shape[0]
    step = width
    chunks = ff // step
    bo, g1, s1, bd, g2, s2 = (vecs[j : j + 1, :].astype(f32) for j in range(2, 8))
    ctx = jnp.concatenate([r[...] for r in ctx_r], axis=1)
    pre = tok[...].astype(f32) + nn(ctx, wo[...]) + bo
    mean = lambda v: jnp.mean(v, axis=1, keepdims=True)
    centre = pre - mean(pre)
    r1 = lax.rsqrt(mean(centre * centre) + 1e-05)
    n1 = centre * r1
    normed = n1 * g1 + s1
    low = normed.astype(bf16)
    low_o[...] = low
    acc = normed + bd
    for c in range(chunks):
        cols = slice(c * step, (c + 1) * step)
        hp = nn(low, wu[:, cols]) + bu[:, cols].astype(f32)
        cdf, pdf = phi(hp)
        slope[:, cols] = cdf + hp * pdf
        hid = (hp * cdf).astype(bf16)
        hid_o[:, cols] = hid
        acc = acc + nn(hid, wd[cols, :])
    centre = acc - mean(acc)
    r2 = lax.rsqrt(mean(centre * centre) + 1e-05)
    n2 = centre * r2
    out_o[...] = (n2 * g2 + s2).astype(bf16)
    ct = cot[...].astype(f32)
    e = ct * g2
    gp2 = r2 * (e - mean(e) - n2 * mean(e * n2))
    gd = gp2.astype(bf16)
    gd_o[...] = gd
    acc = gp2
    total = lambda v: jnp.sum(v, axis=0, keepdims=True)

    def put(ref, at, v):
        @pl.when(i == 0)
        def _():
            ref[at] = v

        @pl.when(i > 0)
        def _():
            ref[at] += v

    for c in range(chunks):
        cols = slice(c * step, (c + 1) * step)
        gu = (nt(gd, wd[cols, :]) * slope[:, cols]).astype(bf16)
        gu_o[:, cols] = gu
        put(bup_o, (slice(0, 1), cols), total(gu.astype(f32)))
        acc = acc + nt(gu, wu[:, cols])
    e = acc * g1
    gp1 = r1 * (e - mean(e) - n1 * mean(e * n1))
    gb = gp1.astype(bf16)
    gb_o[...] = gb
    gc_o[...] = nt(gb, wo[...]).astype(bf16)
    for at, v in enumerate((gb.astype(f32), acc * n1, acc, gd.astype(f32), ct * n2, ct)):
        put(vec_o, (slice(at, at + 1), slice(None)), total(v))


def middle(tokens, ctx, cot, wo, vecs, wu, bu, wd, tile=256):
    rows, width = tokens.shape
    ff = wd.shape[0]
    act = pl.BlockSpec((tile, width), lambda i: (i, 0))
    wide = pl.BlockSpec((tile, ff), lambda i: (i, 0))
    whole = lambda a: pl.BlockSpec(a.shape, lambda i: (0, 0), pipeline_mode=pl.Buffered(1))
    S = jax.ShapeDtypeStruct
    shapes = [(rows, width), (rows, width), (rows, ff), (rows, width), (rows, ff), (rows, width), (rows, width)]
    return pl.pallas_call(
        functools.partial(middle_kernel, len(ctx)),
        grid=(rows // tile,),
        in_specs=[act] + [pl.BlockSpec((tile, GW), lambda i: (i, 0)) for _ in ctx] + [act] + [whole(a) for a in (wo, vecs, wu, bu, wd)],
        out_specs=[act, act, wide, act, wide, act, act, pl.BlockSpec((8, width), lambda i: (0, 0)), pl.BlockSpec((8, ff), lambda i: (0, 0))],
        out_shape=[S(s, bf16) for s in shapes] + [S((8, width), f32), S((8, ff), f32)],
        scratch_shapes=[pltpu.VMEM((tile, ff), f32)],
        compiler_params=params(),
        cost_estimate=cost(30_000_000_000, 40_000_000),
        name="middle",
    )(tokens, *ctx, cot, wo, vecs, wu, bu, wd)


def grad_down_kernel(groups, at_r, *refs):
    ctx = refs[:groups]
    gb, hid, gd, own_o, other_o = refs[groups:]
    p = pl.program_id(0)
    turns = ((0, at_r[1]), (1, at_r[0]))
    wide = gd.shape[1] // 2
    tall = hid.shape[1] // 2

    @pl.when(p == 0)
    def _():
        lhs = jnp.concatenate([r[...] for r in ctx], axis=1)
        res = tn(lhs, gb[...]).astype(bf16)
        piece = res.shape[0] // 8
        half = piece // 2
        for s in range(8):
            kk, far = owner_of(s, at_r)
            for ab, turn in turns:
                for h in range(2):
                    val = res[s * piece + ab * half : s * piece + (ab + 1) * half, h * wide : (h + 1) * wide]
                    rel = lax.rem(h + turn, 2)
                    for ref, cond in ((other_o, far), (own_o, ~far)):

                        @pl.when(cond)
                        def _(val=val, rel=rel, kk=kk, ab=ab, ref=ref):
                            ref[ab, rel, kk, tall : tall + half] = val

    @pl.when(p > 0)
    def _():
        res = tn(hid[...], gd[...]).astype(bf16)
        kk = lax.rem(p - 1, 4)
        for ab, turn in turns:
            for h in range(2):
                val = res[ab * tall : (ab + 1) * tall, h * wide : (h + 1) * wide]
                rel = lax.rem(h + turn, 2)
                for ref, cond in ((other_o, p < 5), (own_o, p >= 5)):

                    @pl.when(cond)
                    def _(val=val, rel=rel, ab=ab, ref=ref):
                        ref[ab, rel, kk, 0:tall] = val


def grad_down(at, ctx, gb, hid, gd):
    rows, ff = hid.shape
    width = gd.shape[1]
    piece = ff // 8
    part = (2, 2, 4, (piece + width // 8) // 2, width // 2)

    def owner(p, at_r):
        j = jnp.maximum(p - 1, 0)
        z = lax.rem(at_r[2] + lax.rem(j, 4), 4)
        return 0, 2 * z + jnp.where(j < 4, 1 - at_r[3], at_r[3])

    whole = lambda s: pl.BlockSpec(s, lambda p, at_r: (0,) * len(s))
    return pl.pallas_call(
        functools.partial(grad_down_kernel, len(ctx)),
        grid_spec=pltpu.PrefetchScalarGridSpec(
            num_scalar_prefetch=1,
            grid=(9,),
            in_specs=[whole(c.shape) for c in ctx] + [whole(gb.shape), pl.BlockSpec((rows, piece), owner), whole(gd.shape)],
            out_specs=[whole(part), whole(part)],
        ),
        out_shape=[jax.ShapeDtypeStruct(part, bf16)] * 2,
        compiler_params=params(),
        cost_estimate=cost(9_000_000_000, 14_000_000),
        name="grad_down",
    )(at, *ctx, gb, hid, gd)


def grad_up_kernel(at_r, low, gu, own_o, other_o, turned):
    j = pl.program_id(0)
    y, x = at_r[0], at_r[1]

    @pl.when(j == 0)
    def _():
        turned[...] = low[...].T

    res = nn(turned[...], gu[...]).astype(bf16)
    step = res.shape[1]
    piece = res.shape[0] // 8
    half = piece // 2
    i, l = lax.rem(j // 4 + x, 2), lax.rem(lax.rem(j // 2, 2) + y, 2)
    col = pl.multiple_of(lax.rem(j, 2) * step, 128)
    for s in range(8):
        kk, far = owner_of(s, at_r)
        for ab, one, two in ((0, i, l), (1, l, i)):
            val = res[s * piece + ab * half : s * piece + (ab + 1) * half]
            for ref, cond in ((other_o, far), (own_o, ~far)):

                @pl.when(cond)
                def _(val=val, kk=kk, ab=ab, one=one, two=two, ref=ref):
                    ref[ab, one, two, kk, :, pl.ds(col, step)] = val


def grad_up(at, low, gu):
    rows, width = low.shape
    ff = gu.shape[1]
    step = ff // 8
    part = (2, 2, 2, 4, width // 16, ff // 4)
    whole = pl.BlockSpec(part, lambda j: (0, 0, 0, 0, 0, 0))
    return pl.pallas_call(
        grad_up_kernel,
        grid=(8,),
        in_specs=[SMEM, pl.BlockSpec((rows, width), lambda j: (0, 0)), pl.BlockSpec((rows, step), lambda j: (0, j))],
        out_specs=[whole, whole],
        out_shape=[jax.ShapeDtypeStruct(part, bf16)] * 2,
        scratch_shapes=[pltpu.VMEM((width, rows), bf16)],
        compiler_params=params(),
        cost_estimate=cost(9_000_000_000, 14_000_000),
        name="grad_up",
    )(at, low, gu)


AXES = ("rep", "shard")


def pairs(move):
    found = []
    for y in range(2):
        for x in range(2):
            for z in range(4):
                for c in range(2):
                    j, i, k, d = move(y, x, z, c)
                    found.append(((y * 2 + x) * 8 + z * 2 + c, (j * 2 + i) * 8 + k * 2 + d))
    return found


CORE = pairs(lambda y, x, z, c: (y, x, z, 1 - c))
ACROSS = pairs(lambda y, x, z, c: (y, 1 - x, z, c))
ALONG = pairs(lambda y, x, z, c: (1 - y, x, z, c))
SHIFT = [None] + [pairs(lambda y, x, z, c, n=n: (y, x, (z + n) % 4, c)) for n in (1, 2, 3)]


def send(a, where):
    return lax.ppermute(a, AXES, where)


def tie(values, *after):
    flat, tree = jax.tree.flatten(values)
    return jax.tree.unflatten(tree, lax.optimization_barrier(tuple(flat) + tuple(jax.tree.leaves(after)))[: len(flat)])


def place(own, received, at_r, rows, out, base, quarter):
    y, x, z = at_r[0], at_r[1], at_r[2]
    cols = out.shape[1]
    half = rows // 2
    out[pl.ds(pl.multiple_of(base(z), 16), rows), :] = own
    for k in range(1, 4):
        start = base(lax.rem(z - k + 4, 4))
        for ab in range(2):
            at = pl.ds(pl.multiple_of(start + ab * half, 16), half)
            if quarter:
                wide = cols // 4
                for i in range(2):
                    for l in range(2):
                        one, two = (i, l) if ab == 0 else (l, i)
                        col = (lax.rem(x + i, 2) * 2 + lax.rem(y + l, 2)) * wide
                        out[at, pl.ds(pl.multiple_of(col, 128), wide)] = received(ab, one, two, k)
            else:
                wide = cols // 2
                for one in range(2):
                    col = lax.rem((x, y)[ab] + one, 2) * wide
                    out[at, pl.ds(pl.multiple_of(col, 128), wide)] = received(ab, one, 0, k)


def assemble_half_kernel(out_rows, at_r, *refs):
    n = len(out_rows)
    outs = refs[-n:]
    c = at_r[3]
    for turn, (own, ring, far_x, far_y) in ((c, refs[:4]), (1 - c, refs[4:8])):
        off = 0
        total_half = own.shape[0] // 2
        for out, rows in zip(outs, out_rows):
            half = rows // 2

            def received(ab, one, two, k):
                if one == 0:
                    return ring[k - 1, ab * total_half + off : ab * total_half + off + half, :]
                return (far_x, far_y)[ab][k - 1, off : off + half, :]

            whole = jnp.concatenate([own[off : off + half], own[total_half + off : total_half + off + half]], axis=0)
            place(whole, received, at_r, rows, out, lambda z: (2 * z + turn) * rows, False)
            off += half


def assemble_quarter_kernel(at_r, *refs):
    out = refs[-1]
    c = at_r[3]
    for turn, (own, mine, first_a, first_b, second_a, second_b) in ((c, refs[:6]), (1 - c, refs[6:12])):
        rows = own.shape[0]
        half = rows // 2

        def received(ab, one, two, k):
            if two == 1:
                return (second_a, second_b)[ab][one, k - 1]
            if one == 1:
                return (first_a, first_b)[ab][k - 1]
            return mine[k - 1, ab * half : (ab + 1) * half, :]

        place(own[...], received, at_r, rows, out, lambda z: (2 * z + turn) * rows, True)


def assemble(kernel, at, parts, shapes):
    return pl.pallas_call(
        kernel,
        in_specs=[SMEM] + [VMEM] * len(parts),
        out_specs=[VMEM] * len(shapes),
        out_shape=[jax.ShapeDtypeStruct(s, bf16) for s in shapes],
        compiler_params=params(),
        cost_estimate=cost(0, sum(4 * s[0] * s[1] for s in shapes)),
        name="assemble",
    )(at, *parts)


def halves(w, x, y):
    half, wide = w.shape[0] // 2, w.shape[1] // 2
    a = lax.dynamic_slice(w, (0, x * wide), (half, wide))
    b = lax.dynamic_slice(w, (half, y * wide), (half, wide))
    return jnp.concatenate([a, b], axis=0)


def spread_half(ring):
    half = ring.shape[1] // 2
    return send(ring[:, :half], ACROSS), send(ring[:, half:], ALONG)


def swap(parts):
    return tuple(send(p, CORE) for p in parts)


def total(*terms):
    out = terms[0].astype(f32)
    for t in terms[1:]:
        out = out + t.astype(f32)
    return out.astype(bf16)


def finish_kernel(kind, at_r, *refs):
    y, x = at_r[0], at_r[1]
    if kind == "up":
        fa, fb, ga, gb, ha, hb, out = refs
        half, wide = out.shape[0] // 2, out.shape[1] // 4
        for i in range(2):
            for l in range(2):
                col = pl.ds(pl.multiple_of((lax.rem(x + i, 2) * 2 + lax.rem(y + l, 2)) * wide, 128), wide)
                a = ha[i] if l else (ga if i else fa)[...]
                b = hb[l] if i else (gb if l else fb)[...]
                out[0:half, col] = a.astype(f32)
                out[half:, col] = b.astype(f32)
        return
    blocks, outs = refs[:4], refs[4:]
    for ab, turn in ((0, x), (1, y)):
        one, two = (blocks[2 * ab + i][...].astype(f32) for i in range(2))
        left = jnp.where(turn == 0, one, two)
        right = jnp.where(turn == 0, two, one)
        both = jnp.concatenate([left, right], axis=1)
        if kind == "down":
            off = 0
            for out in outs:
                half = out.shape[0] // 2
                out[ab * half : (ab + 1) * half, :] = both[off : off + half]
                off += half
        elif ab == 0 and len(outs) > 1:
            outs[0][0] = both[0:48]
            outs[1][...] = left[48:64, :128]
        else:
            n = outs[0].shape[1] // 48
            for g in range(n):
                outs[0][ab, g * 48 : (g + 1) * 48] = both[g * 48 : (g + 1) * 48]


def finish(at, kind, blocks, shapes):
    return pl.pallas_call(
        functools.partial(finish_kernel, kind),
        in_specs=[SMEM] + [VMEM] * len(blocks),
        out_specs=[VMEM] * len(shapes),
        out_shape=[jax.ShapeDtypeStruct(s, f32) for s in shapes],
        compiler_params=params(),
        cost_estimate=cost(0, 4_000_000),
        name="finish_" + kind,
    )(at, *blocks)


def pack(vectors, wide):
    block = jnp.concatenate([v.reshape(-1, vectors[1].shape[0]) for v in vectors] + [wide.reshape(4, -1)], axis=0)
    return jnp.pad(block, ((0, 16 - block.shape[0]), (0, 128 - block.shape[1])))


def whole_vectors(every, z, c, piece):
    k = lax.broadcasted_iota(jnp.int32, (2, 4, 8), 1)
    d = lax.broadcasted_iota(jnp.int32, (2, 4, 8), 0)
    s = lax.broadcasted_iota(jnp.int32, (2, 4, 8), 2)
    pick = (s == 2 * ((z - k) % 4) + (c + d) % 2).astype(bf16)
    table = jnp.einsum("dks,dkrl->srl", pick, every, preferred_element_type=f32).astype(bf16)
    table = table[:, :, :piece]
    wide = table[:, 8:12].reshape(1, -1)
    return table.transpose(1, 0, 2).reshape(16, -1), wide


class HalfSum:
    def __init__(self, own, other):
        self.own, self.got = own, send(other, CORE)

    def halve(self):
        own, got = self.own, self.got
        self.sent = total(own[0, 1], got[0, 1]), total(own[1, 1], got[1, 1])
        self.far = send(self.sent[0], ACROSS), send(self.sent[1], ALONG)

    def along_z(self):
        own, got, far = self.own, self.got, self.far
        self.mine = [jnp.stack([total(own[i, 0, k], got[i, 0, k], far[i][k]) for i in range(2)]) for k in range(4)]
        self.sent = self.mine[1:]
        self.parts = [send(self.mine[k], SHIFT[k]) for k in range(1, 4)]

    def across(self):
        both = total(self.mine[0], *self.parts)
        self.sent = both[0], both[1]
        self.far = send(both[0], ALONG), send(both[1], ACROSS)

    def share(self):
        a, b = (total(self.sent[i], self.far[i]) for i in range(2))
        self.sent = a, b
        self.out = a, send(a, ACROSS), b, send(b, ALONG)


class QuarterSum:
    def __init__(self, own, other):
        self.own, self.got = own, send(other, CORE)

    def halve(self):
        own, got = self.own, self.got
        self.sent = total(own[0, 1], got[0, 1]), total(own[1, 1], got[1, 1])
        self.far = send(self.sent[0], ACROSS), send(self.sent[1], ALONG)

    def quarter(self):
        own, got, far = self.own, self.got, self.far
        part = lambda i, j: total(own[i, 0, j], got[i, 0, j], far[i][j])
        self.sent = part(0, 1), part(1, 1)
        self.near = part(0, 0), part(1, 0)
        self.far = send(self.sent[0], ALONG), send(self.sent[1], ACROSS)

    def along_z(self):
        self.mine = [jnp.stack([total(self.near[i][k], self.far[i][k]) for i in range(2)]) for k in range(4)]
        self.sent = self.mine[1:]
        self.parts = [send(self.mine[k], SHIFT[k]) for k in range(1, 4)]

    def share(self):
        both = total(self.mine[0], *self.parts)
        self.sent = both[0], both[1]
        self.far = send(both[0], ACROSS), send(both[1], ALONG)

    def share_more(self):
        a, b = (jnp.stack([self.sent[i], self.far[i]]) for i in range(2))
        self.out = self.sent + self.far + (send(a, ALONG), send(b, ACROSS))


def shards_near(
    tokens,
    cotangent,
    qkv_weight,
    query_value_bias,
    out_weight,
    out_bias,
    norm_one_gain,
    norm_one_shift,
    up_weight,
    up_bias,
    down_weight,
    down_bias,
    norm_two_gain,
    norm_two_shift,
    segment_ids,
    valid,
):
    length = segment_ids.shape[1]
    width = tokens.shape[1]
    groups = width // GW
    ff = up_bias.shape[0] * 8
    piece = out_bias.shape[0]
    r, s = lax.axis_index("rep"), lax.axis_index("shard")
    y, x, z, c = r // 2, r % 2, s // 2, s % 2
    at = jnp.stack([y, x, z, c]).astype(jnp.int32)

    held = halves(qkv_weight, x, y)
    ring = []
    for _ in range(3):
        held = send(held, SHIFT[1])
        ring.append(held)
    ring_q = jnp.stack(ring)
    far_q = spread_half(ring_q)
    parts_q = (qkv_weight, ring_q) + far_q
    (wqkv,) = assemble(
        functools.partial(assemble_half_kernel, [qkv_weight.shape[0]]), at, parts_q + swap(parts_q), [(width, 3 * width)]
    )

    block = pack(
        (query_value_bias, out_bias, norm_one_gain, norm_one_shift, down_bias, norm_two_gain, norm_two_shift), up_bias
    )
    ring_v = jnp.stack([block] + [send(block, SHIFT[k]) for k in range(1, 4)])
    vecs, bu = whole_vectors(jnp.stack([ring_v, send(ring_v, CORE)]), z, c, piece)

    half, wide = piece // 2, ff // 4
    first = lax.dynamic_slice(up_weight, (0, (2 * x + y) * wide), (piece, wide))
    first = tie(first, held)
    ring_u = jnp.stack([send(first, SHIFT[k]) for k in range(1, 4)])
    a, b = ring_u[:, :half], ring_u[:, half:]
    a2, b2 = send(a, ACROSS), send(b, ALONG)
    a4, b4 = send(jnp.stack([a, a2]), ALONG), send(jnp.stack([b, b2]), ACROSS)
    parts_u = (up_weight, ring_u, a2, b2, a4, b4)
    (wu,) = assemble(assemble_quarter_kernel, at, parts_u + swap(parts_u), [(width, ff)])

    dr = down_weight.shape[0] // 2
    both = jnp.concatenate([down_weight[:dr], out_weight[:half], down_weight[dr:], out_weight[half:]], axis=0)
    first = tie(halves(both, x, y), ring_u)
    ring_d = jnp.stack([send(first, SHIFT[k]) for k in range(1, 4)])
    far_d = spread_half(ring_d)
    parts_d = (both, ring_d) + far_d
    wd, wo = assemble(
        functools.partial(assemble_half_kernel, [2 * dr, piece]), at, parts_d + swap(parts_d), [(ff, width), (width, width)]
    )

    aq, ak = masks(segment_ids, valid)
    saved = [attend(g, tokens, wqkv, vecs, aq, ak, length) for g in range(groups)]
    ctx = [f[3] for f in saved]
    result, low, hid, gd, gu, gb, gc, vec, bup = middle(tokens, ctx, cotangent, wo, vecs, wu, bu, wd)

    own, other = grad_down(at, ctx, gb, hid, gd)
    down = HalfSum(own, other)
    own, other = grad_up(at, *tie((low, gu), other))
    up = QuarterSum(own, other)
    down.halve()
    gc = tie(gc, down.sent, other)
    own, other, dx, db0 = attend_back("first", 0, at, saved[0], gc, aq, ak, tokens, wqkv, gb, length)
    down.along_z()
    up.halve()
    gc = tie(gc, down.sent, up.sent, dx)
    own, other, dx, db1 = attend_back("second", 1, at, saved[1], gc, aq, ak, tokens, wqkv, dx, length, (own, other))
    first_two = HalfSum(own, other)
    up.quarter()
    gc = tie(gc, up.sent, dx)
    wide = bup[0].reshape(8, 4, piece).transpose(1, 0, 2).reshape(4, width)
    table = jnp.concatenate([vec[:6], wide, jnp.zeros((4, width), f32)], axis=0)
    own, other, dx, _ = attend_back(
        "third", 2, at, saved[2], gc, aq, ak, tokens, wqkv, dx, length, (db0, db1, table)
    )
    third = HalfSum(own, other)
    down.across()
    up.along_z()
    first_two.halve()
    third.halve()
    first_two.along_z()
    third.along_z()
    down.share()
    up.share()
    up.share_more()
    first_two.across()
    third.across()
    first_two.share()
    third.share()
    dwd, dwo = finish(at, "down", down.out, [down_weight.shape, out_weight.shape])
    (dwu,) = finish(at, "up", up.out, [up_weight.shape])
    (q01,) = finish(at, "qkv", first_two.out, [(2, piece, 3 * GW)])
    q2, small = finish(at, "qkv", third.out, [(2, half, 3 * GW), (16, 128)])
    by_group = [q01[:, :half], q01[:, half:], q2]
    by_group = [q.reshape(piece, 3, GW) for q in by_group]
    dwq = jnp.concatenate([q[:, i] for i in range(3) for q in by_group], axis=1)
    one = lambda i: small[i, :piece]
    return (
        result,
        dx,
        dwq,
        small[:2, :piece],
        dwo,
        one(2),
        one(3),
        one(4),
        dwu,
        small[8:12, :piece].reshape(-1),
        dwd,
        one(5),
        one(6),
        one(7),
    )


def spread(args):
    flat = [a.reshape(-1) for a in args]
    packed = jnp.concatenate(flat)
    every = lax.all_gather(packed, "shard", axis=0)
    out, at = [], 0
    for a in args:
        part = every[:, at : at + a.size].reshape((-1,) + a.shape)
        at += a.size
        out.append(jnp.moveaxis(part, 0, -2).reshape(a.shape[:-1] + (-1,)))
    return out


def shards(
    tokens,
    cotangent,
    qkv_weight,
    query_value_bias,
    out_weight,
    out_bias,
    norm_one_gain,
    norm_one_shift,
    up_weight,
    up_bias,
    down_weight,
    down_bias,
    norm_two_gain,
    norm_two_shift,
    segment_ids,
    valid,
):
    length = segment_ids.shape[1]
    width = tokens.shape[1]
    groups = width // GW
    gather = lambda a: lax.all_gather(a, "shard", axis=0, tiled=True)
    *rest, bu = spread(
        (query_value_bias, out_bias, norm_one_gain, norm_one_shift, down_bias, norm_two_gain, norm_two_shift, up_bias)
    )
    vecs = jnp.concatenate([v.reshape(-1, width) for v in rest] + [jnp.zeros((8, width), bf16)], axis=0)
    wqkv, wd, wo, wu = gather(qkv_weight), gather(down_weight), gather(out_weight), gather(up_weight)
    at = jnp.zeros((4,), jnp.int32)
    aq, ak = masks(segment_ids, valid)
    saved = [attend(g, tokens, wqkv, vecs, aq, ak, length) for g in range(groups)]
    ctx = [f[3] for f in saved]
    result, low, hid, gd, gu, gb, gc, vec, bup = middle(tokens, ctx, cotangent, wo, vecs, wu, bu[None], wd)
    dwd = tn(hid, gd).astype(bf16)
    dwu = tn(low, gu).astype(bf16)
    dwo = tn(jnp.concatenate(ctx, axis=1), gb).astype(bf16)
    dx, dws, dbs = gb, [], []
    for g in range(groups):
        dw, dx, db = attend_back("plain", g, at, saved[g], gc, aq, ak, tokens, wqkv, dx, length)
        dws.append(dw)
        dbs.append(db)
    dwq = jnp.concatenate([dw[i] for i in range(3) for dw in dws], axis=1)
    db = jnp.stack(dbs).reshape(groups, 3, GW).transpose(1, 0, 2).reshape(3, width)
    small = jnp.concatenate([db[0], db[2], vec[:6].reshape(-1), bup[0]])
    small = lax.psum(small.reshape(-1, 128), ("rep", "shard")).reshape(-1)

    def owned(a):
        part = lax.psum_scatter(a, "shard", scatter_dimension=0, tiled=True)
        return lax.psum(part, "rep").astype(f32)

    rank = lax.axis_index("shard")
    own = lambda at, size: lax.dynamic_slice(small, (at + rank * size,), (size,))
    piece = out_bias.shape[0]
    vs = [own(width * i, piece) for i in range(8)]
    dbu = own(8 * width, up_bias.shape[0])
    gd_w, gu_w, go_w, gq_w = owned(dwd), owned(dwu), owned(dwo), owned(dwq)
    return result, dx, gq_w, jnp.stack(vs[:2]), go_w, vs[2], vs[3], vs[4], gu_w, dbu, gd_w, vs[5], vs[6], vs[7]


def solution(mesh):
    rows, one = P(("rep", "shard"), None), P("shard")
    mat, two = P("shard", None), P(None, "shard")
    near = mesh.shape["rep"] == 4 and mesh.shape["shard"] == 8
    return jax.shard_map(
        shards_near if near else shards,
        mesh=mesh,
        in_specs=(rows, rows, mat, two, mat, one, one, one, mat, one, mat, one, one, one, rows, rows),
        out_specs=(rows, rows, mat, two, mat, one, one, one, mat, one, mat, one, one, one),
        check_vma=False,
    )
```

```python
import functools

import jax
import jax.numpy as jnp
from jax import lax
from jax.experimental import pallas as pl
from jax.experimental.pallas import tpu as pltpu
from jax.sharding import PartitionSpec as P

HD = 64
GW = 256
SCALE = 0.125 * 1.4426950408889634
BIG = 1e30
VMEM_LIMIT = 60 * 1024 * 1024
bf16 = jnp.bfloat16
f32 = jnp.float32
SMEM = pl.BlockSpec(memory_space=pltpu.SMEM)
VMEM = pl.BlockSpec(memory_space=pltpu.VMEM)


def nn(a, b):
    return lax.dot_general(a, b, (((1,), (0,)), ((), ())), preferred_element_type=f32)


def nt(a, b):
    return lax.dot_general(a, b, (((1,), (1,)), ((), ())), preferred_element_type=f32)


def tn(a, b):
    return lax.dot_general(a, b, (((0,), (0,)), ((), ())), preferred_element_type=f32)


def params(**more):
    return pltpu.CompilerParams(vmem_limit_bytes=VMEM_LIMIT, **more)


def cost(flops, moved):
    return pl.CostEstimate(flops=flops, bytes_accessed=moved, transcendentals=0)


def attend_kernel(tok, wq, wk, wv, vecs, aq, ak, q_o, k_o, v_o, ctx_o, lse_o):
    x = tok[...]
    q = (nn(x, wq[...]) + vecs[0:1, :].astype(f32)).astype(bf16)
    k = nn(x, wk[...]).astype(bf16)
    v = (nn(x, wv[...]) + vecs[1:2, :].astype(f32)).astype(bf16)
    q_o[...] = q
    k_o[...] = k
    v_o[...] = v
    length, width = q.shape
    lane = lax.broadcasted_iota(jnp.int32, (length, width), 1) // HD
    slot = lax.broadcasted_iota(jnp.int32, (length, 128), 1)
    acc = None
    scale = jnp.zeros((length, width), f32)
    stat = jnp.zeros((length, 128), f32)
    for h in range(width // HD):
        mine = lane == h
        qa = jnp.where(mine, q, aq[...])
        ka = jnp.where(mine, k, ak[...])
        va = jnp.where(mine, v, jnp.zeros_like(v))
        t = nt(qa, ka) * SCALE
        m = jnp.max(t, axis=1, keepdims=True)
        p = jnp.exp2(t - m)
        total = jnp.sum(p, axis=1, keepdims=True)
        part = nn(p.astype(bf16), va)
        acc = part if acc is None else acc + part
        scale = jnp.where(mine, 1.0 / total, scale)
        stat = jnp.where(slot == h, m + jnp.log2(total), stat)
    ctx_o[...] = (acc * scale).astype(bf16)
    lse_o[0] = stat.T[:8]


def attend(g, tokens, w, vecs, aq, ak, length):
    rows, width = tokens.shape
    groups = width // GW
    seqs = rows // length
    col = lambda o: pl.BlockSpec((width, GW), lambda b: (0, o * groups + g))
    seq = pl.BlockSpec((length, width), lambda b: (b, 0))
    blk = pl.BlockSpec((length, GW), lambda b: (b, 0))
    act = jax.ShapeDtypeStruct((rows, GW), bf16)
    return pl.pallas_call(
        attend_kernel,
        grid=(seqs,),
        in_specs=[seq, col(0), col(1), col(2), pl.BlockSpec((16, GW), lambda b: (0, g)), blk, blk],
        out_specs=[blk, blk, blk, blk, pl.BlockSpec((1, 8, length), lambda b: (b, 0, 0))],
        out_shape=[act, act, act, act, jax.ShapeDtypeStruct((seqs, 8, length), f32)],
        compiler_params=params(),
        cost_estimate=cost(4_000_000_000, 5_000_000),
        name="attend",
    )(tokens, w, w, w, vecs, aq, ak)


def owner_of(s, at_r):
    return lax.rem(s // 2 - at_r[2] + 4, 4), at_r[3] != s % 2


def select_lanes(s, piece, width):
    i = lax.broadcasted_iota(jnp.int32, (128, width), 0)
    j = lax.broadcasted_iota(jnp.int32, (128, width), 1)
    return ((j == s * piece + i) & (i < piece)).astype(f32).astype(bf16)


def attend_back_kernel(mode, at_r, q_r, k_r, v_r, do_r, ctx_r, lse_r, aq, ak, tok, wq, wk, wv, dx_i, *rest):
    b = pl.program_id(0)
    last = b == pl.num_programs(0) - 1
    if mode == "plain":
        dw_o, dx_o, db_o, dw_s = rest
    elif mode == "first":
        own_o, other_o, dx_o, db_o, dw_s = rest
    elif mode == "second":
        _, _, own_o, other_o, dx_o, db_o, dw_s = rest
    else:
        db0, db1, tbl, own_o, other_o, dx_o, db_o, dw_s = rest
    q, k, v, do = q_r[...], k_r[...], v_r[...], do_r[...]
    length, width = q.shape
    lane = lax.broadcasted_iota(jnp.int32, (length, width), 1) // HD
    sel = lax.broadcasted_iota(jnp.int32, (8, width), 1) // HD == lax.broadcasted_iota(jnp.int32, (8, width), 0)
    sel = sel.astype(f32).astype(bf16)
    prod = do.astype(f32) * ctx_r[...].astype(f32)
    hi = prod.astype(bf16)
    lo = (prod - hi.astype(f32)).astype(bf16)
    delta = nt(sel, hi) + nt(sel, lo)
    dq = dk = dv = None
    zero = jnp.zeros_like(q)
    for h in range(width // HD):
        mine = lane == h
        qa = jnp.where(mine, q, aq[...])
        ka = jnp.where(mine, k, ak[...])
        va = jnp.where(mine, v, zero)
        p = jnp.exp2(nt(ka, qa) * SCALE - lse_r[0, h : h + 1, :])
        dp = nt(va, do)
        ds = (p * (dp - delta[h : h + 1, :])).astype(bf16)
        dv_h = nn(p.astype(bf16), jnp.where(mine, do, zero))
        dk_h = nn(ds, jnp.where(mine, q, zero))
        dq_h = tn(ds, jnp.where(mine, k, zero))
        dv = dv_h if dv is None else dv + dv_h
        dk = dk_h if dk is None else dk + dk_h
        dq = dq_h if dq is None else dq + dq_h
    dq = (dq * 0.125).astype(bf16)
    dk = (dk * 0.125).astype(bf16)
    dv = dv.astype(bf16)
    back = jnp.concatenate([dq, dk, dv], axis=1)
    dw = tn(tok[...], back)
    dx = nt(dq, wq[...]) + nt(dk, wk[...]) + nt(dv, wv[...])
    dx_o[...] = (dx_i[...].astype(f32) + dx).astype(dx_o.dtype)
    sums = jnp.sum(back.astype(f32), axis=0, keepdims=True)

    @pl.when(b == 0)
    def _():
        dw_s[...] = dw
        db_o[...] = sums

    @pl.when(b > 0)
    def _():
        dw_s[...] += dw
        db_o[...] += sums

    @pl.when(last)
    def _():
        if mode == "plain":
            for i in range(3):
                dw_o[i] = dw_s[:, i * width : (i + 1) * width].astype(bf16)
            return
        res = dw_s[...].astype(bf16)
        piece = res.shape[0] // 8
        half, wide = piece // 2, res.shape[1] // 2
        for s in range(8):
            kk, far = owner_of(s, at_r)
            for ab, turn in ((0, at_r[1]), (1, at_r[0])):
                for h in range(2):
                    val = res[s * piece + ab * half : s * piece + (ab + 1) * half, h * wide : (h + 1) * wide]
                    rel = lax.rem(h + turn, 2)
                    for ref, cond in ((other_o, far), (own_o, ~far)):

                        @pl.when(cond)
                        def _(val=val, rel=rel, kk=kk, ab=ab, ref=ref):
                            ref[ab, rel, kk, 0:half] = val

        if mode == "third":
            sums = [r[...] for r in (db0, db1, db_o)]
            dbq = jnp.concatenate([r[:, :width] for r in sums], axis=1)
            dbv = jnp.concatenate([r[:, 2 * width :] for r in sums], axis=1)
            table = jnp.concatenate([dbq, dbv, tbl[...]], axis=0).astype(bf16)
            extra = jnp.zeros((4, 16, wide), bf16)
            for ab in range(2):
                for h in range(2):
                    own_o[ab, h, :, half : half + 16, :] = extra
                    other_o[ab, h, :, half : half + 16, :] = extra
            for s in range(8):
                blk = nt(table, select_lanes(s, piece, table.shape[1])).astype(bf16)
                kk, far = owner_of(s, at_r)
                for ref, cond in ((other_o, far), (own_o, ~far)):

                    @pl.when(cond)
                    def _(blk=blk, kk=kk, ref=ref):
                        ref[0, at_r[1], kk, half : half + 16, 0:128] = blk


def attend_back(mode, g, at, saved, gc, aq, ak, tokens, w, dx, length, extra=()):
    rows, width = tokens.shape
    groups = width // GW
    seqs = rows // length
    half = width // 16
    col = lambda o: pl.BlockSpec((width, GW), lambda b: (0, o * groups + g))
    seq = pl.BlockSpec((length, width), lambda b: (b, 0))
    blk = pl.BlockSpec((length, GW), lambda b: (b, 0))
    whole = lambda s: pl.BlockSpec(s, lambda b: (0,) * len(s))
    S = jax.ShapeDtypeStruct
    tall = {"first": 2 * half, "second": 2 * half, "third": half + 16, "plain": 0}[mode]
    at_row = 1 if mode == "second" else 0
    block = half + 16 if mode == "third" else half
    part = pl.BlockSpec((2, 2, 4, block, 3 * GW // 2), lambda b: (0, 0, 0, at_row, 0))
    if mode == "plain":
        out_specs, out_shape = [whole((3, width, GW))], [S((3, width, GW), bf16)]
    else:
        out_specs, out_shape = [part, part], [S((2, 2, 4, tall, 3 * GW // 2), bf16)] * 2
    out_specs += [seq, whole((1, 3 * GW))]
    out_shape += [S((rows, width), bf16 if mode == "third" or g == groups - 1 else f32), S((1, 3 * GW), f32)]
    in_specs = [SMEM, blk, blk, blk, pl.BlockSpec((length, GW), lambda b: (b, g)), blk]
    in_specs += [pl.BlockSpec((1, 8, length), lambda b: (b, 0, 0)), blk, blk, seq, col(0), col(1), col(2), seq]
    aliases = {}
    if mode == "second":
        in_specs += [pl.BlockSpec(memory_space=pl.ANY)] * 2
        aliases = {len(in_specs) - 2: 0, len(in_specs) - 1: 1}
    elif mode == "third":
        in_specs += [whole(e.shape) for e in extra]
    q, k, v, ctx, lse = saved
    return pl.pallas_call(
        functools.partial(attend_back_kernel, mode),
        grid=(seqs,),
        in_specs=in_specs,
        out_specs=out_specs,
        out_shape=out_shape,
        scratch_shapes=[pltpu.VMEM((width, 3 * GW), f32)],
        input_output_aliases=aliases,
        compiler_params=params(),
        cost_estimate=cost(8_000_000_000, 8_000_000),
        name="attend_back",
    )(at, q, k, v, gc, ctx, lse, aq, ak, tokens, w, w, w, dx, *extra)


def masks(segment_ids, valid):
    code = (segment_ids + 8 * valid).reshape(-1, 1)
    lane = lax.broadcasted_iota(jnp.int32, (1, GW), 1) % HD
    same = code == lane
    aq = same.astype(bf16)
    ak = jnp.where((lane < 16) & ~same, -BIG, 0.0).astype(bf16)
    return aq, ak


def phi(x):
    return 0.5 * (1.0 + lax.erf(x * 0.7071067811865476)), jnp.exp(-0.5 * x * x) * 0.3989422804014327


def middle_kernel(groups, tok, *refs):
    ctx_r = refs[:groups]
    cot, wo, vecs, wu, bu, wd, out_o, low_o, hid_o, gd_o, gu_o, gb_o, gc_o, vec_o, bup_o, slope = refs[groups:]
    i = pl.program_id(0)
    width = tok.shape[1]
    ff = wd.shape[0]
    step = width
    chunks = ff // step
    bo, g1, s1, bd, g2, s2 = (vecs[j : j + 1, :].astype(f32) for j in range(2, 8))
    ctx = jnp.concatenate([r[...] for r in ctx_r], axis=1)
    pre = tok[...].astype(f32) + nn(ctx, wo[...]) + bo
    mean = lambda v: jnp.mean(v, axis=1, keepdims=True)
    centre = pre - mean(pre)
    r1 = lax.rsqrt(mean(centre * centre) + 1e-05)
    n1 = centre * r1
    normed = n1 * g1 + s1
    low = normed.astype(bf16)
    low_o[...] = low
    acc = normed + bd
    for c in range(chunks):
        cols = slice(c * step, (c + 1) * step)
        hp = nn(low, wu[:, cols]) + bu[:, cols].astype(f32)
        cdf, pdf = phi(hp)
        slope[:, cols] = cdf + hp * pdf
        hid = (hp * cdf).astype(bf16)
        hid_o[:, cols] = hid
        acc = acc + nn(hid, wd[cols, :])
    centre = acc - mean(acc)
    r2 = lax.rsqrt(mean(centre * centre) + 1e-05)
    n2 = centre * r2
    out_o[...] = (n2 * g2 + s2).astype(bf16)
    ct = cot[...].astype(f32)
    e = ct * g2
    gp2 = r2 * (e - mean(e) - n2 * mean(e * n2))
    gd = gp2.astype(bf16)
    gd_o[...] = gd
    acc = gp2
    total = lambda v: jnp.sum(v, axis=0, keepdims=True)

    def put(ref, at, v):
        @pl.when(i == 0)
        def _():
            ref[at] = v

        @pl.when(i > 0)
        def _():
            ref[at] += v

    for c in range(chunks):
        cols = slice(c * step, (c + 1) * step)
        gu = (nt(gd, wd[cols, :]) * slope[:, cols]).astype(bf16)
        gu_o[:, cols] = gu
        put(bup_o, (slice(0, 1), cols), total(gu.astype(f32)))
        acc = acc + nt(gu, wu[:, cols])
    e = acc * g1
    gp1 = r1 * (e - mean(e) - n1 * mean(e * n1))
    gb = gp1.astype(bf16)
    gb_o[...] = gb
    gc_o[...] = nt(gb, wo[...]).astype(bf16)
    for at, v in enumerate((gb.astype(f32), acc * n1, acc, gd.astype(f32), ct * n2, ct)):
        put(vec_o, (slice(at, at + 1), slice(None)), total(v))


def middle(tokens, ctx, cot, wo, vecs, wu, bu, wd, tile=256):
    rows, width = tokens.shape
    ff = wd.shape[0]
    act = pl.BlockSpec((tile, width), lambda i: (i, 0))
    wide = pl.BlockSpec((tile, ff), lambda i: (i, 0))
    whole = lambda a: pl.BlockSpec(a.shape, lambda i: (0, 0), pipeline_mode=pl.Buffered(1))
    S = jax.ShapeDtypeStruct
    shapes = [(rows, width), (rows, width), (rows, ff), (rows, width), (rows, ff), (rows, width), (rows, width)]
    return pl.pallas_call(
        functools.partial(middle_kernel, len(ctx)),
        grid=(rows // tile,),
        in_specs=[act] + [pl.BlockSpec((tile, GW), lambda i: (i, 0)) for _ in ctx] + [act] + [whole(a) for a in (wo, vecs, wu, bu, wd)],
        out_specs=[act, act, wide, act, wide, act, act, pl.BlockSpec((8, width), lambda i: (0, 0)), pl.BlockSpec((8, ff), lambda i: (0, 0))],
        out_shape=[S(s, bf16) for s in shapes] + [S((8, width), f32), S((8, ff), f32)],
        scratch_shapes=[pltpu.VMEM((tile, ff), f32)],
        compiler_params=params(),
        cost_estimate=cost(30_000_000_000, 40_000_000),
        name="middle",
    )(tokens, *ctx, cot, wo, vecs, wu, bu, wd)


def grad_down_kernel(groups, at_r, *refs):
    ctx = refs[:groups]
    gb, hid, gd, own_o, other_o = refs[groups:]
    p = pl.program_id(0)
    turns = ((0, at_r[1]), (1, at_r[0]))
    wide = gd.shape[1] // 2
    tall = hid.shape[1] // 2

    @pl.when(p == 0)
    def _():
        lhs = jnp.concatenate([r[...] for r in ctx], axis=1)
        res = tn(lhs, gb[...]).astype(bf16)
        piece = res.shape[0] // 8
        half = piece // 2
        for s in range(8):
            kk, far = owner_of(s, at_r)
            for ab, turn in turns:
                for h in range(2):
                    val = res[s * piece + ab * half : s * piece + (ab + 1) * half, h * wide : (h + 1) * wide]
                    rel = lax.rem(h + turn, 2)
                    for ref, cond in ((other_o, far), (own_o, ~far)):

                        @pl.when(cond)
                        def _(val=val, rel=rel, kk=kk, ab=ab, ref=ref):
                            ref[ab, rel, kk, tall : tall + half] = val

    @pl.when(p > 0)
    def _():
        res = tn(hid[...], gd[...]).astype(bf16)
        kk = lax.rem(p - 1, 4)
        for ab, turn in turns:
            for h in range(2):
                val = res[ab * tall : (ab + 1) * tall, h * wide : (h + 1) * wide]
                rel = lax.rem(h + turn, 2)
                for ref, cond in ((other_o, p < 5), (own_o, p >= 5)):

                    @pl.when(cond)
                    def _(val=val, rel=rel, ab=ab, ref=ref):
                        ref[ab, rel, kk, 0:tall] = val


def grad_down(at, ctx, gb, hid, gd):
    rows, ff = hid.shape
    width = gd.shape[1]
    piece = ff // 8
    part = (2, 2, 4, (piece + width // 8) // 2, width // 2)

    def owner(p, at_r):
        j = jnp.maximum(p - 1, 0)
        z = lax.rem(at_r[2] + lax.rem(j, 4), 4)
        return 0, 2 * z + jnp.where(j < 4, 1 - at_r[3], at_r[3])

    whole = lambda s: pl.BlockSpec(s, lambda p, at_r: (0,) * len(s))
    return pl.pallas_call(
        functools.partial(grad_down_kernel, len(ctx)),
        grid_spec=pltpu.PrefetchScalarGridSpec(
            num_scalar_prefetch=1,
            grid=(9,),
            in_specs=[whole(c.shape) for c in ctx] + [whole(gb.shape), pl.BlockSpec((rows, piece), owner), whole(gd.shape)],
            out_specs=[whole(part), whole(part)],
        ),
        out_shape=[jax.ShapeDtypeStruct(part, bf16)] * 2,
        compiler_params=params(),
        cost_estimate=cost(9_000_000_000, 14_000_000),
        name="grad_down",
    )(at, *ctx, gb, hid, gd)


def grad_up_kernel(at_r, low, gu, own_o, other_o, turned):
    j = pl.program_id(0)
    y, x = at_r[0], at_r[1]

    @pl.when(j == 0)
    def _():
        turned[...] = low[...].T

    res = nn(turned[...], gu[...]).astype(bf16)
    step = res.shape[1]
    piece = res.shape[0] // 8
    half = piece // 2
    h = j // 4
    col = pl.multiple_of(lax.rem(j, 4) * step, 128)
    for s in range(8):
        kk, far = owner_of(s, at_r)
        for ab, turn in ((0, x), (1, y)):
            val = res[s * piece + ab * half : s * piece + (ab + 1) * half]
            for ref, cond in ((other_o, far), (own_o, ~far)):

                @pl.when(cond)
                def _(val=val, kk=kk, ab=ab, turn=turn, ref=ref):
                    ref[ab, lax.rem(h + turn, 2), kk, :, pl.ds(col, step)] = val


def grad_up(at, low, gu):
    rows, width = low.shape
    ff = gu.shape[1]
    step = ff // 8
    part = (2, 2, 4, width // 16, ff // 2)
    whole = pl.BlockSpec(part, lambda j: (0, 0, 0, 0, 0))
    return pl.pallas_call(
        grad_up_kernel,
        grid=(8,),
        in_specs=[SMEM, pl.BlockSpec((rows, width), lambda j: (0, 0)), pl.BlockSpec((rows, step), lambda j: (0, j))],
        out_specs=[whole, whole],
        out_shape=[jax.ShapeDtypeStruct(part, bf16)] * 2,
        scratch_shapes=[pltpu.VMEM((width, rows), bf16)],
        compiler_params=params(),
        cost_estimate=cost(9_000_000_000, 14_000_000),
        name="grad_up",
    )(at, low, gu)


AXES = ("rep", "shard")


def pairs(move):
    found = []
    for y in range(2):
        for x in range(2):
            for z in range(4):
                for c in range(2):
                    j, i, k, d = move(y, x, z, c)
                    found.append(((y * 2 + x) * 8 + z * 2 + c, (j * 2 + i) * 8 + k * 2 + d))
    return found


CORE = pairs(lambda y, x, z, c: (y, x, z, 1 - c))
ACROSS = pairs(lambda y, x, z, c: (y, 1 - x, z, c))
ALONG = pairs(lambda y, x, z, c: (1 - y, x, z, c))
SHIFT = [None] + [pairs(lambda y, x, z, c, n=n: (y, x, (z + n) % 4, c)) for n in (1, 2, 3)]


def send(a, where):
    return lax.ppermute(a, AXES, where)


def tie(values, *after):
    flat, tree = jax.tree.flatten(values)
    return jax.tree.unflatten(tree, lax.optimization_barrier(tuple(flat) + tuple(jax.tree.leaves(after)))[: len(flat)])


def place(own, received, at_r, rows, out, base, quarter):
    y, x, z = at_r[0], at_r[1], at_r[2]
    cols = out.shape[1]
    half = rows // 2
    out[pl.ds(pl.multiple_of(base(z), 16), rows), :] = own
    for k in range(1, 4):
        start = base(lax.rem(z - k + 4, 4))
        for ab in range(2):
            at = pl.ds(pl.multiple_of(start + ab * half, 16), half)
            if quarter:
                wide = cols // 4
                for i in range(2):
                    for l in range(2):
                        one, two = (i, l) if ab == 0 else (l, i)
                        col = (lax.rem(x + i, 2) * 2 + lax.rem(y + l, 2)) * wide
                        out[at, pl.ds(pl.multiple_of(col, 128), wide)] = received(ab, one, two, k)
            else:
                wide = cols // 2
                for one in range(2):
                    col = lax.rem((x, y)[ab] + one, 2) * wide
                    out[at, pl.ds(pl.multiple_of(col, 128), wide)] = received(ab, one, 0, k)


def assemble_half_kernel(out_rows, at_r, *refs):
    n = len(out_rows)
    outs = refs[-n:]
    c = at_r[3]
    for turn, (own, ring, far_x, far_y) in ((c, refs[:4]), (1 - c, refs[4:8])):
        off = 0
        total_half = sum(out_rows) // 2
        for out, rows in zip(outs, out_rows):
            half = rows // 2

            def received(ab, one, two, k):
                if one == 0:
                    return ring[k - 1, ab * total_half + off : ab * total_half + off + half, :]
                return (far_x, far_y)[ab][k - 1, off : off + half, :]

            whole = jnp.concatenate([own[off : off + half], own[total_half + off : total_half + off + half]], axis=0)
            place(whole, received, at_r, rows, out, lambda z: (2 * z + turn) * rows, False)
            off += half


def assemble_quarter_kernel(at_r, *refs):
    out = refs[-1]
    c = at_r[3]
    for turn, (own, mine, first_a, first_b, second_a, second_b) in ((c, refs[:6]), (1 - c, refs[6:12])):
        rows = own.shape[0]
        half = rows // 2

        def received(ab, one, two, k):
            if two == 1:
                return (second_a, second_b)[ab][one, k - 1]
            if one == 1:
                return (first_a, first_b)[ab][k - 1]
            return mine[k - 1, ab * half : (ab + 1) * half, :]

        place(own[...], received, at_r, rows, out, lambda z: (2 * z + turn) * rows, True)


def assemble(kernel, at, parts, shapes):
    return pl.pallas_call(
        kernel,
        in_specs=[SMEM] + [VMEM] * len(parts),
        out_specs=[VMEM] * len(shapes),
        out_shape=[jax.ShapeDtypeStruct(s, bf16) for s in shapes],
        compiler_params=params(),
        cost_estimate=cost(0, sum(4 * s[0] * s[1] for s in shapes)),
        name="assemble",
    )(at, *parts)


def halves(w, x, y):
    half, wide = w.shape[0] // 2, w.shape[1] // 2
    a = lax.dynamic_slice(w, (0, x * wide), (half, wide))
    b = lax.dynamic_slice(w, (half, y * wide), (half, wide))
    return jnp.concatenate([a, b], axis=0)


def spread_half(ring, half):
    return send(ring[:, :half], ACROSS), send(ring[:, half : 2 * half], ALONG)


def swap(parts):
    return tuple(send(p, CORE) for p in parts)


def total(*terms):
    out = terms[0].astype(f32)
    for t in terms[1:]:
        out = out + t.astype(f32)
    return out.astype(bf16)


def finish_kernel(kind, at_r, *refs):
    y, x = at_r[0], at_r[1]
    blocks, outs = refs[:4], refs[4:]
    for ab, turn in ((0, x), (1, y)):
        one, two = (blocks[2 * ab + i][...].astype(f32) for i in range(2))
        left = jnp.where(turn == 0, one, two)
        right = jnp.where(turn == 0, two, one)
        both = jnp.concatenate([left, right], axis=1)
        if kind == "down":
            off = 0
            for out in outs:
                half = out.shape[0] // 2
                out[ab * half : (ab + 1) * half, :] = both[off : off + half]
                off += half
        else:
            rows = outs[0].shape[1]
            outs[0][ab] = both[:rows]
            if ab == 0:
                outs[1][...] = left[rows : rows + 16, :128]


def finish(at, kind, blocks, shapes):
    return pl.pallas_call(
        functools.partial(finish_kernel, kind),
        in_specs=[SMEM] + [VMEM] * len(blocks),
        out_specs=[VMEM] * len(shapes),
        out_shape=[jax.ShapeDtypeStruct(s, f32) for s in shapes],
        compiler_params=params(),
        cost_estimate=cost(0, 4_000_000),
        name="finish_" + kind,
    )(at, *blocks)


def pack(vectors, wide):
    block = jnp.concatenate([v.reshape(-1, vectors[1].shape[0]) for v in vectors] + [wide.reshape(4, -1)], axis=0)
    return jnp.pad(block, ((0, 16 - block.shape[0]), (0, 128 - block.shape[1])))


def whole_vectors(every, z, c, piece):
    k = lax.broadcasted_iota(jnp.int32, (2, 4, 8), 1)
    d = lax.broadcasted_iota(jnp.int32, (2, 4, 8), 0)
    s = lax.broadcasted_iota(jnp.int32, (2, 4, 8), 2)
    pick = (s == 2 * ((z - k) % 4) + (c + d) % 2).astype(bf16)
    table = jnp.einsum("dks,dkrl->srl", pick, every, preferred_element_type=f32).astype(bf16)
    table = table[:, :, :piece]
    wide = table[:, 8:12].reshape(1, -1)
    return table.transpose(1, 0, 2).reshape(16, -1), wide


class Sum:
    def __init__(self):
        self.own, self.got = [], []

    def add(self, own, other):
        self.own.append(own)
        self.got.append(send(other, CORE))

    def after(self, *values):
        self.got, self.far, self.parts = tie((self.got, self.far, self.parts), *values)

    far = parts = ()

    def pair(self, pick, *more):
        found = [total(pick(o), pick(g)) for o, g in zip(self.own, self.got)]
        found = found[0] if len(found) == 1 else jnp.concatenate(found, axis=-2)
        return total(found, *more) if more else found

    def halve(self):
        self.sent = self.pair(lambda a: a[0, 1]), self.pair(lambda a: a[1, 1])
        self.far = send(self.sent[0], ACROSS), send(self.sent[1], ALONG)

    def along_z(self):
        far = self.far
        self.mine = [jnp.stack([self.near(i, k) for i in range(2)]) for k in range(4)]
        self.sent = self.mine[1:]
        self.far = ()
        self.parts = [send(self.mine[k], SHIFT[k]) for k in range(1, 4)]

    def near(self, i, k):
        terms = []
        at = 0
        for o, g in zip(self.own, self.got):
            rows = o.shape[3]
            terms.append(total(o[i, 0, k], g[i, 0, k], self.far[i][k, at : at + rows]))
            at += rows
        return terms[0] if len(terms) == 1 else jnp.concatenate(terms, axis=0)

    def across(self):
        both = total(self.mine[0], *self.parts)
        self.got = self.parts = ()
        self.sent = both[0], both[1]
        self.far = send(both[0], ALONG), send(both[1], ACROSS)

    def share(self):
        a, b = (total(self.sent[i], self.far[i]) for i in range(2))
        self.sent = a, b
        self.out = a, send(a, ACROSS), b, send(b, ALONG)


def shards_near(
    tokens,
    cotangent,
    qkv_weight,
    query_value_bias,
    out_weight,
    out_bias,
    norm_one_gain,
    norm_one_shift,
    up_weight,
    up_bias,
    down_weight,
    down_bias,
    norm_two_gain,
    norm_two_shift,
    segment_ids,
    valid,
):
    length = segment_ids.shape[1]
    width = tokens.shape[1]
    groups = width // GW
    ff = up_bias.shape[0] * 8
    piece = out_bias.shape[0]
    r, s = lax.axis_index("rep"), lax.axis_index("shard")
    y, x, z, c = r // 2, r % 2, s // 2, s % 2
    at = jnp.stack([y, x, z, c]).astype(jnp.int32)

    half = piece // 2
    block = pack(
        (query_value_bias, out_bias, norm_one_gain, norm_one_shift, down_bias, norm_two_gain, norm_two_shift), up_bias
    )
    lines = lambda n, cols: jnp.pad(block.reshape(n, -1), ((0, 8 - n), (0, cols - 2048 // n)))
    dr = down_weight.shape[0] // 2
    own_q = jnp.concatenate([qkv_weight, lines(1, 3 * width)], axis=0)
    own_d = jnp.concatenate([down_weight[:dr], out_weight[:half], down_weight[dr:], out_weight[half:]], axis=0)
    other_q, other_u, other_d = swap((own_q, up_weight, own_d))
    held = jnp.concatenate([halves(qkv_weight, x, y), lines(2, 3 * width // 2)], axis=0)
    ring = []
    for step in range(3):
        if step == 2:
            held = tie(held, other_q, other_u, other_d)
        held = send(held, SHIFT[1])
        ring.append(held)
    ring_q = jnp.stack(ring)
    far_q = spread_half(ring_q, half)
    first_u = lax.dynamic_slice(up_weight, (0, (2 * x + y) * (ff // 4)), (piece, ff // 4))
    first_u = tie(first_u, held)
    ring_u = [send(first_u, SHIFT[k]) for k in range(1, 4)]
    rest_q = swap(tie((ring_q,) + far_q, ring_u))
    swapped_q = rest_q[0]
    parts_q = (own_q, ring_q) + far_q + (other_q,) + rest_q
    (wqkv,) = assemble(
        functools.partial(assemble_half_kernel, [qkv_weight.shape[0]]), at, parts_q, [(width, 3 * width)]
    )
    blocks = lambda own, ring: jnp.concatenate([own[None, piece : piece + 1, :2048].reshape(1, 16, 128), ring[:, piece : piece + 2, :1024].reshape(3, 16, 128)])
    vecs, bu = whole_vectors(jnp.stack([blocks(own_q, ring_q), blocks(other_q, swapped_q)]), z, c, piece)

    aq, ak = masks(segment_ids, valid)
    ring_u = jnp.stack(tie(ring_u, far_q))
    held = tie(halves(own_d, x, y), ring_u)
    ring = [send(held, SHIFT[1])]
    a, b = ring_u[:, :half], ring_u[:, half:]
    a2, b2 = send(a, ACROSS), send(b, ALONG)
    s0 = send(ring_u, CORE)
    saved = [attend(0, tie(tokens, a, b, held), wqkv, vecs, aq, ak, length)]
    a2, b2, s0, held = tie((a2, b2, s0, ring[0]), saved[0][3])
    ring = [held, send(held, SHIFT[1])]
    a3, b3 = jnp.stack([a, a2]), jnp.stack([b, b2])
    a4, b4 = send(a3, ALONG), send(b3, ACROSS)
    s2 = swap((a2, b2))
    saved.append(attend(1, tie(tokens, a3, b3, held), wqkv, vecs, aq, ak, length))
    a4, b4, s2, held = tie((a4, b4, s2, ring[1]), saved[1][3])
    ring = [ring[0], held, send(held, SHIFT[1])]
    s4 = swap((a4, b4))
    saved.append(attend(2, tie(tokens, a4, b4, held), wqkv, vecs, aq, ak, length))
    s4, held = tie((s4, ring[2]), saved[2][3])
    ring_d = jnp.stack([ring[0], ring[1], held])
    far_d = spread_half(ring_d, dr + half)
    parts_u = (up_weight, ring_u, a2, b2, a4, b4, other_u, s0) + s2 + s4
    (wu,) = assemble(assemble_quarter_kernel, at, parts_u, [(width, ff)])
    parts_d = (own_d, ring_d) + far_d + (other_d,) + swap((ring_d,) + far_d)
    wd, wo = assemble(
        functools.partial(assemble_half_kernel, [2 * dr, piece]), at, parts_d, [(ff, width), (width, width)]
    )

    ctx = [f[3] for f in saved]
    result, low, hid, gd, gu, gb, gc, vec, bup = middle(tokens, ctx, cotangent, wo, vecs, wu, bu, wd)

    down, up, qkv = Sum(), Sum(), Sum()
    own, other = grad_down(at, ctx, gb, hid, gd)
    down.add(own, other)
    own, other = grad_up(at, *tie((low, gu), other))
    up.add(own, other)
    down.after(other)
    down.halve()
    own, other, dx, db0 = attend_back("first", 0, at, saved[0], tie(gc, down.sent, other), aq, ak, tokens, wqkv, gb, length)
    down.after(dx)
    up.after(dx)
    down.along_z()
    up.halve()
    dx = tie(dx, down.sent, up.sent)
    own, other, dx, db1 = attend_back("second", 1, at, saved[1], gc, aq, ak, tokens, wqkv, dx, length, (own, other))
    two = own, other
    down.after(dx)
    up.after(dx)
    down.across()
    up.along_z()
    wide = bup[0].reshape(8, 4, piece).transpose(1, 0, 2).reshape(4, width)
    table = jnp.concatenate([vec[:6], wide, jnp.zeros((4, width), f32)], axis=0)
    dx = tie(dx, down.sent, up.sent)
    own, other, dx, _ = attend_back(
        "third", 2, at, saved[2], gc, aq, ak, tokens, wqkv, dx, length, (db0, db1, table)
    )
    down.after(dx)
    up.after(dx)
    qkv.add(two[0], tie(two[1], down.far, up.parts))
    qkv.add(own, tie(other, down.far, up.parts))
    down.share()
    up.across()
    qkv.halve()
    up.share()
    qkv.along_z()
    qkv.across()
    qkv.share()
    dwd, dwo = finish(at, "down", down.out, [down_weight.shape, out_weight.shape])
    (dwu,) = finish(at, "down", up.out, [up_weight.shape])
    q, small = finish(at, "qkv", qkv.out, [(2, 3 * half, 3 * GW), (16, 128)])
    by_group = [q[:, g * half : (g + 1) * half].reshape(piece, 3, GW) for g in range(groups)]
    dwq = jnp.concatenate([q[:, i] for i in range(3) for q in by_group], axis=1)
    one = lambda i: small[i, :piece]
    return (
        result,
        dx,
        dwq,
        small[:2, :piece],
        dwo,
        one(2),
        one(3),
        one(4),
        dwu,
        small[8:12, :piece].reshape(-1),
        dwd,
        one(5),
        one(6),
        one(7),
    )


def spread(args):
    flat = [a.reshape(-1) for a in args]
    packed = jnp.concatenate(flat)
    every = lax.all_gather(packed, "shard", axis=0)
    out, at = [], 0
    for a in args:
        part = every[:, at : at + a.size].reshape((-1,) + a.shape)
        at += a.size
        out.append(jnp.moveaxis(part, 0, -2).reshape(a.shape[:-1] + (-1,)))
    return out


def shards(
    tokens,
    cotangent,
    qkv_weight,
    query_value_bias,
    out_weight,
    out_bias,
    norm_one_gain,
    norm_one_shift,
    up_weight,
    up_bias,
    down_weight,
    down_bias,
    norm_two_gain,
    norm_two_shift,
    segment_ids,
    valid,
):
    length = segment_ids.shape[1]
    width = tokens.shape[1]
    groups = width // GW
    gather = lambda a: lax.all_gather(a, "shard", axis=0, tiled=True)
    *rest, bu = spread(
        (query_value_bias, out_bias, norm_one_gain, norm_one_shift, down_bias, norm_two_gain, norm_two_shift, up_bias)
    )
    vecs = jnp.concatenate([v.reshape(-1, width) for v in rest] + [jnp.zeros((8, width), bf16)], axis=0)
    wqkv, wd, wo, wu = gather(qkv_weight), gather(down_weight), gather(out_weight), gather(up_weight)
    at = jnp.zeros((4,), jnp.int32)
    aq, ak = masks(segment_ids, valid)
    saved = [attend(g, tokens, wqkv, vecs, aq, ak, length) for g in range(groups)]
    ctx = [f[3] for f in saved]
    result, low, hid, gd, gu, gb, gc, vec, bup = middle(tokens, ctx, cotangent, wo, vecs, wu, bu[None], wd)
    dwd = tn(hid, gd).astype(bf16)
    dwu = tn(low, gu).astype(bf16)
    dwo = tn(jnp.concatenate(ctx, axis=1), gb).astype(bf16)
    dx, dws, dbs = gb, [], []
    for g in range(groups):
        dw, dx, db = attend_back("plain", g, at, saved[g], gc, aq, ak, tokens, wqkv, dx, length)
        dws.append(dw)
        dbs.append(db)
    dwq = jnp.concatenate([dw[i] for i in range(3) for dw in dws], axis=1)
    db = jnp.stack(dbs).reshape(groups, 3, GW).transpose(1, 0, 2).reshape(3, width)
    small = jnp.concatenate([db[0], db[2], vec[:6].reshape(-1), bup[0]])
    small = lax.psum(small.reshape(-1, 128), ("rep", "shard")).reshape(-1)

    def owned(a):
        part = lax.psum_scatter(a, "shard", scatter_dimension=0, tiled=True)
        return lax.psum(part, "rep").astype(f32)

    rank = lax.axis_index("shard")
    own = lambda at, size: lax.dynamic_slice(small, (at + rank * size,), (size,))
    piece = out_bias.shape[0]
    vs = [own(width * i, piece) for i in range(8)]
    dbu = own(8 * width, up_bias.shape[0])
    gd_w, gu_w, go_w, gq_w = owned(dwd), owned(dwu), owned(dwo), owned(dwq)
    return result, dx, gq_w, jnp.stack(vs[:2]), go_w, vs[2], vs[3], vs[4], gu_w, dbu, gd_w, vs[5], vs[6], vs[7]


def solution(mesh):
    rows, one = P(("rep", "shard"), None), P("shard")
    mat, two = P("shard", None), P(None, "shard")
    near = mesh.shape["rep"] == 4 and mesh.shape["shard"] == 8
    return jax.shard_map(
        shards_near if near else shards,
        mesh=mesh,
        in_specs=(rows, rows, mat, two, mat, one, one, one, mat, one, mat, one, one, one, rows, rows),
        out_specs=(rows, rows, mat, two, mat, one, one, one, mat, one, mat, one, one, one),
        check_vma=False,
    )
```

```python
import functools

import jax
import jax.numpy as jnp
from jax import lax
from jax.experimental import pallas as pl
from jax.experimental.pallas import tpu as pltpu
from jax.sharding import PartitionSpec as P

HD = 64
GW = 256
SCALE = 0.125 * 1.4426950408889634
BIG = 1e30
VMEM_LIMIT = 60 * 1024 * 1024
bf16 = jnp.bfloat16
f32 = jnp.float32
SMEM = pl.BlockSpec(memory_space=pltpu.SMEM)
VMEM = pl.BlockSpec(memory_space=pltpu.VMEM)


def nn(a, b):
    return lax.dot_general(a, b, (((1,), (0,)), ((), ())), preferred_element_type=f32)


def nt(a, b):
    return lax.dot_general(a, b, (((1,), (1,)), ((), ())), preferred_element_type=f32)


def tn(a, b):
    return lax.dot_general(a, b, (((0,), (0,)), ((), ())), preferred_element_type=f32)


def params(**more):
    return pltpu.CompilerParams(vmem_limit_bytes=VMEM_LIMIT, **more)


def cost(flops, moved):
    return pl.CostEstimate(flops=flops, bytes_accessed=moved, transcendentals=0)


def attend_kernel(tok, wq, wk, wv, vecs, aq, ak, q_o, k_o, v_o, ctx_o, lse_o):
    x = tok[...]
    q = (nn(x, wq[...]) + vecs[0:1, :].astype(f32)).astype(bf16)
    k = nn(x, wk[...]).astype(bf16)
    v = (nn(x, wv[...]) + vecs[1:2, :].astype(f32)).astype(bf16)
    q_o[...] = q
    k_o[...] = k
    v_o[...] = v
    length, width = q.shape
    lane = lax.broadcasted_iota(jnp.int32, (length, width), 1) // HD
    slot = lax.broadcasted_iota(jnp.int32, (length, 128), 1)
    acc = None
    scale = jnp.zeros((length, width), f32)
    stat = jnp.zeros((length, 128), f32)
    for h in range(width // HD):
        mine = lane == h
        qa = jnp.where(mine, q, aq[...])
        ka = jnp.where(mine, k, ak[...])
        va = jnp.where(mine, v, jnp.zeros_like(v))
        t = nt(qa, ka) * SCALE
        m = jnp.max(t, axis=1, keepdims=True)
        p = jnp.exp2(t - m)
        total = jnp.sum(p, axis=1, keepdims=True)
        part = nn(p.astype(bf16), va)
        acc = part if acc is None else acc + part
        scale = jnp.where(mine, 1.0 / total, scale)
        stat = jnp.where(slot == h, m + jnp.log2(total), stat)
    ctx_o[...] = (acc * scale).astype(bf16)
    lse_o[0] = stat.T[:8]


def attend(g, tokens, w, vecs, aq, ak, length):
    rows, width = tokens.shape
    groups = width // GW
    seqs = rows // length
    col = lambda o: pl.BlockSpec((width, GW), lambda b: (0, o * groups + g))
    seq = pl.BlockSpec((length, width), lambda b: (b, 0))
    blk = pl.BlockSpec((length, GW), lambda b: (b, 0))
    act = jax.ShapeDtypeStruct((rows, GW), bf16)
    return pl.pallas_call(
        attend_kernel,
        grid=(seqs,),
        in_specs=[seq, col(0), col(1), col(2), pl.BlockSpec((16, GW), lambda b: (0, g)), blk, blk],
        out_specs=[blk, blk, blk, blk, pl.BlockSpec((1, 8, length), lambda b: (b, 0, 0))],
        out_shape=[act, act, act, act, jax.ShapeDtypeStruct((seqs, 8, length), f32)],
        compiler_params=params(),
        cost_estimate=cost(4_000_000_000, 5_000_000),
        name="attend",
    )(tokens, w, w, w, vecs, aq, ak)


def owner_of(s, at_r):
    return lax.rem(s // 2 - at_r[2] + 4, 4), at_r[3] != s % 2


def select_lanes(s, piece, width):
    i = lax.broadcasted_iota(jnp.int32, (128, width), 0)
    j = lax.broadcasted_iota(jnp.int32, (128, width), 1)
    return ((j == s * piece + i) & (i < piece)).astype(f32).astype(bf16)


def attend_back_kernel(mode, at_r, q_r, k_r, v_r, do_r, ctx_r, lse_r, aq, ak, tok, wq, wk, wv, dx_i, *rest):
    b = pl.program_id(0)
    last = b == pl.num_programs(0) - 1
    if mode == "plain":
        dw_o, dx_o, db_o, dw_s = rest
    elif mode == "first":
        own_o, other_o, dx_o, db_o, dw_s = rest
    elif mode == "second":
        _, _, own_o, other_o, dx_o, db_o, dw_s = rest
    else:
        db0, db1, tbl, own_o, other_o, dx_o, db_o, dw_s = rest
    q, k, v, do = q_r[...], k_r[...], v_r[...], do_r[...]
    length, width = q.shape
    lane = lax.broadcasted_iota(jnp.int32, (length, width), 1) // HD
    sel = lax.broadcasted_iota(jnp.int32, (8, width), 1) // HD == lax.broadcasted_iota(jnp.int32, (8, width), 0)
    sel = sel.astype(f32).astype(bf16)
    prod = do.astype(f32) * ctx_r[...].astype(f32)
    hi = prod.astype(bf16)
    lo = (prod - hi.astype(f32)).astype(bf16)
    delta = nt(sel, hi) + nt(sel, lo)
    dq = dk = dv = None
    zero = jnp.zeros_like(q)
    for h in range(width // HD):
        mine = lane == h
        qa = jnp.where(mine, q, aq[...])
        ka = jnp.where(mine, k, ak[...])
        va = jnp.where(mine, v, zero)
        p = jnp.exp2(nt(ka, qa) * SCALE - lse_r[0, h : h + 1, :])
        dp = nt(va, do)
        ds = (p * (dp - delta[h : h + 1, :])).astype(bf16)
        dv_h = nn(p.astype(bf16), jnp.where(mine, do, zero))
        dk_h = nn(ds, jnp.where(mine, q, zero))
        dq_h = tn(ds, jnp.where(mine, k, zero))
        dv = dv_h if dv is None else dv + dv_h
        dk = dk_h if dk is None else dk + dk_h
        dq = dq_h if dq is None else dq + dq_h
    dq = (dq * 0.125).astype(bf16)
    dk = (dk * 0.125).astype(bf16)
    dv = dv.astype(bf16)
    back = jnp.concatenate([dq, dk, dv], axis=1)
    dw = tn(tok[...], back)
    dx = nt(dq, wq[...]) + nt(dk, wk[...]) + nt(dv, wv[...])
    dx_o[...] = (dx_i[...].astype(f32) + dx).astype(dx_o.dtype)
    sums = jnp.sum(back.astype(f32), axis=0, keepdims=True)

    @pl.when(b == 0)
    def _():
        dw_s[...] = dw
        db_o[...] = sums

    @pl.when(b > 0)
    def _():
        dw_s[...] += dw
        db_o[...] += sums

    @pl.when(last)
    def _():
        if mode == "plain":
            for i in range(3):
                dw_o[i] = dw_s[:, i * width : (i + 1) * width].astype(bf16)
            return
        res = dw_s[...].astype(bf16)
        piece = res.shape[0] // 8
        half, wide = piece // 2, res.shape[1] // 2
        for s in range(8):
            kk, far = owner_of(s, at_r)
            for ab, turn in ((0, at_r[1]), (1, at_r[0])):
                for h in range(2):
                    val = res[s * piece + ab * half : s * piece + (ab + 1) * half, h * wide : (h + 1) * wide]
                    rel = lax.rem(h + turn, 2)
                    for ref, cond in ((other_o, far), (own_o, ~far)):

                        @pl.when(cond)
                        def _(val=val, rel=rel, kk=kk, ab=ab, ref=ref):
                            ref[ab, rel, kk, 0:half] = val

        if mode == "third":
            sums = [r[...] for r in (db0, db1, db_o)]
            dbq = jnp.concatenate([r[:, :width] for r in sums], axis=1)
            dbv = jnp.concatenate([r[:, 2 * width :] for r in sums], axis=1)
            table = jnp.concatenate([dbq, dbv, tbl[...]], axis=0).astype(bf16)
            extra = jnp.zeros((4, 16, wide), bf16)
            for ab in range(2):
                for h in range(2):
                    own_o[ab, h, :, half : half + 16, :] = extra
                    other_o[ab, h, :, half : half + 16, :] = extra
            for s in range(8):
                blk = nt(table, select_lanes(s, piece, table.shape[1])).astype(bf16)
                kk, far = owner_of(s, at_r)
                for ref, cond in ((other_o, far), (own_o, ~far)):

                    @pl.when(cond)
                    def _(blk=blk, kk=kk, ref=ref):
                        ref[0, at_r[1], kk, half : half + 16, 0:128] = blk


def attend_back(mode, g, at, saved, gc, aq, ak, tokens, w, dx, length, extra=()):
    rows, width = tokens.shape
    groups = width // GW
    seqs = rows // length
    half = width // 16
    col = lambda o: pl.BlockSpec((width, GW), lambda b: (0, o * groups + g))
    seq = pl.BlockSpec((length, width), lambda b: (b, 0))
    blk = pl.BlockSpec((length, GW), lambda b: (b, 0))
    whole = lambda s: pl.BlockSpec(s, lambda b: (0,) * len(s))
    S = jax.ShapeDtypeStruct
    tall = {"first": 2 * half, "second": 2 * half, "third": half + 16, "plain": 0}[mode]
    at_row = 1 if mode == "second" else 0
    block = half + 16 if mode == "third" else half
    part = pl.BlockSpec((2, 2, 4, block, 3 * GW // 2), lambda b: (0, 0, 0, at_row, 0))
    if mode == "plain":
        out_specs, out_shape = [whole((3, width, GW))], [S((3, width, GW), bf16)]
    else:
        out_specs, out_shape = [part, part], [S((2, 2, 4, tall, 3 * GW // 2), bf16)] * 2
    out_specs += [seq, whole((1, 3 * GW))]
    out_shape += [S((rows, width), bf16 if mode == "third" or g == groups - 1 else f32), S((1, 3 * GW), f32)]
    in_specs = [SMEM, blk, blk, blk, pl.BlockSpec((length, GW), lambda b: (b, g)), blk]
    in_specs += [pl.BlockSpec((1, 8, length), lambda b: (b, 0, 0)), blk, blk, seq, col(0), col(1), col(2), seq]
    aliases = {}
    if mode == "second":
        in_specs += [pl.BlockSpec(memory_space=pl.ANY)] * 2
        aliases = {len(in_specs) - 2: 0, len(in_specs) - 1: 1}
    elif mode == "third":
        in_specs += [whole(e.shape) for e in extra]
    q, k, v, ctx, lse = saved
    return pl.pallas_call(
        functools.partial(attend_back_kernel, mode),
        grid=(seqs,),
        in_specs=in_specs,
        out_specs=out_specs,
        out_shape=out_shape,
        scratch_shapes=[pltpu.VMEM((width, 3 * GW), f32)],
        input_output_aliases=aliases,
        compiler_params=params(),
        cost_estimate=cost(8_000_000_000, 8_000_000),
        name="attend_back",
    )(at, q, k, v, gc, ctx, lse, aq, ak, tokens, w, w, w, dx, *extra)


def masks(segment_ids, valid):
    code = (segment_ids + 8 * valid).reshape(-1, 1)
    lane = lax.broadcasted_iota(jnp.int32, (1, GW), 1) % HD
    same = code == lane
    aq = same.astype(bf16)
    ak = jnp.where((lane < 16) & ~same, -BIG, 0.0).astype(bf16)
    return aq, ak


def phi(x):
    return 0.5 * (1.0 + lax.erf(x * 0.7071067811865476)), jnp.exp(-0.5 * x * x) * 0.3989422804014327


def middle_kernel(groups, tok, *refs):
    ctx_r = refs[:groups]
    cot, wo, vecs, wu, bu, wd, out_o, low_o, hid_o, gd_o, gu_o, gb_o, gc_o, vec_o, bup_o, slope = refs[groups:]
    i = pl.program_id(0)
    width = tok.shape[1]
    ff = wd.shape[0]
    step = width
    chunks = ff // step
    bo, g1, s1, bd, g2, s2 = (vecs[j : j + 1, :].astype(f32) for j in range(2, 8))
    ctx = jnp.concatenate([r[...] for r in ctx_r], axis=1)
    pre = tok[...].astype(f32) + nn(ctx, wo[...]) + bo
    mean = lambda v: jnp.mean(v, axis=1, keepdims=True)
    centre = pre - mean(pre)
    r1 = lax.rsqrt(mean(centre * centre) + 1e-05)
    n1 = centre * r1
    normed = n1 * g1 + s1
    low = normed.astype(bf16)
    low_o[...] = low
    acc = normed + bd
    for c in range(chunks):
        cols = slice(c * step, (c + 1) * step)
        hp = nn(low, wu[:, cols]) + bu[:, cols].astype(f32)
        cdf, pdf = phi(hp)
        slope[:, cols] = cdf + hp * pdf
        hid = (hp * cdf).astype(bf16)
        hid_o[:, cols] = hid
        acc = acc + nn(hid, wd[cols, :])
    centre = acc - mean(acc)
    r2 = lax.rsqrt(mean(centre * centre) + 1e-05)
    n2 = centre * r2
    out_o[...] = (n2 * g2 + s2).astype(bf16)
    ct = cot[...].astype(f32)
    e = ct * g2
    gp2 = r2 * (e - mean(e) - n2 * mean(e * n2))
    gd = gp2.astype(bf16)
    gd_o[...] = gd
    acc = gp2
    total = lambda v: jnp.sum(v, axis=0, keepdims=True)

    def put(ref, at, v):
        @pl.when(i == 0)
        def _():
            ref[at] = v

        @pl.when(i > 0)
        def _():
            ref[at] += v

    for c in range(chunks):
        cols = slice(c * step, (c + 1) * step)
        gu = (nt(gd, wd[cols, :]) * slope[:, cols]).astype(bf16)
        gu_o[:, cols] = gu
        put(bup_o, (slice(0, 1), cols), total(gu.astype(f32)))
        acc = acc + nt(gu, wu[:, cols])
    e = acc * g1
    gp1 = r1 * (e - mean(e) - n1 * mean(e * n1))
    gb = gp1.astype(bf16)
    gb_o[...] = gb
    gc_o[...] = nt(gb, wo[...]).astype(bf16)
    for at, v in enumerate((gb.astype(f32), acc * n1, acc, gd.astype(f32), ct * n2, ct)):
        put(vec_o, (slice(at, at + 1), slice(None)), total(v))


def middle(tokens, ctx, cot, wo, vecs, wu, bu, wd, tile=256):
    rows, width = tokens.shape
    ff = wd.shape[0]
    act = pl.BlockSpec((tile, width), lambda i: (i, 0))
    wide = pl.BlockSpec((tile, ff), lambda i: (i, 0))
    whole = lambda a: pl.BlockSpec(a.shape, lambda i: (0, 0), pipeline_mode=pl.Buffered(1))
    S = jax.ShapeDtypeStruct
    shapes = [(rows, width), (rows, width), (rows, ff), (rows, width), (rows, ff), (rows, width), (rows, width)]
    return pl.pallas_call(
        functools.partial(middle_kernel, len(ctx)),
        grid=(rows // tile,),
        in_specs=[act] + [pl.BlockSpec((tile, GW), lambda i: (i, 0)) for _ in ctx] + [act] + [whole(a) for a in (wo, vecs, wu, bu, wd)],
        out_specs=[act, act, wide, act, wide, act, act, pl.BlockSpec((8, width), lambda i: (0, 0)), pl.BlockSpec((8, ff), lambda i: (0, 0))],
        out_shape=[S(s, bf16) for s in shapes] + [S((8, width), f32), S((8, ff), f32)],
        scratch_shapes=[pltpu.VMEM((tile, ff), f32)],
        compiler_params=params(),
        cost_estimate=cost(30_000_000_000, 40_000_000),
        name="middle",
    )(tokens, *ctx, cot, wo, vecs, wu, bu, wd)


def grad_down_kernel(groups, at_r, *refs):
    ctx = refs[:groups]
    gb, hid, gd, own_o, other_o = refs[groups:]
    p = pl.program_id(0)
    turns = ((0, at_r[1]), (1, at_r[0]))
    wide = gd.shape[1] // 2
    tall = hid.shape[1] // 2

    @pl.when(p == 0)
    def _():
        lhs = jnp.concatenate([r[...] for r in ctx], axis=1)
        res = tn(lhs, gb[...]).astype(bf16)
        piece = res.shape[0] // 8
        half = piece // 2
        for s in range(8):
            kk, far = owner_of(s, at_r)
            for ab, turn in turns:
                for h in range(2):
                    val = res[s * piece + ab * half : s * piece + (ab + 1) * half, h * wide : (h + 1) * wide]
                    rel = lax.rem(h + turn, 2)
                    for ref, cond in ((other_o, far), (own_o, ~far)):

                        @pl.when(cond)
                        def _(val=val, rel=rel, kk=kk, ab=ab, ref=ref):
                            ref[ab, rel, kk, tall : tall + half] = val

    @pl.when(p > 0)
    def _():
        res = tn(hid[...], gd[...]).astype(bf16)
        kk = lax.rem(p - 1, 4)
        for ab, turn in turns:
            for h in range(2):
                val = res[ab * tall : (ab + 1) * tall, h * wide : (h + 1) * wide]
                rel = lax.rem(h + turn, 2)
                for ref, cond in ((other_o, p < 5), (own_o, p >= 5)):

                    @pl.when(cond)
                    def _(val=val, rel=rel, ab=ab, ref=ref):
                        ref[ab, rel, kk, 0:tall] = val


def grad_down(at, ctx, gb, hid, gd):
    rows, ff = hid.shape
    width = gd.shape[1]
    piece = ff // 8
    part = (2, 2, 4, (piece + width // 8) // 2, width // 2)

    def owner(p, at_r):
        j = jnp.maximum(p - 1, 0)
        z = lax.rem(at_r[2] + lax.rem(j, 4), 4)
        return 0, 2 * z + jnp.where(j < 4, 1 - at_r[3], at_r[3])

    whole = lambda s: pl.BlockSpec(s, lambda p, at_r: (0,) * len(s))
    return pl.pallas_call(
        functools.partial(grad_down_kernel, len(ctx)),
        grid_spec=pltpu.PrefetchScalarGridSpec(
            num_scalar_prefetch=1,
            grid=(9,),
            in_specs=[whole(c.shape) for c in ctx] + [whole(gb.shape), pl.BlockSpec((rows, piece), owner), whole(gd.shape)],
            out_specs=[whole(part), whole(part)],
        ),
        out_shape=[jax.ShapeDtypeStruct(part, bf16)] * 2,
        compiler_params=params(),
        cost_estimate=cost(9_000_000_000, 14_000_000),
        name="grad_down",
    )(at, *ctx, gb, hid, gd)


def grad_up_kernel(at_r, low, gu, own_o, other_o, turned):
    j = pl.program_id(0)
    y, x = at_r[0], at_r[1]

    @pl.when(j == 0)
    def _():
        turned[...] = low[...].T

    res = nn(turned[...], gu[...]).astype(bf16)
    piece = res.shape[0] // 8
    half = piece // 2
    h = j // 4
    row = pl.multiple_of(lax.rem(j, 4) * half, 16)
    for s in range(8):
        kk, far = owner_of(s, at_r)
        for ab, turn in ((0, x), (1, y)):
            val = res[s * piece + ab * half : s * piece + (ab + 1) * half]
            for ref, cond in ((other_o, far), (own_o, ~far)):

                @pl.when(cond)
                def _(val=val, kk=kk, ab=ab, turn=turn, ref=ref):
                    ref[ab, lax.rem(h + turn, 2), kk, pl.ds(row, half), :] = val


def grad_up(at, low, gu):
    rows, width = low.shape
    ff = gu.shape[1]
    step = ff // 8
    part = (2, 2, 4, width // 4, ff // 8)
    whole = pl.BlockSpec(part, lambda j: (0, 0, 0, 0, 0))
    return pl.pallas_call(
        grad_up_kernel,
        grid=(8,),
        in_specs=[SMEM, pl.BlockSpec((rows, width), lambda j: (0, 0)), pl.BlockSpec((rows, step), lambda j: (0, j))],
        out_specs=[whole, whole],
        out_shape=[jax.ShapeDtypeStruct(part, bf16)] * 2,
        scratch_shapes=[pltpu.VMEM((width, rows), bf16)],
        compiler_params=params(),
        cost_estimate=cost(9_000_000_000, 14_000_000),
        name="grad_up",
    )(at, low, gu)


AXES = ("rep", "shard")


def pairs(move):
    found = []
    for y in range(2):
        for x in range(2):
            for z in range(4):
                for c in range(2):
                    j, i, k, d = move(y, x, z, c)
                    found.append(((y * 2 + x) * 8 + z * 2 + c, (j * 2 + i) * 8 + k * 2 + d))
    return found


CORE = pairs(lambda y, x, z, c: (y, x, z, 1 - c))
ACROSS = pairs(lambda y, x, z, c: (y, 1 - x, z, c))
ALONG = pairs(lambda y, x, z, c: (1 - y, x, z, c))
SHIFT = [None] + [pairs(lambda y, x, z, c, n=n: (y, x, (z + n) % 4, c)) for n in (1, 2, 3)]


def send(a, where):
    return lax.ppermute(a, AXES, where)


def tie(values, *after):
    flat, tree = jax.tree.flatten(values)
    return jax.tree.unflatten(tree, lax.optimization_barrier(tuple(flat) + tuple(jax.tree.leaves(after)))[: len(flat)])


def place(own, received, at_r, rows, out, base, quarter):
    y, x, z = at_r[0], at_r[1], at_r[2]
    cols = out.shape[1]
    half = rows // 2
    out[pl.ds(pl.multiple_of(base(z), 16), rows), :] = own
    for k in range(1, 4):
        start = base(lax.rem(z - k + 4, 4))
        for ab in range(2):
            at = pl.ds(pl.multiple_of(start + ab * half, 16), half)
            if quarter:
                wide = cols // 4
                for i in range(2):
                    for l in range(2):
                        one, two = (i, l) if ab == 0 else (l, i)
                        col = (lax.rem(x + i, 2) * 2 + lax.rem(y + l, 2)) * wide
                        out[at, pl.ds(pl.multiple_of(col, 128), wide)] = received(ab, one, two, k)
            else:
                wide = cols // 2
                for one in range(2):
                    col = lax.rem((x, y)[ab] + one, 2) * wide
                    out[at, pl.ds(pl.multiple_of(col, 128), wide)] = received(ab, one, 0, k)


def assemble_half_kernel(out_rows, at_r, *refs):
    n = len(out_rows)
    outs = refs[-n:]
    c = at_r[3]
    for turn, (own, ring, far_x, far_y) in ((c, refs[:4]), (1 - c, refs[4:8])):
        off = 0
        total_half = sum(out_rows) // 2
        for out, rows in zip(outs, out_rows):
            half = rows // 2

            def received(ab, one, two, k):
                if one == 0:
                    return ring[k - 1, ab * total_half + off : ab * total_half + off + half, :]
                return (far_x, far_y)[ab][k - 1, off : off + half, :]

            whole = jnp.concatenate([own[off : off + half], own[total_half + off : total_half + off + half]], axis=0)
            place(whole, received, at_r, rows, out, lambda z: (2 * z + turn) * rows, False)
            off += half


def assemble_quarter_kernel(at_r, *refs):
    out = refs[-1]
    c = at_r[3]
    for turn, (own, near_a, near_b, far) in ((c, refs[:4]), (1 - c, refs[4:8])):
        rows = own.shape[0]

        def received(ab, one, two, k):
            if two == 1:
                return far[ab, one, k - 1]
            return (near_a, near_b)[ab][one, k - 1]

        place(own[...], received, at_r, rows, out, lambda z: (2 * z + turn) * rows, True)


def assemble(kernel, at, parts, shapes):
    return pl.pallas_call(
        kernel,
        in_specs=[SMEM] + [VMEM] * len(parts),
        out_specs=[VMEM] * len(shapes),
        out_shape=[jax.ShapeDtypeStruct(s, bf16) for s in shapes],
        compiler_params=params(),
        cost_estimate=cost(0, sum(4 * s[0] * s[1] for s in shapes)),
        name="assemble",
    )(at, *parts)


def halves(w, x, y):
    half, wide = w.shape[0] // 2, w.shape[1] // 2
    a = lax.dynamic_slice(w, (0, x * wide), (half, wide))
    b = lax.dynamic_slice(w, (half, y * wide), (half, wide))
    return jnp.concatenate([a, b], axis=0)


def spread_half(ring, half):
    return send(ring[:, :half], ACROSS), send(ring[:, half : 2 * half], ALONG)


def swap(parts):
    return tuple(send(p, CORE) for p in parts)


def total(*terms):
    out = terms[0].astype(f32)
    for t in terms[1:]:
        out = out + t.astype(f32)
    return out.astype(bf16)


def finish_kernel(kind, at_r, *refs):
    y, x = at_r[0], at_r[1]
    blocks, outs = refs[:4], refs[4:]
    for ab, turn in ((0, x), (1, y)):
        one, two = (blocks[2 * ab + i][...].astype(f32) for i in range(2))
        left = jnp.where(turn == 0, one, two)
        right = jnp.where(turn == 0, two, one)
        both = jnp.concatenate([left, right], axis=1)
        if kind == "ffn":
            off = 0
            for out in outs[:2]:
                half = out.shape[0] // 2
                out[ab * half : (ab + 1) * half, :] = both[off : off + half]
                off += half
            half = outs[2].shape[0] // 2
            eighth = left.shape[1]
            for i in range(4):
                for h, val in ((0, left), (1, right)):
                    col = (4 * h + i) * eighth
                    outs[2][ab * half : (ab + 1) * half, col : col + eighth] = val[off + i * half : off + (i + 1) * half]
        else:
            half = outs[0].shape[0] // 2
            groups = outs[0].shape[1] // (3 * GW)
            for g in range(groups):
                for i in range(3):
                    col = (i * groups + g) * GW
                    outs[0][ab * half : (ab + 1) * half, col : col + GW] = both[g * half : (g + 1) * half, i * GW : (i + 1) * GW]
            if ab == 0:
                rows = groups * half
                outs[1][...] = left[rows : rows + 16, :128]


def finish(at, kind, blocks, shapes):
    return pl.pallas_call(
        functools.partial(finish_kernel, kind),
        in_specs=[SMEM] + [VMEM] * len(blocks),
        out_specs=[VMEM] * len(shapes),
        out_shape=[jax.ShapeDtypeStruct(s, f32) for s in shapes],
        compiler_params=params(),
        cost_estimate=cost(0, 4_000_000),
        name="finish_" + kind,
    )(at, *blocks)


def pack(vectors, wide):
    block = jnp.concatenate([v.reshape(-1, vectors[1].shape[0]) for v in vectors] + [wide.reshape(4, -1)], axis=0)
    return jnp.pad(block, ((0, 16 - block.shape[0]), (0, 128 - block.shape[1])))


def whole_vectors(every, z, c, piece):
    k = lax.broadcasted_iota(jnp.int32, (2, 4, 8), 1)
    d = lax.broadcasted_iota(jnp.int32, (2, 4, 8), 0)
    s = lax.broadcasted_iota(jnp.int32, (2, 4, 8), 2)
    pick = (s == 2 * ((z - k) % 4) + (c + d) % 2).astype(bf16)
    table = jnp.einsum("dks,dkrl->srl", pick, every, preferred_element_type=f32).astype(bf16)
    table = table[:, :, :piece]
    wide = table[:, 8:12].reshape(1, -1)
    return table.transpose(1, 0, 2).reshape(16, -1), wide


class Sum:
    def __init__(self):
        self.own, self.got = [], []

    def add(self, own, other):
        self.own.append(own)
        self.got.append(send(other, CORE))

    def after(self, *values):
        self.got, self.far, self.parts = tie((self.got, self.far, self.parts), *values)

    far = parts = ()

    def pair(self, pick, *more):
        found = [total(pick(o), pick(g)) for o, g in zip(self.own, self.got)]
        found = found[0] if len(found) == 1 else jnp.concatenate(found, axis=-2)
        return total(found, *more) if more else found

    def halve(self):
        self.sent = self.pair(lambda a: a[0, 1]), self.pair(lambda a: a[1, 1])
        self.far = send(self.sent[0], ACROSS), send(self.sent[1], ALONG)

    def along_z(self):
        far = self.far
        self.mine = [jnp.stack([self.near(i, k) for i in range(2)]) for k in range(4)]
        self.sent = self.mine[1:]
        self.far = ()
        self.parts = [send(self.mine[k], SHIFT[k]) for k in range(1, 4)]

    def near(self, i, k):
        terms = []
        at = 0
        for o, g in zip(self.own, self.got):
            rows = o.shape[3]
            terms.append(total(o[i, 0, k], g[i, 0, k], self.far[i][k, at : at + rows]))
            at += rows
        return terms[0] if len(terms) == 1 else jnp.concatenate(terms, axis=0)

    def across(self, *more):
        both = [total(v.mine[0], *v.parts) for v in (self,) + more]
        both = both[0] if len(both) == 1 else jnp.concatenate(both, axis=1)
        self.got = self.parts = ()
        self.sent = both[0], both[1]
        self.far = send(both[0], ALONG), send(both[1], ACROSS)

    def share(self):
        a, b = (total(self.sent[i], self.far[i]) for i in range(2))
        self.sent = a, b
        self.out = a, send(a, ACROSS), b, send(b, ALONG)


def shards_near(
    tokens,
    cotangent,
    qkv_weight,
    query_value_bias,
    out_weight,
    out_bias,
    norm_one_gain,
    norm_one_shift,
    up_weight,
    up_bias,
    down_weight,
    down_bias,
    norm_two_gain,
    norm_two_shift,
    segment_ids,
    valid,
):
    length = segment_ids.shape[1]
    width = tokens.shape[1]
    groups = width // GW
    ff = up_bias.shape[0] * 8
    piece = out_bias.shape[0]
    r, s = lax.axis_index("rep"), lax.axis_index("shard")
    y, x, z, c = r // 2, r % 2, s // 2, s % 2
    at = jnp.stack([y, x, z, c]).astype(jnp.int32)

    half = piece // 2
    block = pack(
        (query_value_bias, out_bias, norm_one_gain, norm_one_shift, down_bias, norm_two_gain, norm_two_shift), up_bias
    )
    lines = lambda n, cols: jnp.pad(block.reshape(n, -1), ((0, 8 - n), (0, cols - 2048 // n)))
    dr = down_weight.shape[0] // 2
    own_q = jnp.concatenate([qkv_weight, lines(1, 3 * width)], axis=0)
    own_d = jnp.concatenate([down_weight[:dr], out_weight[:half], down_weight[dr:], out_weight[half:]], axis=0)
    other_q, other_u, other_d = swap((own_q, up_weight, own_d))
    held = jnp.concatenate([halves(qkv_weight, x, y), lines(2, 3 * width // 2)], axis=0)
    ring = []
    for step in range(3):
        if step == 2:
            held = tie(held, other_q, other_u, other_d)
        held = send(held, SHIFT[1])
        ring.append(held)
    ring_q = jnp.stack(ring)
    far_q = spread_half(ring_q, half)
    first_u = lax.dynamic_slice(up_weight, (0, (2 * x + y) * (ff // 4)), (piece, ff // 4))
    first_u = tie(first_u, held)
    ring_u = [send(first_u, SHIFT[k]) for k in range(1, 4)]
    rest_q = swap(tie((ring_q,) + far_q, ring_u))
    swapped_q = rest_q[0]
    parts_q = (own_q, ring_q) + far_q + (other_q,) + rest_q
    (wqkv,) = assemble(
        functools.partial(assemble_half_kernel, [qkv_weight.shape[0]]), at, parts_q, [(width, 3 * width)]
    )
    blocks = lambda own, ring: jnp.concatenate([own[None, piece : piece + 1, :2048].reshape(1, 16, 128), ring[:, piece : piece + 2, :1024].reshape(3, 16, 128)])
    vecs, bu = whole_vectors(jnp.stack([blocks(own_q, ring_q), blocks(other_q, swapped_q)]), z, c, piece)

    aq, ak = masks(segment_ids, valid)
    ring_u = jnp.stack(tie(ring_u, far_q))
    first_d = tie(halves(own_d, x, y), ring_u)
    ring_d = [send(first_d, SHIFT[k]) for k in range(1, 4)]
    a, b = ring_u[:, :half], ring_u[:, half:]
    a2, b2 = send(a, ACROSS), send(b, ALONG)
    saved = [attend(0, tie(tokens, a, b, first_d), wqkv, vecs, aq, ak, length)]
    a2, b2 = tie((a2, b2), saved[0][3])
    a3, b3 = jnp.stack([a, a2]), jnp.stack([b, b2])
    a4, b4 = send(a3, ALONG), send(b3, ACROSS)
    saved.append(attend(1, tie(tokens, a3, b3), wqkv, vecs, aq, ak, length))
    a4, b4, ring_d = tie((a4, b4, ring_d), saved[1][3])
    ring_d = jnp.stack(ring_d)
    ab4 = jnp.stack([a4, b4])
    far_d = spread_half(ring_d, dr + half)
    rest_u = swap((a3, b3, ab4))
    saved.append(attend(2, tie(tokens, ring_d, ab4), wqkv, vecs, aq, ak, length))
    far_d, rest_u = tie((far_d, rest_u), saved[2][3])
    rest_d = swap(tie((ring_d,) + far_d, rest_u))
    (wu,) = assemble(assemble_quarter_kernel, at, tie((up_weight, a3, b3, ab4, other_u) + rest_u, far_d), [(width, ff)])
    wd, wo = assemble(
        functools.partial(assemble_half_kernel, [2 * dr, piece]),
        at,
        (own_d, ring_d) + far_d + (other_d,) + tie(rest_d, wu),
        [(ff, width), (width, width)],
    )

    ctx = [f[3] for f in saved]
    result, low, hid, gd, gu, gb, gc, vec, bup = middle(tokens, ctx, cotangent, wo, vecs, wu, bu, wd)

    down, up, qkv = Sum(), Sum(), Sum()
    own, other = grad_down(at, ctx, gb, hid, gd)
    down.add(own, other)
    own, other = grad_up(at, *tie((low, gu), other))
    up.add(own, other)
    down.after(other)
    down.halve()
    own, other, dx, db0 = attend_back("first", 0, at, saved[0], tie(gc, down.sent, other), aq, ak, tokens, wqkv, gb, length)
    down.after(dx)
    up.after(dx)
    down.along_z()
    up.halve()
    dx = tie(dx, down.sent, up.sent)
    own, other, dx, db1 = attend_back("second", 1, at, saved[1], gc, aq, ak, tokens, wqkv, dx, length, (own, other))
    qkv.add(own, other)
    up.after(dx)
    wide = bup[0].reshape(8, 4, piece).transpose(1, 0, 2).reshape(4, width)
    table = jnp.concatenate([vec[:6], wide, jnp.zeros((4, width), f32)], axis=0)
    own, other, dx, _ = attend_back(
        "third", 2, at, saved[2], gc, aq, ak, tokens, wqkv, tie(dx, up.far), length, (db0, db1, table)
    )
    down.after(dx)
    qkv.after(dx)
    qkv.add(own, other)
    up.after(down.parts)
    up.along_z()
    qkv.halve()
    up.after(qkv.far)
    qkv.after(up.parts)
    qkv.along_z()
    down.across(up)
    down.share()
    dwd, dwo, dwu = finish(at, "ffn", down.out, [down_weight.shape, out_weight.shape, up_weight.shape])
    qkv.after(dwd, dwo, dwu)
    qkv.across()
    qkv.share()
    dwq, small = finish(at, "qkv", qkv.out, [qkv_weight.shape, (16, 128)])
    one = lambda i: small[i, :piece]
    return (
        result,
        dx,
        dwq,
        small[:2, :piece],
        dwo,
        one(2),
        one(3),
        one(4),
        dwu,
        small[8:12, :piece].reshape(-1),
        dwd,
        one(5),
        one(6),
        one(7),
    )


def spread(args):
    flat = [a.reshape(-1) for a in args]
    packed = jnp.concatenate(flat)
    every = lax.all_gather(packed, "shard", axis=0)
    out, at = [], 0
    for a in args:
        part = every[:, at : at + a.size].reshape((-1,) + a.shape)
        at += a.size
        out.append(jnp.moveaxis(part, 0, -2).reshape(a.shape[:-1] + (-1,)))
    return out


def shards(
    tokens,
    cotangent,
    qkv_weight,
    query_value_bias,
    out_weight,
    out_bias,
    norm_one_gain,
    norm_one_shift,
    up_weight,
    up_bias,
    down_weight,
    down_bias,
    norm_two_gain,
    norm_two_shift,
    segment_ids,
    valid,
):
    length = segment_ids.shape[1]
    width = tokens.shape[1]
    groups = width // GW
    gather = lambda a: lax.all_gather(a, "shard", axis=0, tiled=True)
    *rest, bu = spread(
        (query_value_bias, out_bias, norm_one_gain, norm_one_shift, down_bias, norm_two_gain, norm_two_shift, up_bias)
    )
    vecs = jnp.concatenate([v.reshape(-1, width) for v in rest] + [jnp.zeros((8, width), bf16)], axis=0)
    wqkv, wd, wo, wu = gather(qkv_weight), gather(down_weight), gather(out_weight), gather(up_weight)
    at = jnp.zeros((4,), jnp.int32)
    aq, ak = masks(segment_ids, valid)
    saved = [attend(g, tokens, wqkv, vecs, aq, ak, length) for g in range(groups)]
    ctx = [f[3] for f in saved]
    result, low, hid, gd, gu, gb, gc, vec, bup = middle(tokens, ctx, cotangent, wo, vecs, wu, bu[None], wd)
    dwd = tn(hid, gd).astype(bf16)
    dwu = tn(low, gu).astype(bf16)
    dwo = tn(jnp.concatenate(ctx, axis=1), gb).astype(bf16)
    dx, dws, dbs = gb, [], []
    for g in range(groups):
        dw, dx, db = attend_back("plain", g, at, saved[g], gc, aq, ak, tokens, wqkv, dx, length)
        dws.append(dw)
        dbs.append(db)
    dwq = jnp.concatenate([dw[i] for i in range(3) for dw in dws], axis=1)
    db = jnp.stack(dbs).reshape(groups, 3, GW).transpose(1, 0, 2).reshape(3, width)
    small = jnp.concatenate([db[0], db[2], vec[:6].reshape(-1), bup[0]])
    small = lax.psum(small.reshape(-1, 128), ("rep", "shard")).reshape(-1)

    def owned(a):
        part = lax.psum_scatter(a, "shard", scatter_dimension=0, tiled=True)
        return lax.psum(part, "rep").astype(f32)

    rank = lax.axis_index("shard")
    own = lambda at, size: lax.dynamic_slice(small, (at + rank * size,), (size,))
    piece = out_bias.shape[0]
    vs = [own(width * i, piece) for i in range(8)]
    dbu = own(8 * width, up_bias.shape[0])
    gd_w, gu_w, go_w, gq_w = owned(dwd), owned(dwu), owned(dwo), owned(dwq)
    return result, dx, gq_w, jnp.stack(vs[:2]), go_w, vs[2], vs[3], vs[4], gu_w, dbu, gd_w, vs[5], vs[6], vs[7]


def solution(mesh):
    rows, one = P(("rep", "shard"), None), P("shard")
    mat, two = P("shard", None), P(None, "shard")
    near = mesh.shape["rep"] == 4 and mesh.shape["shard"] == 8
    return jax.shard_map(
        shards_near if near else shards,
        mesh=mesh,
        in_specs=(rows, rows, mat, two, mat, one, one, one, mat, one, mat, one, one, one, rows, rows),
        out_specs=(rows, rows, mat, two, mat, one, one, one, mat, one, mat, one, one, one),
        check_vma=False,
    )
```

```python
import functools

import jax
import jax.numpy as jnp
from jax import lax
from jax.experimental import pallas as pl
from jax.experimental.pallas import tpu as pltpu
from jax.sharding import PartitionSpec as P

HD = 64
GW = 256
SCALE = 0.125 * 1.4426950408889634
BIG = 1e30
VMEM_LIMIT = 60 * 1024 * 1024
bf16 = jnp.bfloat16
f32 = jnp.float32
SMEM = pl.BlockSpec(memory_space=pltpu.SMEM)
VMEM = pl.BlockSpec(memory_space=pltpu.VMEM)


def nn(a, b):
    return lax.dot_general(a, b, (((1,), (0,)), ((), ())), preferred_element_type=f32)


def nt(a, b):
    return lax.dot_general(a, b, (((1,), (1,)), ((), ())), preferred_element_type=f32)


def tn(a, b):
    return lax.dot_general(a, b, (((0,), (0,)), ((), ())), preferred_element_type=f32)


def params(**more):
    return pltpu.CompilerParams(vmem_limit_bytes=VMEM_LIMIT, **more)


def cost(flops, moved):
    return pl.CostEstimate(flops=flops, bytes_accessed=moved, transcendentals=0)


def attend_kernel(tok, wq, wk, wv, vecs, aq, ak, q_o, k_o, v_o, ctx_o, lse_o):
    x = tok[...]
    q = (nn(x, wq[...]) + vecs[0:1, :].astype(f32)).astype(bf16)
    k = nn(x, wk[...]).astype(bf16)
    v = (nn(x, wv[...]) + vecs[1:2, :].astype(f32)).astype(bf16)
    q_o[...] = q
    k_o[...] = k
    v_o[...] = v
    length, width = q.shape
    lane = lax.broadcasted_iota(jnp.int32, (length, width), 1) // HD
    slot = lax.broadcasted_iota(jnp.int32, (length, 128), 1)
    acc = None
    scale = jnp.zeros((length, width), f32)
    stat = jnp.zeros((length, 128), f32)
    for h in range(width // HD):
        mine = lane == h
        qa = jnp.where(mine, q, aq[...])
        ka = jnp.where(mine, k, ak[...])
        va = jnp.where(mine, v, jnp.zeros_like(v))
        t = nt(qa, ka) * SCALE
        m = jnp.max(t, axis=1, keepdims=True)
        p = jnp.exp2(t - m)
        total = jnp.sum(p, axis=1, keepdims=True)
        part = nn(p.astype(bf16), va)
        acc = part if acc is None else acc + part
        scale = jnp.where(mine, 1.0 / total, scale)
        stat = jnp.where(slot == h, m + jnp.log2(total), stat)
    ctx_o[...] = (acc * scale).astype(bf16)
    lse_o[0] = stat.T[:8]


def attend(g, tokens, w, vecs, aq, ak, length):
    rows, width = tokens.shape
    groups = width // GW
    seqs = rows // length
    col = lambda o: pl.BlockSpec((width, GW), lambda b: (0, o * groups + g))
    seq = pl.BlockSpec((length, width), lambda b: (b, 0))
    blk = pl.BlockSpec((length, GW), lambda b: (b, 0))
    act = jax.ShapeDtypeStruct((rows, GW), bf16)
    return pl.pallas_call(
        attend_kernel,
        grid=(seqs,),
        in_specs=[seq, col(0), col(1), col(2), pl.BlockSpec((16, GW), lambda b: (0, g)), blk, blk],
        out_specs=[blk, blk, blk, blk, pl.BlockSpec((1, 8, length), lambda b: (b, 0, 0))],
        out_shape=[act, act, act, act, jax.ShapeDtypeStruct((seqs, 8, length), f32)],
        compiler_params=params(),
        cost_estimate=cost(4_000_000_000, 5_000_000),
        name="attend",
    )(tokens, w, w, w, vecs, aq, ak)


def owner_of(s, at_r):
    return lax.rem(s // 2 - at_r[2] + 4, 4), at_r[3] != s % 2


def select_lanes(s, piece, width):
    i = lax.broadcasted_iota(jnp.int32, (128, width), 0)
    j = lax.broadcasted_iota(jnp.int32, (128, width), 1)
    return ((j == s * piece + i) & (i < piece)).astype(f32).astype(bf16)


def attend_back_kernel(mode, at_r, q_r, k_r, v_r, do_r, ctx_r, lse_r, aq, ak, tok, wq, wk, wv, dx_i, *rest):
    b = pl.program_id(0)
    last = b == pl.num_programs(0) - 1
    if mode == "plain":
        dw_o, dx_o, db_o, dw_s = rest
    elif mode == "first":
        own_o, other_o, dx_o, db_o, dw_s = rest
    elif mode == "second":
        _, _, own_o, other_o, dx_o, db_o, dw_s = rest
    else:
        db0, db1, tbl, own_o, other_o, dx_o, db_o, dw_s = rest
    q, k, v, do = q_r[...], k_r[...], v_r[...], do_r[...]
    length, width = q.shape
    lane = lax.broadcasted_iota(jnp.int32, (length, width), 1) // HD
    sel = lax.broadcasted_iota(jnp.int32, (8, width), 1) // HD == lax.broadcasted_iota(jnp.int32, (8, width), 0)
    sel = sel.astype(f32).astype(bf16)
    prod = do.astype(f32) * ctx_r[...].astype(f32)
    hi = prod.astype(bf16)
    lo = (prod - hi.astype(f32)).astype(bf16)
    delta = nt(sel, hi) + nt(sel, lo)
    dq = dk = dv = None
    zero = jnp.zeros_like(q)
    for h in range(width // HD):
        mine = lane == h
        qa = jnp.where(mine, q, aq[...])
        ka = jnp.where(mine, k, ak[...])
        va = jnp.where(mine, v, zero)
        p = jnp.exp2(nt(ka, qa) * SCALE - lse_r[0, h : h + 1, :])
        dp = nt(va, do)
        ds = (p * (dp - delta[h : h + 1, :])).astype(bf16)
        dv_h = nn(p.astype(bf16), jnp.where(mine, do, zero))
        dk_h = nn(ds, jnp.where(mine, q, zero))
        dq_h = tn(ds, jnp.where(mine, k, zero))
        dv = dv_h if dv is None else dv + dv_h
        dk = dk_h if dk is None else dk + dk_h
        dq = dq_h if dq is None else dq + dq_h
    dq = (dq * 0.125).astype(bf16)
    dk = (dk * 0.125).astype(bf16)
    dv = dv.astype(bf16)
    back = jnp.concatenate([dq, dk, dv], axis=1)
    dw = tn(tok[...], back)
    dx = nt(dq, wq[...]) + nt(dk, wk[...]) + nt(dv, wv[...])
    dx_o[...] = (dx_i[...].astype(f32) + dx).astype(dx_o.dtype)
    sums = jnp.sum(back.astype(f32), axis=0, keepdims=True)

    @pl.when(b == 0)
    def _():
        dw_s[...] = dw
        db_o[...] = sums

    @pl.when(b > 0)
    def _():
        dw_s[...] += dw
        db_o[...] += sums

    @pl.when(last)
    def _():
        if mode == "plain":
            for i in range(3):
                dw_o[i] = dw_s[:, i * width : (i + 1) * width].astype(bf16)
            return
        res = dw_s[...].astype(bf16)
        piece = res.shape[0] // 8
        half, wide = piece // 2, res.shape[1] // 2
        for s in range(8):
            kk, far = owner_of(s, at_r)
            for ab, turn in ((0, at_r[1]), (1, at_r[0])):
                for h in range(2):
                    val = res[s * piece + ab * half : s * piece + (ab + 1) * half, h * wide : (h + 1) * wide]
                    rel = lax.rem(h + turn, 2)
                    for ref, cond in ((other_o, far), (own_o, ~far)):

                        @pl.when(cond)
                        def _(val=val, rel=rel, kk=kk, ab=ab, ref=ref):
                            ref[ab, rel, kk, 0:half] = val

        if mode == "third":
            sums = [r[...] for r in (db0, db1, db_o)]
            dbq = jnp.concatenate([r[:, :width] for r in sums], axis=1)
            dbv = jnp.concatenate([r[:, 2 * width :] for r in sums], axis=1)
            table = jnp.concatenate([dbq, dbv, tbl[...]], axis=0).astype(bf16)
            extra = jnp.zeros((4, 16, wide), bf16)
            for ab in range(2):
                for h in range(2):
                    own_o[ab, h, :, half : half + 16, :] = extra
                    other_o[ab, h, :, half : half + 16, :] = extra
            for s in range(8):
                blk = nt(table, select_lanes(s, piece, table.shape[1])).astype(bf16)
                kk, far = owner_of(s, at_r)
                for ref, cond in ((other_o, far), (own_o, ~far)):

                    @pl.when(cond)
                    def _(blk=blk, kk=kk, ref=ref):
                        ref[0, at_r[1], kk, half : half + 16, 0:128] = blk


def attend_back(mode, g, at, saved, gc, aq, ak, tokens, w, dx, length, extra=()):
    rows, width = tokens.shape
    groups = width // GW
    seqs = rows // length
    half = width // 16
    col = lambda o: pl.BlockSpec((width, GW), lambda b: (0, o * groups + g))
    seq = pl.BlockSpec((length, width), lambda b: (b, 0))
    blk = pl.BlockSpec((length, GW), lambda b: (b, 0))
    whole = lambda s: pl.BlockSpec(s, lambda b: (0,) * len(s))
    S = jax.ShapeDtypeStruct
    tall = {"first": 2 * half, "second": 2 * half, "third": half + 16, "plain": 0}[mode]
    at_row = 1 if mode == "second" else 0
    block = half + 16 if mode == "third" else half
    part = pl.BlockSpec((2, 2, 4, block, 3 * GW // 2), lambda b: (0, 0, 0, at_row, 0))
    if mode == "plain":
        out_specs, out_shape = [whole((3, width, GW))], [S((3, width, GW), bf16)]
    else:
        out_specs, out_shape = [part, part], [S((2, 2, 4, tall, 3 * GW // 2), bf16)] * 2
    out_specs += [seq, whole((1, 3 * GW))]
    out_shape += [S((rows, width), bf16 if mode == "third" or g == groups - 1 else f32), S((1, 3 * GW), f32)]
    in_specs = [SMEM, blk, blk, blk, pl.BlockSpec((length, GW), lambda b: (b, g)), blk]
    in_specs += [pl.BlockSpec((1, 8, length), lambda b: (b, 0, 0)), blk, blk, seq, col(0), col(1), col(2), seq]
    aliases = {}
    if mode == "second":
        in_specs += [pl.BlockSpec(memory_space=pl.ANY)] * 2
        aliases = {len(in_specs) - 2: 0, len(in_specs) - 1: 1}
    elif mode == "third":
        in_specs += [whole(e.shape) for e in extra]
    q, k, v, ctx, lse = saved
    return pl.pallas_call(
        functools.partial(attend_back_kernel, mode),
        grid=(seqs,),
        in_specs=in_specs,
        out_specs=out_specs,
        out_shape=out_shape,
        scratch_shapes=[pltpu.VMEM((width, 3 * GW), f32)],
        input_output_aliases=aliases,
        compiler_params=params(),
        cost_estimate=cost(8_000_000_000, 8_000_000),
        name="attend_back",
    )(at, q, k, v, gc, ctx, lse, aq, ak, tokens, w, w, w, dx, *extra)


def masks(segment_ids, valid):
    code = (segment_ids + 8 * valid).reshape(-1, 1)
    lane = lax.broadcasted_iota(jnp.int32, (1, GW), 1) % HD
    same = code == lane
    aq = same.astype(bf16)
    ak = jnp.where((lane < 16) & ~same, -BIG, 0.0).astype(bf16)
    return aq, ak


def phi(x):
    return 0.5 * (1.0 + lax.erf(x * 0.7071067811865476)), jnp.exp(-0.5 * x * x) * 0.3989422804014327


def middle_kernel(groups, tok, *refs):
    ctx_r = refs[:groups]
    cot, wo, vecs, wu, bu, wd, out_o, low_o, hid_o, gd_o, gu_o, gb_o, gc_o, vec_o, bup_o, slope = refs[groups:]
    i = pl.program_id(0)
    width = tok.shape[1]
    ff = wd.shape[0]
    step = width
    chunks = ff // step
    bo, g1, s1, bd, g2, s2 = (vecs[j : j + 1, :].astype(f32) for j in range(2, 8))
    ctx = jnp.concatenate([r[...] for r in ctx_r], axis=1)
    pre = tok[...].astype(f32) + nn(ctx, wo[...]) + bo
    mean = lambda v: jnp.mean(v, axis=1, keepdims=True)
    centre = pre - mean(pre)
    r1 = lax.rsqrt(mean(centre * centre) + 1e-05)
    n1 = centre * r1
    normed = n1 * g1 + s1
    low = normed.astype(bf16)
    low_o[...] = low
    acc = normed + bd
    for c in range(chunks):
        cols = slice(c * step, (c + 1) * step)
        hp = nn(low, wu[:, cols]) + bu[:, cols].astype(f32)
        cdf, pdf = phi(hp)
        slope[:, cols] = cdf + hp * pdf
        hid = (hp * cdf).astype(bf16)
        hid_o[:, cols] = hid
        acc = acc + nn(hid, wd[cols, :])
    centre = acc - mean(acc)
    r2 = lax.rsqrt(mean(centre * centre) + 1e-05)
    n2 = centre * r2
    out_o[...] = (n2 * g2 + s2).astype(bf16)
    ct = cot[...].astype(f32)
    e = ct * g2
    gp2 = r2 * (e - mean(e) - n2 * mean(e * n2))
    gd = gp2.astype(bf16)
    gd_o[...] = gd
    acc = gp2
    total = lambda v: jnp.sum(v, axis=0, keepdims=True)

    def put(ref, at, v):
        @pl.when(i == 0)
        def _():
            ref[at] = v

        @pl.when(i > 0)
        def _():
            ref[at] += v

    for c in range(chunks):
        cols = slice(c * step, (c + 1) * step)
        gu = (nt(gd, wd[cols, :]) * slope[:, cols]).astype(bf16)
        gu_o[:, cols] = gu
        put(bup_o, (slice(0, 1), cols), total(gu.astype(f32)))
        acc = acc + nt(gu, wu[:, cols])
    e = acc * g1
    gp1 = r1 * (e - mean(e) - n1 * mean(e * n1))
    gb = gp1.astype(bf16)
    gb_o[...] = gb
    gc_o[...] = nt(gb, wo[...]).astype(bf16)
    for at, v in enumerate((gb.astype(f32), acc * n1, acc, gd.astype(f32), ct * n2, ct)):
        put(vec_o, (slice(at, at + 1), slice(None)), total(v))


def middle(tokens, ctx, cot, wo, vecs, wu, bu, wd, tile=256):
    rows, width = tokens.shape
    ff = wd.shape[0]
    act = pl.BlockSpec((tile, width), lambda i: (i, 0))
    wide = pl.BlockSpec((tile, ff), lambda i: (i, 0))
    whole = lambda a: pl.BlockSpec(a.shape, lambda i: (0, 0), pipeline_mode=pl.Buffered(1))
    S = jax.ShapeDtypeStruct
    shapes = [(rows, width), (rows, width), (rows, ff), (rows, width), (rows, ff), (rows, width), (rows, width)]
    return pl.pallas_call(
        functools.partial(middle_kernel, len(ctx)),
        grid=(rows // tile,),
        in_specs=[act] + [pl.BlockSpec((tile, GW), lambda i: (i, 0)) for _ in ctx] + [act] + [whole(a) for a in (wo, vecs, wu, bu, wd)],
        out_specs=[act, act, wide, act, wide, act, act, pl.BlockSpec((8, width), lambda i: (0, 0)), pl.BlockSpec((8, ff), lambda i: (0, 0))],
        out_shape=[S(s, bf16) for s in shapes] + [S((8, width), f32), S((8, ff), f32)],
        scratch_shapes=[pltpu.VMEM((tile, ff), f32)],
        compiler_params=params(),
        cost_estimate=cost(30_000_000_000, 40_000_000),
        name="middle",
    )(tokens, *ctx, cot, wo, vecs, wu, bu, wd)


def grad_down_kernel(groups, at_r, *refs):
    ctx = refs[:groups]
    gb, hid, gd, own_o, other_o = refs[groups:]
    p = pl.program_id(0)
    turns = ((0, at_r[1]), (1, at_r[0]))
    wide = gd.shape[1] // 2
    tall = hid.shape[1] // 2

    @pl.when(p == 0)
    def _():
        lhs = jnp.concatenate([r[...] for r in ctx], axis=1)
        res = tn(lhs, gb[...]).astype(bf16)
        piece = res.shape[0] // 8
        half = piece // 2
        for s in range(8):
            kk, far = owner_of(s, at_r)
            for ab, turn in turns:
                for h in range(2):
                    val = res[s * piece + ab * half : s * piece + (ab + 1) * half, h * wide : (h + 1) * wide]
                    rel = lax.rem(h + turn, 2)
                    for ref, cond in ((other_o, far), (own_o, ~far)):

                        @pl.when(cond)
                        def _(val=val, rel=rel, kk=kk, ab=ab, ref=ref):
                            ref[ab, rel, kk, tall : tall + half] = val

    @pl.when(p > 0)
    def _():
        res = tn(hid[...], gd[...]).astype(bf16)
        kk = lax.rem(p - 1, 4)
        for ab, turn in turns:
            for h in range(2):
                val = res[ab * tall : (ab + 1) * tall, h * wide : (h + 1) * wide]
                rel = lax.rem(h + turn, 2)
                for ref, cond in ((other_o, p < 5), (own_o, p >= 5)):

                    @pl.when(cond)
                    def _(val=val, rel=rel, ab=ab, ref=ref):
                        ref[ab, rel, kk, 0:tall] = val


def grad_down(at, ctx, gb, hid, gd):
    rows, ff = hid.shape
    width = gd.shape[1]
    piece = ff // 8
    part = (2, 2, 4, (piece + width // 8) // 2, width // 2)

    def owner(p, at_r):
        j = jnp.maximum(p - 1, 0)
        z = lax.rem(at_r[2] + lax.rem(j, 4), 4)
        return 0, 2 * z + jnp.where(j < 4, 1 - at_r[3], at_r[3])

    whole = lambda s: pl.BlockSpec(s, lambda p, at_r: (0,) * len(s))
    return pl.pallas_call(
        functools.partial(grad_down_kernel, len(ctx)),
        grid_spec=pltpu.PrefetchScalarGridSpec(
            num_scalar_prefetch=1,
            grid=(9,),
            in_specs=[whole(c.shape) for c in ctx] + [whole(gb.shape), pl.BlockSpec((rows, piece), owner), whole(gd.shape)],
            out_specs=[whole(part), whole(part)],
        ),
        out_shape=[jax.ShapeDtypeStruct(part, bf16)] * 2,
        compiler_params=params(),
        cost_estimate=cost(9_000_000_000, 14_000_000),
        name="grad_down",
    )(at, *ctx, gb, hid, gd)


def grad_up_kernel(at_r, low, gu, own_o, other_o, turned):
    j = pl.program_id(0)
    y, x = at_r[0], at_r[1]

    @pl.when(j == 0)
    def _():
        turned[...] = low[...].T

    res = nn(turned[...], gu[...]).astype(bf16)
    piece = res.shape[0] // 8
    half = piece // 2
    h, l = j // 4, lax.rem(j // 2, 2)
    row = pl.multiple_of(lax.rem(j, 2) * half, 16)
    for s in range(8):
        kk, far = owner_of(s, at_r)
        for ab, turn, other_turn in ((0, x, y), (1, y, x)):
            val = res[s * piece + ab * half : s * piece + (ab + 1) * half]
            one, two = lax.rem(h + turn, 2), lax.rem(l + other_turn, 2)
            for ref, cond in ((other_o, far), (own_o, ~far)):

                @pl.when(cond)
                def _(val=val, kk=kk, ab=ab, one=one, two=two, ref=ref):
                    ref[ab, one, two, kk, pl.ds(row, half), :] = val


def grad_up(at, low, gu):
    rows, width = low.shape
    ff = gu.shape[1]
    step = ff // 8
    part = (2, 2, 2, 4, width // 8, ff // 8)
    whole = pl.BlockSpec(part, lambda j: (0, 0, 0, 0, 0, 0))
    return pl.pallas_call(
        grad_up_kernel,
        grid=(8,),
        in_specs=[SMEM, pl.BlockSpec((rows, width), lambda j: (0, 0)), pl.BlockSpec((rows, step), lambda j: (0, j))],
        out_specs=[whole, whole],
        out_shape=[jax.ShapeDtypeStruct(part, bf16)] * 2,
        scratch_shapes=[pltpu.VMEM((width, rows), bf16)],
        compiler_params=params(),
        cost_estimate=cost(9_000_000_000, 14_000_000),
        name="grad_up",
    )(at, low, gu)


AXES = ("rep", "shard")


def pairs(move):
    found = []
    for y in range(2):
        for x in range(2):
            for z in range(4):
                for c in range(2):
                    j, i, k, d = move(y, x, z, c)
                    found.append(((y * 2 + x) * 8 + z * 2 + c, (j * 2 + i) * 8 + k * 2 + d))
    return found


CORE = pairs(lambda y, x, z, c: (y, x, z, 1 - c))
ACROSS = pairs(lambda y, x, z, c: (y, 1 - x, z, c))
ALONG = pairs(lambda y, x, z, c: (1 - y, x, z, c))
SHIFT = [None] + [pairs(lambda y, x, z, c, n=n: (y, x, (z + n) % 4, c)) for n in (1, 2, 3)]


def send(a, where):
    return lax.ppermute(a, AXES, where)


def tie(values, *after):
    flat, tree = jax.tree.flatten(values)
    return jax.tree.unflatten(tree, lax.optimization_barrier(tuple(flat) + tuple(jax.tree.leaves(after)))[: len(flat)])


def place(own, received, at_r, rows, out, base, quarter):
    y, x, z = at_r[0], at_r[1], at_r[2]
    cols = out.shape[1]
    half = rows // 2
    out[pl.ds(pl.multiple_of(base(z), 16), rows), :] = own
    for k in range(1, 4):
        start = base(lax.rem(z - k + 4, 4))
        for ab in range(2):
            at = pl.ds(pl.multiple_of(start + ab * half, 16), half)
            if quarter:
                wide = cols // 4
                for i in range(2):
                    for l in range(2):
                        one, two = (i, l) if ab == 0 else (l, i)
                        col = (lax.rem(x + i, 2) * 2 + lax.rem(y + l, 2)) * wide
                        out[at, pl.ds(pl.multiple_of(col, 128), wide)] = received(ab, one, two, k)
            else:
                wide = cols // 2
                for one in range(2):
                    col = lax.rem((x, y)[ab] + one, 2) * wide
                    out[at, pl.ds(pl.multiple_of(col, 128), wide)] = received(ab, one, 0, k)


def assemble_half_kernel(out_rows, at_r, *refs):
    n = len(out_rows)
    outs = refs[-n:]
    c = at_r[3]
    for turn, (own, ring, far_x, far_y) in ((c, refs[:4]), (1 - c, refs[4:8])):
        off = 0
        total_half = sum(out_rows) // 2
        for out, rows in zip(outs, out_rows):
            half = rows // 2

            def received(ab, one, two, k):
                if one == 0:
                    return ring[k - 1, ab * total_half + off : ab * total_half + off + half, :]
                return (far_x, far_y)[ab][k - 1, off : off + half, :]

            whole = jnp.concatenate([own[off : off + half], own[total_half + off : total_half + off + half]], axis=0)
            place(whole, received, at_r, rows, out, lambda z: (2 * z + turn) * rows, False)
            off += half


def assemble_quarter_kernel(at_r, *refs):
    out = refs[-1]
    c = at_r[3]
    for turn, (own, near_a, near_b, far) in ((c, refs[:4]), (1 - c, refs[4:8])):
        rows = own.shape[0]

        def received(ab, one, two, k):
            if two == 1:
                return far[ab, one, k - 1]
            return (near_a, near_b)[ab][one, k - 1]

        place(own[...], received, at_r, rows, out, lambda z: (2 * z + turn) * rows, True)


def assemble(kernel, at, parts, shapes):
    return pl.pallas_call(
        kernel,
        in_specs=[SMEM] + [VMEM] * len(parts),
        out_specs=[VMEM] * len(shapes),
        out_shape=[jax.ShapeDtypeStruct(s, bf16) for s in shapes],
        compiler_params=params(),
        cost_estimate=cost(0, sum(4 * s[0] * s[1] for s in shapes)),
        name="assemble",
    )(at, *parts)


def halves(w, x, y):
    half, wide = w.shape[0] // 2, w.shape[1] // 2
    a = lax.dynamic_slice(w, (0, x * wide), (half, wide))
    b = lax.dynamic_slice(w, (half, y * wide), (half, wide))
    return jnp.concatenate([a, b], axis=0)


def spread_half(ring, half):
    return send(ring[:, :half], ACROSS), send(ring[:, half : 2 * half], ALONG)


def swap(parts):
    return tuple(send(p, CORE) for p in parts)


def total(*terms):
    out = terms[0].astype(f32)
    for t in terms[1:]:
        out = out + t.astype(f32)
    return out.astype(bf16)


def finish_kernel(kind, at_r, *refs):
    y, x = at_r[0], at_r[1]
    blocks, outs = refs[:4], refs[4:]
    for ab, turn, other_turn in ((0, x, y), (1, y, x)):
        one, two = (blocks[2 * ab + i][...].astype(f32) for i in range(2))
        left = jnp.where(turn == 0, one, two)
        right = jnp.where(turn == 0, two, one)
        both = jnp.concatenate([left, right], axis=1)
        if kind == "ffn":
            off = 0
            for out in outs[:2]:
                half = out.shape[0] // 2
                out[ab * half : (ab + 1) * half, :] = both[off : off + half]
                off += half
            half = outs[2].shape[0] // 2
            eighth = left.shape[1]
            for h, val in ((0, left), (1, right)):
                near, far = val[off : off + 2 * half], val[off + 2 * half : off + 4 * half]
                quarters = jnp.where(other_turn == 0, near, far), jnp.where(other_turn == 0, far, near)
                for i in range(4):
                    row, col = i % 2 * half, (4 * h + i) * eighth
                    outs[2][ab * half : (ab + 1) * half, col : col + eighth] = quarters[i // 2][row : row + half]
        else:
            half = outs[0].shape[0] // 2
            groups = outs[0].shape[1] // (3 * GW)
            for g in range(groups):
                for i in range(3):
                    col = (i * groups + g) * GW
                    outs[0][ab * half : (ab + 1) * half, col : col + GW] = both[g * half : (g + 1) * half, i * GW : (i + 1) * GW]
            if ab == 0:
                rows = groups * half
                outs[1][...] = left[rows : rows + 16, :128]


def finish(at, kind, blocks, shapes):
    return pl.pallas_call(
        functools.partial(finish_kernel, kind),
        in_specs=[SMEM] + [VMEM] * len(blocks),
        out_specs=[VMEM] * len(shapes),
        out_shape=[jax.ShapeDtypeStruct(s, f32) for s in shapes],
        compiler_params=params(),
        cost_estimate=cost(0, 4_000_000),
        name="finish_" + kind,
    )(at, *blocks)


def pack(vectors, wide):
    block = jnp.concatenate([v.reshape(-1, vectors[1].shape[0]) for v in vectors] + [wide.reshape(4, -1)], axis=0)
    return jnp.pad(block, ((0, 16 - block.shape[0]), (0, 128 - block.shape[1])))


def whole_vectors(every, z, c, piece):
    k = lax.broadcasted_iota(jnp.int32, (2, 4, 8), 1)
    d = lax.broadcasted_iota(jnp.int32, (2, 4, 8), 0)
    s = lax.broadcasted_iota(jnp.int32, (2, 4, 8), 2)
    pick = (s == 2 * ((z - k) % 4) + (c + d) % 2).astype(bf16)
    table = jnp.einsum("dks,dkrl->srl", pick, every, preferred_element_type=f32).astype(bf16)
    table = table[:, :, :piece]
    wide = table[:, 8:12].reshape(1, -1)
    return table.transpose(1, 0, 2).reshape(16, -1), wide


class Sum:
    def __init__(self):
        self.own, self.got = [], []

    def add(self, own, other):
        self.own.append(own)
        self.got.append(send(other, CORE))

    def after(self, *values):
        self.got, self.far, self.parts, self.rest = tie((self.got, self.far, self.parts, self.rest), *values)

    far = parts = ()

    def pair(self, pick, *more):
        found = [total(pick(o), pick(g)) for o, g in zip(self.own, self.got)]
        found = found[0] if len(found) == 1 else jnp.concatenate(found, axis=-2)
        return total(found, *more) if more else found

    def halve(self):
        self.sent = self.pair(lambda a: a[0, 1]), self.pair(lambda a: a[1, 1])
        self.far = send(self.sent[0], ACROSS), send(self.sent[1], ALONG)

    def along_z(self):
        far = self.far
        self.mine = [jnp.stack([self.near(i, k) for i in range(2)]) for k in range(4)]
        self.sent = self.mine[1:]
        self.far = ()
        self.parts = [send(self.mine[k], SHIFT[k]) for k in range(1, 4)]

    def joined(self, i):
        one, two, rows = self.sent[i], self.far[i], self.rows
        summed = total(one[:rows], two[:rows])
        return jnp.concatenate([summed, one[rows:], two[rows:]], axis=0)

    rest = ()

    def near(self, i, k):
        if self.rest:
            return total(self.rest[i][k], self.far[i][k])
        terms = []
        at = 0
        for o, g in zip(self.own, self.got):
            rows = o.shape[3]
            terms.append(total(o[i, 0, k], g[i, 0, k], self.far[i][k, at : at + rows]))
            at += rows
        return terms[0] if len(terms) == 1 else jnp.concatenate(terms, axis=0)

    def quarter(self):
        own, got, far = self.own[0], self.got[0], self.far
        part = lambda i, j: total(own[i, 0, j], got[i, 0, j], far[i][j])
        self.sent = part(0, 1), part(1, 1)
        self.rest = part(0, 0), part(1, 0)
        self.far = send(self.sent[0], ALONG), send(self.sent[1], ACROSS)

    def across(self, more=None):
        both = total(self.mine[0], *self.parts)
        rows = both.shape[1]
        if more is not None:
            extra = total(more.mine[0], *more.parts)
            both = jnp.concatenate([both, extra], axis=1)
        self.got = self.parts = ()
        self.sent = both[0], both[1]
        self.far = send(both[0], ALONG), send(both[1], ACROSS)
        self.rows = rows

    def share(self):
        a, b = (self.joined(i) for i in range(2))
        self.sent = a, b
        self.out = a, send(a, ACROSS), b, send(b, ALONG)


def shards_near(
    tokens,
    cotangent,
    qkv_weight,
    query_value_bias,
    out_weight,
    out_bias,
    norm_one_gain,
    norm_one_shift,
    up_weight,
    up_bias,
    down_weight,
    down_bias,
    norm_two_gain,
    norm_two_shift,
    segment_ids,
    valid,
):
    length = segment_ids.shape[1]
    width = tokens.shape[1]
    groups = width // GW
    ff = up_bias.shape[0] * 8
    piece = out_bias.shape[0]
    r, s = lax.axis_index("rep"), lax.axis_index("shard")
    y, x, z, c = r // 2, r % 2, s // 2, s % 2
    at = jnp.stack([y, x, z, c]).astype(jnp.int32)

    half = piece // 2
    block = pack(
        (query_value_bias, out_bias, norm_one_gain, norm_one_shift, down_bias, norm_two_gain, norm_two_shift), up_bias
    )
    lines = lambda n, cols: jnp.pad(block.reshape(n, -1), ((0, 8 - n), (0, cols - 2048 // n)))
    dr = down_weight.shape[0] // 2
    own_q = jnp.concatenate([qkv_weight, lines(1, 3 * width)], axis=0)
    own_d = jnp.concatenate([down_weight[:dr], out_weight[:half], down_weight[dr:], out_weight[half:]], axis=0)
    other_q, other_u, other_d = swap((own_q, up_weight, own_d))
    held = jnp.concatenate([halves(qkv_weight, x, y), lines(2, 3 * width // 2)], axis=0)
    ring = []
    for step in range(3):
        if step == 2:
            held = tie(held, other_q, other_u, other_d)
        held = send(held, SHIFT[1])
        ring.append(held)
    ring_q = jnp.stack(ring)
    far_q = spread_half(ring_q, half)
    first_u = lax.dynamic_slice(up_weight, (0, (2 * x + y) * (ff // 4)), (piece, ff // 4))
    first_u = tie(first_u, held)
    ring_u = [send(first_u, SHIFT[k]) for k in range(1, 4)]
    rest_q = swap(tie((ring_q,) + far_q, ring_u))
    swapped_q = rest_q[0]
    parts_q = (own_q, ring_q) + far_q + (other_q,) + rest_q
    (wqkv,) = assemble(
        functools.partial(assemble_half_kernel, [qkv_weight.shape[0]]), at, parts_q, [(width, 3 * width)]
    )
    blocks = lambda own, ring: jnp.concatenate([own[None, piece : piece + 1, :2048].reshape(1, 16, 128), ring[:, piece : piece + 2, :1024].reshape(3, 16, 128)])
    vecs, bu = whole_vectors(jnp.stack([blocks(own_q, ring_q), blocks(other_q, swapped_q)]), z, c, piece)

    aq, ak = masks(segment_ids, valid)
    ring_u = jnp.stack(tie(ring_u, far_q))
    first_d = tie(halves(own_d, x, y), ring_u)
    d2 = send(first_d, SHIFT[2])
    a, b = ring_u[:, :half], ring_u[:, half:]
    a2, b2 = send(a, ACROSS), send(b, ALONG)
    saved = [attend(0, tie(tokens, a, b, first_d), wqkv, vecs, aq, ak, length)]
    a2, b2, d2, first_d = tie((a2, b2, d2, first_d), saved[0][3])
    a3, b3 = jnp.stack([a, a2]), jnp.stack([b, b2])
    a4, b4 = send(a3, ALONG), send(b3, ACROSS)
    d1, d3 = send(first_d, SHIFT[1]), send(first_d, SHIFT[3])
    saved.append(attend(1, tie(tokens, a3, b3, d2), wqkv, vecs, aq, ak, length))
    a4, b4, ring_d = tie((a4, b4, [d1, d2, d3]), saved[1][3])
    ring_d = jnp.stack(ring_d)
    ab4 = jnp.stack([a4, b4])
    far_d = spread_half(ring_d, dr + half)
    rest_u = swap((a3, b3, ab4))
    saved.append(attend(2, tie(tokens, ring_d, ab4), wqkv, vecs, aq, ak, length))
    far_d, rest_u = tie((far_d, rest_u), saved[2][3])
    rest_d = swap(tie((ring_d,) + far_d, rest_u))
    (wu,) = assemble(assemble_quarter_kernel, at, tie((up_weight, a3, b3, ab4, other_u) + rest_u, far_d), [(width, ff)])
    wd, wo = assemble(
        functools.partial(assemble_half_kernel, [2 * dr, piece]),
        at,
        (own_d, ring_d) + far_d + (other_d,) + tie(rest_d, wu),
        [(ff, width), (width, width)],
    )

    ctx = [f[3] for f in saved]
    result, low, hid, gd, gu, gb, gc, vec, bup = middle(tokens, ctx, cotangent, wo, vecs, wu, bu, wd)

    down, up, qkv = Sum(), Sum(), Sum()
    own, other = grad_down(at, ctx, gb, hid, gd)
    down.add(own, other)
    own, other = grad_up(at, *tie((low, gu), other))
    up.add(own, other)
    down.after(other)
    down.halve()
    own, other, dx, db0 = attend_back("first", 0, at, saved[0], tie(gc, down.sent, other), aq, ak, tokens, wqkv, gb, length)
    down.after(dx)
    up.after(dx)
    down.along_z()
    up.halve()
    dx = tie(dx, down.sent, up.sent)
    own, other, dx, db1 = attend_back("second", 1, at, saved[1], gc, aq, ak, tokens, wqkv, dx, length, (own, other))
    two = own, other
    up.after(dx)
    up.quarter()
    wide = bup[0].reshape(8, 4, piece).transpose(1, 0, 2).reshape(4, width)
    table = jnp.concatenate([vec[:6], wide, jnp.zeros((4, width), f32)], axis=0)
    own, other, dx, _ = attend_back(
        "third", 2, at, saved[2], gc, aq, ak, tokens, wqkv, tie(dx, up.sent), length, (db0, db1, table)
    )
    down.after(dx)
    qkv.add(two[0], tie(two[1], dx))
    qkv.add(own, other)
    up.after(down.parts, dx)
    up.along_z()
    qkv.halve()
    up.after(qkv.far)
    qkv.after(up.parts)
    qkv.along_z()
    down.across(up)
    down.share()
    dwd, dwo, dwu = finish(at, "ffn", down.out, [down_weight.shape, out_weight.shape, up_weight.shape])
    qkv.after(dwd, dwo, dwu)
    qkv.across()
    qkv.share()
    dwq, small = finish(at, "qkv", qkv.out, [qkv_weight.shape, (16, 128)])
    one = lambda i: small[i, :piece]
    return (
        result,
        dx,
        dwq,
        small[:2, :piece],
        dwo,
        one(2),
        one(3),
        one(4),
        dwu,
        small[8:12, :piece].reshape(-1),
        dwd,
        one(5),
        one(6),
        one(7),
    )


def spread(args):
    flat = [a.reshape(-1) for a in args]
    packed = jnp.concatenate(flat)
    every = lax.all_gather(packed, "shard", axis=0)
    out, at = [], 0
    for a in args:
        part = every[:, at : at + a.size].reshape((-1,) + a.shape)
        at += a.size
        out.append(jnp.moveaxis(part, 0, -2).reshape(a.shape[:-1] + (-1,)))
    return out


def shards(
    tokens,
    cotangent,
    qkv_weight,
    query_value_bias,
    out_weight,
    out_bias,
    norm_one_gain,
    norm_one_shift,
    up_weight,
    up_bias,
    down_weight,
    down_bias,
    norm_two_gain,
    norm_two_shift,
    segment_ids,
    valid,
):
    length = segment_ids.shape[1]
    width = tokens.shape[1]
    groups = width // GW
    gather = lambda a: lax.all_gather(a, "shard", axis=0, tiled=True)
    *rest, bu = spread(
        (query_value_bias, out_bias, norm_one_gain, norm_one_shift, down_bias, norm_two_gain, norm_two_shift, up_bias)
    )
    vecs = jnp.concatenate([v.reshape(-1, width) for v in rest] + [jnp.zeros((8, width), bf16)], axis=0)
    wqkv, wd, wo, wu = gather(qkv_weight), gather(down_weight), gather(out_weight), gather(up_weight)
    at = jnp.zeros((4,), jnp.int32)
    aq, ak = masks(segment_ids, valid)
    saved = [attend(g, tokens, wqkv, vecs, aq, ak, length) for g in range(groups)]
    ctx = [f[3] for f in saved]
    result, low, hid, gd, gu, gb, gc, vec, bup = middle(tokens, ctx, cotangent, wo, vecs, wu, bu[None], wd)
    dwd = tn(hid, gd).astype(bf16)
    dwu = tn(low, gu).astype(bf16)
    dwo = tn(jnp.concatenate(ctx, axis=1), gb).astype(bf16)
    dx, dws, dbs = gb, [], []
    for g in range(groups):
        dw, dx, db = attend_back("plain", g, at, saved[g], gc, aq, ak, tokens, wqkv, dx, length)
        dws.append(dw)
        dbs.append(db)
    dwq = jnp.concatenate([dw[i] for i in range(3) for dw in dws], axis=1)
    db = jnp.stack(dbs).reshape(groups, 3, GW).transpose(1, 0, 2).reshape(3, width)
    small = jnp.concatenate([db[0], db[2], vec[:6].reshape(-1), bup[0]])
    small = lax.psum(small.reshape(-1, 128), ("rep", "shard")).reshape(-1)

    def owned(a):
        part = lax.psum_scatter(a, "shard", scatter_dimension=0, tiled=True)
        return lax.psum(part, "rep").astype(f32)

    rank = lax.axis_index("shard")
    own = lambda at, size: lax.dynamic_slice(small, (at + rank * size,), (size,))
    piece = out_bias.shape[0]
    vs = [own(width * i, piece) for i in range(8)]
    dbu = own(8 * width, up_bias.shape[0])
    gd_w, gu_w, go_w, gq_w = owned(dwd), owned(dwu), owned(dwo), owned(dwq)
    return result, dx, gq_w, jnp.stack(vs[:2]), go_w, vs[2], vs[3], vs[4], gu_w, dbu, gd_w, vs[5], vs[6], vs[7]


def solution(mesh):
    rows, one = P(("rep", "shard"), None), P("shard")
    mat, two = P("shard", None), P(None, "shard")
    near = mesh.shape["rep"] == 4 and mesh.shape["shard"] == 8
    return jax.shard_map(
        shards_near if near else shards,
        mesh=mesh,
        in_specs=(rows, rows, mat, two, mat, one, one, one, mat, one, mat, one, one, one, rows, rows),
        out_specs=(rows, rows, mat, two, mat, one, one, one, mat, one, mat, one, one, one),
        check_vma=False,
    )
```

```python
import functools

import jax
import jax.numpy as jnp
from jax import lax
from jax.experimental import pallas as pl
from jax.experimental.pallas import tpu as pltpu
from jax.sharding import PartitionSpec as P

HD = 64
GW = 256
SCALE = 0.125 * 1.4426950408889634
BIG = 1e30
VMEM_LIMIT = 60 * 1024 * 1024
bf16 = jnp.bfloat16
f32 = jnp.float32
SMEM = pl.BlockSpec(memory_space=pltpu.SMEM)
VMEM = pl.BlockSpec(memory_space=pltpu.VMEM)


def nn(a, b):
    return lax.dot_general(a, b, (((1,), (0,)), ((), ())), preferred_element_type=f32)


def nt(a, b):
    return lax.dot_general(a, b, (((1,), (1,)), ((), ())), preferred_element_type=f32)


def tn(a, b):
    return lax.dot_general(a, b, (((0,), (0,)), ((), ())), preferred_element_type=f32)


def params(**more):
    return pltpu.CompilerParams(vmem_limit_bytes=VMEM_LIMIT, **more)


def cost(flops, moved):
    return pl.CostEstimate(flops=flops, bytes_accessed=moved, transcendentals=0)


def attend_kernel(tok, wq, wk, wv, vecs, aq, ak, q_o, k_o, v_o, ctx_o, lse_o):
    x = tok[...]
    q = (nn(x, wq[...]) + vecs[0:1, :].astype(f32)).astype(bf16)
    k = nn(x, wk[...]).astype(bf16)
    v = (nn(x, wv[...]) + vecs[1:2, :].astype(f32)).astype(bf16)
    q_o[...] = q
    k_o[...] = k
    v_o[...] = v
    length, width = q.shape
    lane = lax.broadcasted_iota(jnp.int32, (length, width), 1) // HD
    slot = lax.broadcasted_iota(jnp.int32, (length, 128), 1)
    acc = None
    scale = jnp.zeros((length, width), f32)
    stat = jnp.zeros((length, 128), f32)
    for h in range(width // HD):
        mine = lane == h
        qa = jnp.where(mine, q, aq[...])
        ka = jnp.where(mine, k, ak[...])
        va = jnp.where(mine, v, jnp.zeros_like(v))
        t = nt(qa, ka) * SCALE
        m = jnp.max(t, axis=1, keepdims=True)
        p = jnp.exp2(t - m)
        total = jnp.sum(p, axis=1, keepdims=True)
        part = nn(p.astype(bf16), va)
        acc = part if acc is None else acc + part
        scale = jnp.where(mine, 1.0 / total, scale)
        stat = jnp.where(slot == h, m + jnp.log2(total), stat)
    ctx_o[...] = (acc * scale).astype(bf16)
    lse_o[0] = stat.T[:8]


def attend(g, tokens, w, vecs, aq, ak, length):
    rows, width = tokens.shape
    groups = width // GW
    seqs = rows // length
    col = lambda o: pl.BlockSpec((width, GW), lambda b: (0, o * groups + g))
    seq = pl.BlockSpec((length, width), lambda b: (b, 0))
    blk = pl.BlockSpec((length, GW), lambda b: (b, 0))
    act = jax.ShapeDtypeStruct((rows, GW), bf16)
    return pl.pallas_call(
        attend_kernel,
        grid=(seqs,),
        in_specs=[seq, col(0), col(1), col(2), pl.BlockSpec((16, GW), lambda b: (0, g)), blk, blk],
        out_specs=[blk, blk, blk, blk, pl.BlockSpec((1, 8, length), lambda b: (b, 0, 0))],
        out_shape=[act, act, act, act, jax.ShapeDtypeStruct((seqs, 8, length), f32)],
        compiler_params=params(),
        cost_estimate=cost(4_000_000_000, 5_000_000),
        name="attend",
    )(tokens, w, w, w, vecs, aq, ak)


def owner_of(s, at_r):
    return lax.rem(s // 2 - at_r[2] + 4, 4), at_r[3] != s % 2


def select_lanes(s, piece, width):
    i = lax.broadcasted_iota(jnp.int32, (128, width), 0)
    j = lax.broadcasted_iota(jnp.int32, (128, width), 1)
    return ((j == s * piece + i) & (i < piece)).astype(f32).astype(bf16)


def attend_back_kernel(mode, at_r, q_r, k_r, v_r, do_r, ctx_r, lse_r, aq, ak, tok, wq, wk, wv, dx_i, *rest):
    b = pl.program_id(0)
    last = b == pl.num_programs(0) - 1
    if mode == "plain":
        dw_o, dx_o, db_o, dw_s = rest
    elif mode == "first":
        own_o, other_o, dx_o, db_o, dw_s = rest
    elif mode == "second":
        _, _, own_o, other_o, dx_o, db_o, dw_s = rest
    else:
        db0, db1, tbl, own_o, other_o, dx_o, db_o, dw_s = rest
    q, k, v, do = q_r[...], k_r[...], v_r[...], do_r[...]
    length, width = q.shape
    lane = lax.broadcasted_iota(jnp.int32, (length, width), 1) // HD
    sel = lax.broadcasted_iota(jnp.int32, (8, width), 1) // HD == lax.broadcasted_iota(jnp.int32, (8, width), 0)
    sel = sel.astype(f32).astype(bf16)
    prod = do.astype(f32) * ctx_r[...].astype(f32)
    hi = prod.astype(bf16)
    lo = (prod - hi.astype(f32)).astype(bf16)
    delta = nt(sel, hi) + nt(sel, lo)
    dq = dk = dv = None
    zero = jnp.zeros_like(q)
    for h in range(width // HD):
        mine = lane == h
        qa = jnp.where(mine, q, aq[...])
        ka = jnp.where(mine, k, ak[...])
        va = jnp.where(mine, v, zero)
        p = jnp.exp2(nt(ka, qa) * SCALE - lse_r[0, h : h + 1, :])
        dp = nt(va, do)
        ds = (p * (dp - delta[h : h + 1, :])).astype(bf16)
        dv_h = nn(p.astype(bf16), jnp.where(mine, do, zero))
        dk_h = nn(ds, jnp.where(mine, q, zero))
        dq_h = tn(ds, jnp.where(mine, k, zero))
        dv = dv_h if dv is None else dv + dv_h
        dk = dk_h if dk is None else dk + dk_h
        dq = dq_h if dq is None else dq + dq_h
    dq = (dq * 0.125).astype(bf16)
    dk = (dk * 0.125).astype(bf16)
    dv = dv.astype(bf16)
    back = jnp.concatenate([dq, dk, dv], axis=1)
    dw = tn(tok[...], back)
    dx = nt(dq, wq[...]) + nt(dk, wk[...]) + nt(dv, wv[...])
    dx_o[...] = (dx_i[...].astype(f32) + dx).astype(dx_o.dtype)
    sums = jnp.sum(back.astype(f32), axis=0, keepdims=True)

    @pl.when(b == 0)
    def _():
        dw_s[...] = dw
        db_o[...] = sums

    @pl.when(b > 0)
    def _():
        dw_s[...] += dw
        db_o[...] += sums

    @pl.when(last)
    def _():
        if mode == "plain":
            for i in range(3):
                dw_o[i] = dw_s[:, i * width : (i + 1) * width].astype(bf16)
            return
        res = dw_s[...].astype(bf16)
        piece = res.shape[0] // 8
        half, wide = piece // 2, res.shape[1] // 2
        for s in range(8):
            kk, far = owner_of(s, at_r)
            for ab, turn in ((0, at_r[1]), (1, at_r[0])):
                for h in range(2):
                    val = res[s * piece + ab * half : s * piece + (ab + 1) * half, h * wide : (h + 1) * wide]
                    rel = lax.rem(h + turn, 2)
                    for ref, cond in ((other_o, far), (own_o, ~far)):

                        @pl.when(cond)
                        def _(val=val, rel=rel, kk=kk, ab=ab, ref=ref):
                            ref[ab, rel, kk, 0:half] = val

        if mode == "third":
            sums = [r[...] for r in (db0, db1, db_o)]
            dbq = jnp.concatenate([r[:, :width] for r in sums], axis=1)
            dbv = jnp.concatenate([r[:, 2 * width :] for r in sums], axis=1)
            table = jnp.concatenate([dbq, dbv, tbl[...]], axis=0).astype(bf16)
            extra = jnp.zeros((4, 16, wide), bf16)
            for ab in range(2):
                for h in range(2):
                    own_o[ab, h, :, half : half + 16, :] = extra
                    other_o[ab, h, :, half : half + 16, :] = extra
            for s in range(8):
                blk = nt(table, select_lanes(s, piece, table.shape[1])).astype(bf16)
                kk, far = owner_of(s, at_r)
                for ref, cond in ((other_o, far), (own_o, ~far)):

                    @pl.when(cond)
                    def _(blk=blk, kk=kk, ref=ref):
                        ref[0, at_r[1], kk, half : half + 16, 0:128] = blk


def attend_back(mode, g, at, saved, gc, aq, ak, tokens, w, dx, length, extra=()):
    rows, width = tokens.shape
    groups = width // GW
    seqs = rows // length
    half = width // 16
    col = lambda o: pl.BlockSpec((width, GW), lambda b: (0, o * groups + g))
    seq = pl.BlockSpec((length, width), lambda b: (b, 0))
    blk = pl.BlockSpec((length, GW), lambda b: (b, 0))
    whole = lambda s: pl.BlockSpec(s, lambda b: (0,) * len(s))
    S = jax.ShapeDtypeStruct
    tall = {"first": 2 * half, "second": 2 * half, "third": half + 16, "plain": 0}[mode]
    at_row = 1 if mode == "second" else 0
    block = half + 16 if mode == "third" else half
    part = pl.BlockSpec((2, 2, 4, block, 3 * GW // 2), lambda b: (0, 0, 0, at_row, 0))
    if mode == "plain":
        out_specs, out_shape = [whole((3, width, GW))], [S((3, width, GW), bf16)]
    else:
        out_specs, out_shape = [part, part], [S((2, 2, 4, tall, 3 * GW // 2), bf16)] * 2
    out_specs += [seq, whole((1, 3 * GW))]
    out_shape += [S((rows, width), bf16 if mode == "third" or g == groups - 1 else f32), S((1, 3 * GW), f32)]
    in_specs = [SMEM, blk, blk, blk, pl.BlockSpec((length, GW), lambda b: (b, g)), blk]
    in_specs += [pl.BlockSpec((1, 8, length), lambda b: (b, 0, 0)), blk, blk, seq, col(0), col(1), col(2), seq]
    aliases = {}
    if mode == "second":
        in_specs += [pl.BlockSpec(memory_space=pl.ANY)] * 2
        aliases = {len(in_specs) - 2: 0, len(in_specs) - 1: 1}
    elif mode == "third":
        in_specs += [whole(e.shape) for e in extra]
    q, k, v, ctx, lse = saved
    return pl.pallas_call(
        functools.partial(attend_back_kernel, mode),
        grid=(seqs,),
        in_specs=in_specs,
        out_specs=out_specs,
        out_shape=out_shape,
        scratch_shapes=[pltpu.VMEM((width, 3 * GW), f32)],
        input_output_aliases=aliases,
        compiler_params=params(),
        cost_estimate=cost(8_000_000_000, 8_000_000),
        name="attend_back",
    )(at, q, k, v, gc, ctx, lse, aq, ak, tokens, w, w, w, dx, *extra)


def masks(segment_ids, valid):
    code = (segment_ids + 8 * valid).reshape(-1, 1)
    lane = lax.broadcasted_iota(jnp.int32, (1, GW), 1) % HD
    same = code == lane
    aq = same.astype(bf16)
    ak = jnp.where((lane < 16) & ~same, -BIG, 0.0).astype(bf16)
    return aq, ak


def phi(x):
    return 0.5 * (1.0 + lax.erf(x * 0.7071067811865476)), jnp.exp(-0.5 * x * x) * 0.3989422804014327


def middle_kernel(groups, split, at_r, tok, *refs):
    ctx_r = refs[:groups]
    cot, vecs, bu = refs[groups : groups + 3]
    refs = refs[groups + 3 :]
    i = pl.program_id(0)
    if split:
        up_parts, down_parts, refs = refs[:8], refs[8:16], refs[16:]
        wu, wd, wo = refs[-3:]
        refs = refs[:-3]

        @pl.when(i == 0)
        def _():
            assemble_quarter_kernel(at_r, *up_parts, wu)
            assemble_half_kernel(split, at_r, *down_parts, wd, wo)

    else:
        wu, wd, wo, refs = *refs[:3], refs[3:]
    out_o, low_o, hid_o, gd_o, gu_o, gb_o, gc_o, vec_o, bup_o, slope = refs
    width = tok.shape[1]
    ff = bu.shape[1]
    step = width
    chunks = ff // step
    bo, g1, s1, bd, g2, s2 = (vecs[j : j + 1, :].astype(f32) for j in range(2, 8))
    ctx = jnp.concatenate([r[...] for r in ctx_r], axis=1)
    pre = tok[...].astype(f32) + nn(ctx, wo[...]) + bo
    mean = lambda v: jnp.mean(v, axis=1, keepdims=True)
    centre = pre - mean(pre)
    r1 = lax.rsqrt(mean(centre * centre) + 1e-05)
    n1 = centre * r1
    normed = n1 * g1 + s1
    low = normed.astype(bf16)
    low_o[...] = low
    acc = normed + bd
    for c in range(chunks):
        cols = slice(c * step, (c + 1) * step)
        hp = nn(low, wu[:, cols]) + bu[:, cols].astype(f32)
        cdf, pdf = phi(hp)
        slope[:, cols] = cdf + hp * pdf
        hid = (hp * cdf).astype(bf16)
        hid_o[:, cols] = hid
        acc = acc + nn(hid, wd[cols, :])
    centre = acc - mean(acc)
    r2 = lax.rsqrt(mean(centre * centre) + 1e-05)
    n2 = centre * r2
    out_o[...] = (n2 * g2 + s2).astype(bf16)
    ct = cot[...].astype(f32)
    e = ct * g2
    gp2 = r2 * (e - mean(e) - n2 * mean(e * n2))
    gd = gp2.astype(bf16)
    gd_o[...] = gd
    acc = gp2
    total = lambda v: jnp.sum(v, axis=0, keepdims=True)

    def put(ref, at, v):
        @pl.when(i == 0)
        def _():
            ref[at] = v

        @pl.when(i > 0)
        def _():
            ref[at] += v

    for c in range(chunks):
        cols = slice(c * step, (c + 1) * step)
        gu = (nt(gd, wd[cols, :]) * slope[:, cols]).astype(bf16)
        gu_o[:, cols] = gu
        put(bup_o, (slice(0, 1), cols), total(gu.astype(f32)))
        acc = acc + nt(gu, wu[:, cols])
    e = acc * g1
    gp1 = r1 * (e - mean(e) - n1 * mean(e * n1))
    gb = gp1.astype(bf16)
    gb_o[...] = gb
    gc_o[...] = nt(gb, wo[...]).astype(bf16)
    for at, v in enumerate((gb.astype(f32), acc * n1, acc, gd.astype(f32), ct * n2, ct)):
        put(vec_o, (slice(at, at + 1), slice(None)), total(v))


def middle(at, tokens, ctx, cot, vecs, bu, weights, split=None, tile=256):
    rows, width = tokens.shape
    ff = bu.shape[1]
    act = pl.BlockSpec((tile, width), lambda i: (i, 0))
    wide = pl.BlockSpec((tile, ff), lambda i: (i, 0))
    whole = lambda a: pl.BlockSpec(a.shape, lambda i: (0,) * a.ndim, pipeline_mode=pl.Buffered(1))
    S = jax.ShapeDtypeStruct
    shapes = [(rows, width), (rows, width), (rows, ff), (rows, width), (rows, ff), (rows, width), (rows, width)]
    scratch = [pltpu.VMEM((tile, ff), f32)]
    if split:
        scratch += [pltpu.VMEM(s, bf16) for s in ((width, ff), (ff, width), (width, width))]
    blocks = [pl.BlockSpec((tile, GW), lambda i: (i, 0)) for _ in ctx]
    return pl.pallas_call(
        functools.partial(middle_kernel, len(ctx), split),
        grid=(rows // tile,),
        in_specs=[SMEM, act] + blocks + [act] + [whole(a) for a in (vecs, bu) + weights],
        out_specs=[act, act, wide, act, wide, act, act, pl.BlockSpec((8, width), lambda i: (0, 0)), pl.BlockSpec((8, ff), lambda i: (0, 0))],
        out_shape=[S(s, bf16) for s in shapes] + [S((8, width), f32), S((8, ff), f32)],
        scratch_shapes=scratch,
        compiler_params=params(),
        cost_estimate=cost(30_000_000_000, 40_000_000),
        name="middle",
    )(at, tokens, *ctx, cot, vecs, bu, *weights)


def grad_down_kernel(groups, at_r, *refs):
    ctx = refs[:groups]
    gb, hid, gd, own_o, other_o = refs[groups:]
    p = pl.program_id(0)
    turns = ((0, at_r[1]), (1, at_r[0]))
    wide = gd.shape[1] // 2
    tall = hid.shape[1] // 2

    @pl.when(p == 0)
    def _():
        lhs = jnp.concatenate([r[...] for r in ctx], axis=1)
        res = tn(lhs, gb[...]).astype(bf16)
        piece = res.shape[0] // 8
        half = piece // 2
        for s in range(8):
            kk, far = owner_of(s, at_r)
            for ab, turn in turns:
                for h in range(2):
                    val = res[s * piece + ab * half : s * piece + (ab + 1) * half, h * wide : (h + 1) * wide]
                    rel = lax.rem(h + turn, 2)
                    for ref, cond in ((other_o, far), (own_o, ~far)):

                        @pl.when(cond)
                        def _(val=val, rel=rel, kk=kk, ab=ab, ref=ref):
                            ref[ab, rel, kk, tall : tall + half] = val

    @pl.when(p > 0)
    def _():
        res = tn(hid[...], gd[...]).astype(bf16)
        kk = lax.rem(p - 1, 4)
        for ab, turn in turns:
            for h in range(2):
                val = res[ab * tall : (ab + 1) * tall, h * wide : (h + 1) * wide]
                rel = lax.rem(h + turn, 2)
                for ref, cond in ((other_o, p < 5), (own_o, p >= 5)):

                    @pl.when(cond)
                    def _(val=val, rel=rel, ab=ab, ref=ref):
                        ref[ab, rel, kk, 0:tall] = val


def grad_down(at, ctx, gb, hid, gd):
    rows, ff = hid.shape
    width = gd.shape[1]
    piece = ff // 8
    part = (2, 2, 4, (piece + width // 8) // 2, width // 2)

    def owner(p, at_r):
        j = jnp.maximum(p - 1, 0)
        z = lax.rem(at_r[2] + lax.rem(j, 4), 4)
        return 0, 2 * z + jnp.where(j < 4, 1 - at_r[3], at_r[3])

    whole = lambda s: pl.BlockSpec(s, lambda p, at_r: (0,) * len(s))
    return pl.pallas_call(
        functools.partial(grad_down_kernel, len(ctx)),
        grid_spec=pltpu.PrefetchScalarGridSpec(
            num_scalar_prefetch=1,
            grid=(9,),
            in_specs=[whole(c.shape) for c in ctx] + [whole(gb.shape), pl.BlockSpec((rows, piece), owner), whole(gd.shape)],
            out_specs=[whole(part), whole(part)],
        ),
        out_shape=[jax.ShapeDtypeStruct(part, bf16)] * 2,
        compiler_params=params(),
        cost_estimate=cost(9_000_000_000, 14_000_000),
        name="grad_down",
    )(at, *ctx, gb, hid, gd)


def grad_up_kernel(at_r, low, gu, own_o, other_o, turned):
    j = pl.program_id(0)
    y, x = at_r[0], at_r[1]

    @pl.when(j == 0)
    def _():
        turned[...] = low[...].T

    res = nn(turned[...], gu[...]).astype(bf16)
    piece = res.shape[0] // 8
    half = piece // 2
    h, l = j // 4, lax.rem(j // 2, 2)
    row = pl.multiple_of(lax.rem(j, 2) * half, 16)
    for s in range(8):
        kk, far = owner_of(s, at_r)
        for ab, turn, other_turn in ((0, x, y), (1, y, x)):
            val = res[s * piece + ab * half : s * piece + (ab + 1) * half]
            one, two = lax.rem(h + turn, 2), lax.rem(l + other_turn, 2)
            for ref, cond in ((other_o, far), (own_o, ~far)):

                @pl.when(cond)
                def _(val=val, kk=kk, ab=ab, one=one, two=two, ref=ref):
                    ref[ab, one, two, kk, pl.ds(row, half), :] = val


def grad_up(at, low, gu):
    rows, width = low.shape
    ff = gu.shape[1]
    step = ff // 8
    part = (2, 2, 2, 4, width // 8, ff // 8)
    whole = pl.BlockSpec(part, lambda j: (0, 0, 0, 0, 0, 0))
    return pl.pallas_call(
        grad_up_kernel,
        grid=(8,),
        in_specs=[SMEM, pl.BlockSpec((rows, width), lambda j: (0, 0)), pl.BlockSpec((rows, step), lambda j: (0, j))],
        out_specs=[whole, whole],
        out_shape=[jax.ShapeDtypeStruct(part, bf16)] * 2,
        scratch_shapes=[pltpu.VMEM((width, rows), bf16)],
        compiler_params=params(),
        cost_estimate=cost(9_000_000_000, 14_000_000),
        name="grad_up",
    )(at, low, gu)


AXES = ("rep", "shard")


def pairs(move):
    found = []
    for y in range(2):
        for x in range(2):
            for z in range(4):
                for c in range(2):
                    j, i, k, d = move(y, x, z, c)
                    found.append(((y * 2 + x) * 8 + z * 2 + c, (j * 2 + i) * 8 + k * 2 + d))
    return found


CORE = pairs(lambda y, x, z, c: (y, x, z, 1 - c))
ACROSS = pairs(lambda y, x, z, c: (y, 1 - x, z, c))
ALONG = pairs(lambda y, x, z, c: (1 - y, x, z, c))
SHIFT = [None] + [pairs(lambda y, x, z, c, n=n: (y, x, (z + n) % 4, c)) for n in (1, 2, 3)]


def send(a, where):
    return lax.ppermute(a, AXES, where)


def tie(values, *after):
    flat, tree = jax.tree.flatten(values)
    return jax.tree.unflatten(tree, lax.optimization_barrier(tuple(flat) + tuple(jax.tree.leaves(after)))[: len(flat)])


def place(own, received, at_r, rows, out, base, quarter):
    y, x, z = at_r[0], at_r[1], at_r[2]
    cols = out.shape[1]
    half = rows // 2
    out[pl.ds(pl.multiple_of(base(z), 16), rows), :] = own
    for k in range(1, 4):
        start = base(lax.rem(z - k + 4, 4))
        for ab in range(2):
            at = pl.ds(pl.multiple_of(start + ab * half, 16), half)
            if quarter:
                wide = cols // 4
                for i in range(2):
                    for l in range(2):
                        one, two = (i, l) if ab == 0 else (l, i)
                        col = (lax.rem(x + i, 2) * 2 + lax.rem(y + l, 2)) * wide
                        out[at, pl.ds(pl.multiple_of(col, 128), wide)] = received(ab, one, two, k)
            else:
                wide = cols // 2
                for one in range(2):
                    col = lax.rem((x, y)[ab] + one, 2) * wide
                    out[at, pl.ds(pl.multiple_of(col, 128), wide)] = received(ab, one, 0, k)


def assemble_half_kernel(out_rows, at_r, *refs):
    n = len(out_rows)
    outs = refs[-n:]
    c = at_r[3]
    for turn, (own, ring, far_x, far_y) in ((c, refs[:4]), (1 - c, refs[4:8])):
        off = 0
        total_half = sum(out_rows) // 2
        for out, rows in zip(outs, out_rows):
            half = rows // 2

            def received(ab, one, two, k):
                if one == 0:
                    return ring[k - 1, ab * total_half + off : ab * total_half + off + half, :]
                return (far_x, far_y)[ab][k - 1, off : off + half, :]

            whole = jnp.concatenate([own[off : off + half], own[total_half + off : total_half + off + half]], axis=0)
            place(whole, received, at_r, rows, out, lambda z: (2 * z + turn) * rows, False)
            off += half


def assemble_quarter_kernel(at_r, *refs):
    out = refs[-1]
    c = at_r[3]
    for turn, (own, near_a, near_b, far) in ((c, refs[:4]), (1 - c, refs[4:8])):
        rows = own.shape[0]

        def received(ab, one, two, k):
            if two == 1:
                return far[ab, one, k - 1]
            return (near_a, near_b)[ab][one, k - 1]

        place(own[...], received, at_r, rows, out, lambda z: (2 * z + turn) * rows, True)


def assemble(kernel, at, parts, shapes):
    return pl.pallas_call(
        kernel,
        in_specs=[SMEM] + [VMEM] * len(parts),
        out_specs=[VMEM] * len(shapes),
        out_shape=[jax.ShapeDtypeStruct(s, bf16) for s in shapes],
        compiler_params=params(),
        cost_estimate=cost(0, sum(4 * s[0] * s[1] for s in shapes)),
        name="assemble",
    )(at, *parts)


def halves(w, x, y):
    half, wide = w.shape[0] // 2, w.shape[1] // 2
    a = lax.dynamic_slice(w, (0, x * wide), (half, wide))
    b = lax.dynamic_slice(w, (half, y * wide), (half, wide))
    return jnp.concatenate([a, b], axis=0)


def spread_half(ring, half):
    return send(ring[:, :half], ACROSS), send(ring[:, half : 2 * half], ALONG)


def swap(parts):
    return tuple(send(p, CORE) for p in parts)


def total(*terms):
    out = terms[0].astype(f32)
    for t in terms[1:]:
        out = out + t.astype(f32)
    return out.astype(bf16)


def finish_kernel(kind, at_r, *refs):
    y, x = at_r[0], at_r[1]
    blocks, outs = refs[:4], refs[4:]
    for ab, turn, other_turn in ((0, x, y), (1, y, x)):
        one, two = (blocks[2 * ab + i][...].astype(f32) for i in range(2))
        left = jnp.where(turn == 0, one, two)
        right = jnp.where(turn == 0, two, one)
        both = jnp.concatenate([left, right], axis=1)
        if kind == "ffn":
            off = 0
            for out in outs[:2]:
                half = out.shape[0] // 2
                out[ab * half : (ab + 1) * half, :] = both[off : off + half]
                off += half
            half = outs[2].shape[0] // 2
            eighth = left.shape[1]
            for h, val in ((0, left), (1, right)):
                near, far = val[off : off + 2 * half], val[off + 2 * half : off + 4 * half]
                quarters = jnp.where(other_turn == 0, near, far), jnp.where(other_turn == 0, far, near)
                for i in range(4):
                    row, col = i % 2 * half, (4 * h + i) * eighth
                    outs[2][ab * half : (ab + 1) * half, col : col + eighth] = quarters[i // 2][row : row + half]
        else:
            half = outs[0].shape[0] // 2
            groups = outs[0].shape[1] // (3 * GW)
            for g in range(groups):
                for i in range(3):
                    col = (i * groups + g) * GW
                    outs[0][ab * half : (ab + 1) * half, col : col + GW] = both[g * half : (g + 1) * half, i * GW : (i + 1) * GW]
            if ab == 0:
                rows = groups * half
                outs[1][...] = left[rows : rows + 16, :128]


def finish(at, kind, blocks, shapes):
    return pl.pallas_call(
        functools.partial(finish_kernel, kind),
        in_specs=[SMEM] + [VMEM] * len(blocks),
        out_specs=[VMEM] * len(shapes),
        out_shape=[jax.ShapeDtypeStruct(s, f32) for s in shapes],
        compiler_params=params(),
        cost_estimate=cost(0, 4_000_000),
        name="finish_" + kind,
    )(at, *blocks)


def pack(vectors, wide):
    block = jnp.concatenate([v.reshape(-1, vectors[1].shape[0]) for v in vectors] + [wide.reshape(4, -1)], axis=0)
    return jnp.pad(block, ((0, 16 - block.shape[0]), (0, 128 - block.shape[1])))


def whole_vectors(every, z, c, piece):
    k = lax.broadcasted_iota(jnp.int32, (2, 4, 8), 1)
    d = lax.broadcasted_iota(jnp.int32, (2, 4, 8), 0)
    s = lax.broadcasted_iota(jnp.int32, (2, 4, 8), 2)
    pick = (s == 2 * ((z - k) % 4) + (c + d) % 2).astype(bf16)
    table = jnp.einsum("dks,dkrl->srl", pick, every, preferred_element_type=f32).astype(bf16)
    table = table[:, :, :piece]
    wide = table[:, 8:12].reshape(1, -1)
    return table.transpose(1, 0, 2).reshape(16, -1), wide


class Sum:
    def __init__(self):
        self.own, self.got = [], []

    def add(self, own, other):
        self.own.append(own)
        self.got.append(send(other, CORE))

    def after(self, *values):
        self.got, self.far, self.parts, self.rest = tie((self.got, self.far, self.parts, self.rest), *values)

    far = parts = ()

    def pair(self, pick, *more):
        found = [total(pick(o), pick(g)) for o, g in zip(self.own, self.got)]
        found = found[0] if len(found) == 1 else jnp.concatenate(found, axis=-2)
        return total(found, *more) if more else found

    def halve(self):
        self.sent = self.pair(lambda a: a[0, 1]), self.pair(lambda a: a[1, 1])
        self.far = send(self.sent[0], ACROSS), send(self.sent[1], ALONG)

    def along_z(self):
        far = self.far
        self.mine = [jnp.stack([self.near(i, k) for i in range(2)]) for k in range(4)]
        self.sent = self.mine[1:]
        self.far = ()
        self.parts = [send(self.mine[k], SHIFT[k]) for k in range(1, 4)]

    def joined(self, i):
        one, two, rows = self.sent[i], self.far[i], self.rows
        summed = total(one[:rows], two[:rows])
        return jnp.concatenate([summed, one[rows:], two[rows:]], axis=0)

    rest = ()

    def near(self, i, k):
        if self.rest:
            return total(self.rest[i][k], self.far[i][k])
        terms = []
        at = 0
        for o, g in zip(self.own, self.got):
            rows = o.shape[3]
            terms.append(total(o[i, 0, k], g[i, 0, k], self.far[i][k, at : at + rows]))
            at += rows
        return terms[0] if len(terms) == 1 else jnp.concatenate(terms, axis=0)

    def quarter(self):
        own, got, far = self.own[0], self.got[0], self.far
        part = lambda i, j: total(own[i, 0, j], got[i, 0, j], far[i][j])
        self.sent = part(0, 1), part(1, 1)
        self.rest = part(0, 0), part(1, 0)
        self.far = send(self.sent[0], ALONG), send(self.sent[1], ACROSS)

    def across(self, more=None):
        both = total(self.mine[0], *self.parts)
        rows = both.shape[1]
        if more is not None:
            extra = total(more.mine[0], *more.parts)
            both = jnp.concatenate([both, extra], axis=1)
        self.got = self.parts = ()
        self.sent = both[0], both[1]
        self.far = send(both[0], ALONG), send(both[1], ACROSS)
        self.rows = rows

    def share(self):
        a, b = (self.joined(i) for i in range(2))
        self.sent = a, b
        self.out = a, send(a, ACROSS), b, send(b, ALONG)


def shards_near(
    tokens,
    cotangent,
    qkv_weight,
    query_value_bias,
    out_weight,
    out_bias,
    norm_one_gain,
    norm_one_shift,
    up_weight,
    up_bias,
    down_weight,
    down_bias,
    norm_two_gain,
    norm_two_shift,
    segment_ids,
    valid,
):
    length = segment_ids.shape[1]
    width = tokens.shape[1]
    groups = width // GW
    ff = up_bias.shape[0] * 8
    piece = out_bias.shape[0]
    r, s = lax.axis_index("rep"), lax.axis_index("shard")
    y, x, z, c = r // 2, r % 2, s // 2, s % 2
    at = jnp.stack([y, x, z, c]).astype(jnp.int32)

    half = piece // 2
    block = pack(
        (query_value_bias, out_bias, norm_one_gain, norm_one_shift, down_bias, norm_two_gain, norm_two_shift), up_bias
    )
    lines = lambda n, cols: jnp.pad(block.reshape(n, -1), ((0, 8 - n), (0, cols - 2048 // n)))
    dr = down_weight.shape[0] // 2
    own_q = jnp.concatenate([qkv_weight, lines(1, 3 * width)], axis=0)
    own_d = jnp.concatenate([down_weight[:dr], out_weight[:half], down_weight[dr:], out_weight[half:]], axis=0)
    other_q, other_u, other_d = swap((own_q, up_weight, own_d))
    held = jnp.concatenate([halves(qkv_weight, x, y), lines(2, 3 * width // 2)], axis=0)
    ring = []
    for step in range(3):
        if step == 2:
            held = tie(held, other_q, other_u, other_d)
        held = send(held, SHIFT[1])
        ring.append(held)
    ring_q = jnp.stack(ring)
    far_q = spread_half(ring_q, half)
    first_u = lax.dynamic_slice(up_weight, (0, (2 * x + y) * (ff // 4)), (piece, ff // 4))
    first_u = tie(first_u, held)
    ring_u = [send(first_u, SHIFT[k]) for k in range(1, 4)]
    rest_q = swap(tie((ring_q,) + far_q, ring_u))
    swapped_q = rest_q[0]
    parts_q = (own_q, ring_q) + far_q + (other_q,) + rest_q
    (wqkv,) = assemble(
        functools.partial(assemble_half_kernel, [qkv_weight.shape[0]]), at, parts_q, [(width, 3 * width)]
    )
    blocks = lambda own, ring: jnp.concatenate([own[None, piece : piece + 1, :2048].reshape(1, 16, 128), ring[:, piece : piece + 2, :1024].reshape(3, 16, 128)])
    vecs, bu = whole_vectors(jnp.stack([blocks(own_q, ring_q), blocks(other_q, swapped_q)]), z, c, piece)

    aq, ak = masks(segment_ids, valid)
    ring_u = jnp.stack(tie(ring_u, far_q))
    first_d = tie(halves(own_d, x, y), ring_u)
    d2 = send(first_d, SHIFT[2])
    a, b = ring_u[:, :half], ring_u[:, half:]
    a2, b2 = send(a, ACROSS), send(b, ALONG)
    saved = [attend(0, tie(tokens, a, b, first_d), wqkv, vecs, aq, ak, length)]
    a2, b2, d2, first_d = tie((a2, b2, d2, first_d), saved[0][3])
    a3, b3 = jnp.stack([a, a2]), jnp.stack([b, b2])
    a4, b4 = send(a3, ALONG), send(b3, ACROSS)
    d1, d3 = send(first_d, SHIFT[1]), send(first_d, SHIFT[3])
    other_a = send(a3, CORE)
    saved.append(attend(1, tie(tokens, a3, b3, d2), wqkv, vecs, aq, ak, length))
    a4, b4, other_a, ring_d = tie((a4, b4, other_a, [d1, d2, d3]), saved[1][3])
    ring_d = jnp.stack(ring_d)
    ab4 = jnp.stack([a4, b4])
    far_d = spread_half(ring_d, dr + half)
    other_b, other_ab, other_ring = swap((b3, ab4, ring_d))
    saved.append(attend(2, tie(tokens, ring_d, ab4), wqkv, vecs, aq, ak, length))
    far_d, other_b, other_ab, other_ring = tie((far_d, other_b, other_ab, other_ring), saved[2][3])
    parts_u = (up_weight, a3, b3, ab4, other_u, other_a, other_b, other_ab)
    parts_d = (own_d, ring_d) + far_d + (other_d, other_ring) + swap(far_d)

    ctx = [f[3] for f in saved]
    result, low, hid, gd, gu, gb, gc, vec, bup = middle(
        at, tokens, ctx, cotangent, vecs, bu, parts_u + parts_d, (2 * dr, piece)
    )

    down, up, qkv = Sum(), Sum(), Sum()
    own, other = grad_down(at, ctx, gb, hid, gd)
    down.add(own, other)
    own, other = grad_up(at, *tie((low, gu), other))
    up.add(own, other)
    down.after(other)
    down.halve()
    own, other, dx, db0 = attend_back("first", 0, at, saved[0], tie(gc, down.sent, other), aq, ak, tokens, wqkv, gb, length)
    down.after(dx)
    up.after(dx)
    down.along_z()
    up.halve()
    dx = tie(dx, down.sent, up.sent)
    own, other, dx, db1 = attend_back("second", 1, at, saved[1], gc, aq, ak, tokens, wqkv, dx, length, (own, other))
    two = own, other
    up.after(dx)
    up.quarter()
    wide = bup[0].reshape(8, 4, piece).transpose(1, 0, 2).reshape(4, width)
    table = jnp.concatenate([vec[:6], wide, jnp.zeros((4, width), f32)], axis=0)
    own, other, dx, _ = attend_back(
        "third", 2, at, saved[2], gc, aq, ak, tokens, wqkv, tie(dx, up.sent), length, (db0, db1, table)
    )
    down.after(dx)
    up.after(dx)
    other, first_other = tie((other, two[1]), up.far)
    qkv.add(two[0], first_other)
    qkv.add(own, other)
    up.after(down.parts)
    up.along_z()
    qkv.halve()
    up.after(qkv.far)
    qkv.after(up.parts)
    qkv.along_z()
    down.across(up)
    down.share()
    dwd, dwo, dwu = finish(at, "ffn", down.out, [down_weight.shape, out_weight.shape, up_weight.shape])
    qkv.after(dwd, dwo, dwu)
    qkv.across()
    qkv.share()
    dwq, small = finish(at, "qkv", qkv.out, [qkv_weight.shape, (16, 128)])
    one = lambda i: small[i, :piece]
    return (
        result,
        dx,
        dwq,
        small[:2, :piece],
        dwo,
        one(2),
        one(3),
        one(4),
        dwu,
        small[8:12, :piece].reshape(-1),
        dwd,
        one(5),
        one(6),
        one(7),
    )


def spread(args):
    flat = [a.reshape(-1) for a in args]
    packed = jnp.concatenate(flat)
    every = lax.all_gather(packed, "shard", axis=0)
    out, at = [], 0
    for a in args:
        part = every[:, at : at + a.size].reshape((-1,) + a.shape)
        at += a.size
        out.append(jnp.moveaxis(part, 0, -2).reshape(a.shape[:-1] + (-1,)))
    return out


def shards(
    tokens,
    cotangent,
    qkv_weight,
    query_value_bias,
    out_weight,
    out_bias,
    norm_one_gain,
    norm_one_shift,
    up_weight,
    up_bias,
    down_weight,
    down_bias,
    norm_two_gain,
    norm_two_shift,
    segment_ids,
    valid,
):
    length = segment_ids.shape[1]
    width = tokens.shape[1]
    groups = width // GW
    gather = lambda a: lax.all_gather(a, "shard", axis=0, tiled=True)
    *rest, bu = spread(
        (query_value_bias, out_bias, norm_one_gain, norm_one_shift, down_bias, norm_two_gain, norm_two_shift, up_bias)
    )
    vecs = jnp.concatenate([v.reshape(-1, width) for v in rest] + [jnp.zeros((8, width), bf16)], axis=0)
    wqkv, wd, wo, wu = gather(qkv_weight), gather(down_weight), gather(out_weight), gather(up_weight)
    at = jnp.zeros((4,), jnp.int32)
    aq, ak = masks(segment_ids, valid)
    saved = [attend(g, tokens, wqkv, vecs, aq, ak, length) for g in range(groups)]
    ctx = [f[3] for f in saved]
    result, low, hid, gd, gu, gb, gc, vec, bup = middle(at, tokens, ctx, cotangent, vecs, bu[None], (wu, wd, wo))
    dwd = tn(hid, gd).astype(bf16)
    dwu = tn(low, gu).astype(bf16)
    dwo = tn(jnp.concatenate(ctx, axis=1), gb).astype(bf16)
    dx, dws, dbs = gb, [], []
    for g in range(groups):
        dw, dx, db = attend_back("plain", g, at, saved[g], gc, aq, ak, tokens, wqkv, dx, length)
        dws.append(dw)
        dbs.append(db)
    dwq = jnp.concatenate([dw[i] for i in range(3) for dw in dws], axis=1)
    db = jnp.stack(dbs).reshape(groups, 3, GW).transpose(1, 0, 2).reshape(3, width)
    small = jnp.concatenate([db[0], db[2], vec[:6].reshape(-1), bup[0]])
    small = lax.psum(small.reshape(-1, 128), ("rep", "shard")).reshape(-1)

    def owned(a):
        part = lax.psum_scatter(a, "shard", scatter_dimension=0, tiled=True)
        return lax.psum(part, "rep").astype(f32)

    rank = lax.axis_index("shard")
    own = lambda at, size: lax.dynamic_slice(small, (at + rank * size,), (size,))
    piece = out_bias.shape[0]
    vs = [own(width * i, piece) for i in range(8)]
    dbu = own(8 * width, up_bias.shape[0])
    gd_w, gu_w, go_w, gq_w = owned(dwd), owned(dwu), owned(dwo), owned(dwq)
    return result, dx, gq_w, jnp.stack(vs[:2]), go_w, vs[2], vs[3], vs[4], gu_w, dbu, gd_w, vs[5], vs[6], vs[7]


def solution(mesh):
    rows, one = P(("rep", "shard"), None), P("shard")
    mat, two = P("shard", None), P(None, "shard")
    near = mesh.shape["rep"] == 4 and mesh.shape["shard"] == 8
    return jax.shard_map(
        shards_near if near else shards,
        mesh=mesh,
        in_specs=(rows, rows, mat, two, mat, one, one, one, mat, one, mat, one, one, one, rows, rows),
        out_specs=(rows, rows, mat, two, mat, one, one, one, mat, one, mat, one, one, one),
        check_vma=False,
    )
```

```python
import functools

import jax
import jax.numpy as jnp
from jax import lax
from jax.experimental import pallas as pl
from jax.experimental.pallas import tpu as pltpu
from jax.sharding import PartitionSpec as P

HD = 64
GW = 256
SCALE = 0.125 * 1.4426950408889634
BIG = 1e30
VMEM_LIMIT = 60 * 1024 * 1024
bf16 = jnp.bfloat16
f32 = jnp.float32
SMEM = pl.BlockSpec(memory_space=pltpu.SMEM)
VMEM = pl.BlockSpec(memory_space=pltpu.VMEM)


def nn(a, b):
    return lax.dot_general(a, b, (((1,), (0,)), ((), ())), preferred_element_type=f32)


def nt(a, b):
    return lax.dot_general(a, b, (((1,), (1,)), ((), ())), preferred_element_type=f32)


def tn(a, b):
    return lax.dot_general(a, b, (((0,), (0,)), ((), ())), preferred_element_type=f32)


def params(**more):
    return pltpu.CompilerParams(vmem_limit_bytes=VMEM_LIMIT, **more)


def cost(flops, moved):
    return pl.CostEstimate(flops=flops, bytes_accessed=moved, transcendentals=0)


def attend_kernel(tok, wq, wk, wv, vecs, aq, ak, q_o, k_o, v_o, ctx_o, lse_o):
    x = tok[...]
    q = (nn(x, wq[...]) + vecs[0:1, :].astype(f32)).astype(bf16)
    k = nn(x, wk[...]).astype(bf16)
    v = (nn(x, wv[...]) + vecs[1:2, :].astype(f32)).astype(bf16)
    q_o[...] = q
    k_o[...] = k
    v_o[...] = v
    length, width = q.shape
    lane = lax.broadcasted_iota(jnp.int32, (length, width), 1) // HD
    slot = lax.broadcasted_iota(jnp.int32, (length, 128), 1)
    acc = None
    scale = jnp.zeros((length, width), f32)
    stat = jnp.zeros((length, 128), f32)
    for h in range(width // HD):
        mine = lane == h
        qa = jnp.where(mine, q, aq[...])
        ka = jnp.where(mine, k, ak[...])
        va = jnp.where(mine, v, jnp.zeros_like(v))
        t = nt(qa, ka) * SCALE
        m = jnp.max(t, axis=1, keepdims=True)
        p = jnp.exp2(t - m)
        total = jnp.sum(p, axis=1, keepdims=True)
        part = nn(p.astype(bf16), va)
        acc = part if acc is None else acc + part
        scale = jnp.where(mine, 1.0 / total, scale)
        stat = jnp.where(slot == h, m + jnp.log2(total), stat)
    ctx_o[...] = (acc * scale).astype(bf16)
    lse_o[0] = stat.T[:8]


def attend(g, tokens, w, vecs, aq, ak, length):
    rows, width = tokens.shape
    groups = width // GW
    seqs = rows // length
    col = lambda o: pl.BlockSpec((width, GW), lambda b: (0, o * groups + g))
    seq = pl.BlockSpec((length, width), lambda b: (b, 0))
    blk = pl.BlockSpec((length, GW), lambda b: (b, 0))
    act = jax.ShapeDtypeStruct((rows, GW), bf16)
    return pl.pallas_call(
        attend_kernel,
        grid=(seqs,),
        in_specs=[seq, col(0), col(1), col(2), pl.BlockSpec((16, GW), lambda b: (0, g)), blk, blk],
        out_specs=[blk, blk, blk, blk, pl.BlockSpec((1, 8, length), lambda b: (b, 0, 0))],
        out_shape=[act, act, act, act, jax.ShapeDtypeStruct((seqs, 8, length), f32)],
        compiler_params=params(),
        cost_estimate=cost(4_000_000_000, 5_000_000),
        name="attend",
    )(tokens, w, w, w, vecs, aq, ak)


def owners(at_r, own, other):
    for k in range(4):
        z = lax.rem(k + at_r[2], 4)
        for core, ref in ((at_r[3], own), (1 - at_r[3], other)):
            yield k, 2 * z + core, ref


def select_lanes(s, piece, width):
    i = lax.broadcasted_iota(jnp.int32, (128, width), 0)
    j = lax.broadcasted_iota(jnp.int32, (128, width), 1)
    return ((j == s * piece + i) & (i < piece)).astype(f32).astype(bf16)


def attend_back_kernel(mode, at_r, q_r, k_r, v_r, do_r, ctx_r, lse_r, aq, ak, tok, wq, wk, wv, dx_i, *rest):
    b = pl.program_id(0)
    last = b == pl.num_programs(0) - 1
    if mode == "plain":
        dw_o, dx_o, db_o, dw_s = rest
    elif mode == "first":
        own_o, other_o, dx_o, db_o, dw_s = rest
    elif mode == "second":
        _, _, own_o, other_o, dx_o, db_o, dw_s = rest
    else:
        db0, db1, tbl, own_o, other_o, dx_o, db_o, dw_s = rest
    q, k, v, do = q_r[...], k_r[...], v_r[...], do_r[...]
    length, width = q.shape
    lane = lax.broadcasted_iota(jnp.int32, (length, width), 1) // HD
    sel = lax.broadcasted_iota(jnp.int32, (8, width), 1) // HD == lax.broadcasted_iota(jnp.int32, (8, width), 0)
    sel = sel.astype(f32).astype(bf16)
    prod = do.astype(f32) * ctx_r[...].astype(f32)
    hi = prod.astype(bf16)
    lo = (prod - hi.astype(f32)).astype(bf16)
    delta = nt(sel, hi) + nt(sel, lo)
    dq = dk = dv = None
    zero = jnp.zeros_like(q)
    for h in range(width // HD):
        mine = lane == h
        qa = jnp.where(mine, q, aq[...])
        ka = jnp.where(mine, k, ak[...])
        va = jnp.where(mine, v, zero)
        p = jnp.exp2(nt(ka, qa) * SCALE - lse_r[0, h : h + 1, :])
        dp = nt(va, do)
        ds = (p * (dp - delta[h : h + 1, :])).astype(bf16)
        dv_h = nn(p.astype(bf16), jnp.where(mine, do, zero))
        dk_h = nn(ds, jnp.where(mine, q, zero))
        dq_h = tn(ds, jnp.where(mine, k, zero))
        dv = dv_h if dv is None else dv + dv_h
        dk = dk_h if dk is None else dk + dk_h
        dq = dq_h if dq is None else dq + dq_h
    dq = (dq * 0.125).astype(bf16)
    dk = (dk * 0.125).astype(bf16)
    dv = dv.astype(bf16)
    back = jnp.concatenate([dq, dk, dv], axis=1)
    dw = tn(tok[...], back)
    dx = nt(dq, wq[...]) + nt(dk, wk[...]) + nt(dv, wv[...])
    dx_o[...] = (dx_i[...].astype(f32) + dx).astype(dx_o.dtype)
    sums = jnp.sum(back.astype(f32), axis=0, keepdims=True)

    @pl.when(b == 0)
    def _():
        dw_s[...] = dw
        db_o[...] = sums

    @pl.when(b > 0)
    def _():
        dw_s[...] += dw
        db_o[...] += sums

    @pl.when(last)
    def _():
        if mode == "plain":
            for i in range(3):
                dw_o[i] = dw_s[:, i * width : (i + 1) * width].astype(bf16)
            return
        piece = dw_s.shape[0] // 8
        half, wide = piece // 2, dw_s.shape[1] // 2
        for k, s, ref in owners(at_r, own_o, other_o):
            for ab, turn in ((0, at_r[1]), (1, at_r[0])):
                row = pl.multiple_of(s * piece + ab * half, 16)
                for h in range(2):
                    val = dw_s[pl.ds(row, half), h * wide : (h + 1) * wide]
                    ref[ab, lax.rem(h + turn, 2), k, 0:half] = val.astype(bf16)

        if mode == "third":
            sums = [r[...] for r in (db0, db1, db_o)]
            dbq = jnp.concatenate([r[:, :width] for r in sums], axis=1)
            dbv = jnp.concatenate([r[:, 2 * width :] for r in sums], axis=1)
            table = jnp.concatenate([dbq, dbv, tbl[...]], axis=0).astype(bf16)
            extra = jnp.zeros((4, 16, wide), bf16)
            for ab in range(2):
                for h in range(2):
                    own_o[ab, h, :, half : half + 16, :] = extra
                    other_o[ab, h, :, half : half + 16, :] = extra
            for k, s, ref in owners(at_r, own_o, other_o):
                blk = nt(table, select_lanes(s, piece, table.shape[1])).astype(bf16)
                ref[0, at_r[1], k, half : half + 16, 0:128] = blk


def attend_back(mode, g, at, saved, gc, aq, ak, tokens, w, dx, length, extra=()):
    rows, width = tokens.shape
    groups = width // GW
    seqs = rows // length
    half = width // 16
    col = lambda o: pl.BlockSpec((width, GW), lambda b: (0, o * groups + g))
    seq = pl.BlockSpec((length, width), lambda b: (b, 0))
    blk = pl.BlockSpec((length, GW), lambda b: (b, 0))
    whole = lambda s: pl.BlockSpec(s, lambda b: (0,) * len(s))
    S = jax.ShapeDtypeStruct
    tall = {"first": 2 * half, "second": 2 * half, "third": half + 16, "plain": 0}[mode]
    at_row = 1 if mode == "second" else 0
    block = half + 16 if mode == "third" else half
    part = pl.BlockSpec((2, 2, 4, block, 3 * GW // 2), lambda b: (0, 0, 0, at_row, 0))
    if mode == "plain":
        out_specs, out_shape = [whole((3, width, GW))], [S((3, width, GW), bf16)]
    else:
        out_specs, out_shape = [part, part], [S((2, 2, 4, tall, 3 * GW // 2), bf16)] * 2
    out_specs += [seq, whole((1, 3 * GW))]
    out_shape += [S((rows, width), bf16 if mode == "third" or g == groups - 1 else f32), S((1, 3 * GW), f32)]
    in_specs = [SMEM, blk, blk, blk, pl.BlockSpec((length, GW), lambda b: (b, g)), blk]
    in_specs += [pl.BlockSpec((1, 8, length), lambda b: (b, 0, 0)), blk, blk, seq, col(0), col(1), col(2), seq]
    aliases = {}
    if mode == "second":
        in_specs += [pl.BlockSpec(memory_space=pl.ANY)] * 2
        aliases = {len(in_specs) - 2: 0, len(in_specs) - 1: 1}
    elif mode == "third":
        in_specs += [whole(e.shape) for e in extra]
    q, k, v, ctx, lse = saved
    return pl.pallas_call(
        functools.partial(attend_back_kernel, mode),
        grid=(seqs,),
        in_specs=in_specs,
        out_specs=out_specs,
        out_shape=out_shape,
        scratch_shapes=[pltpu.VMEM((width, 3 * GW), f32)],
        input_output_aliases=aliases,
        compiler_params=params(),
        cost_estimate=cost(8_000_000_000, 8_000_000),
        name="attend_back",
    )(at, q, k, v, gc, ctx, lse, aq, ak, tokens, w, w, w, dx, *extra)


def masks(segment_ids, valid):
    code = (segment_ids + 8 * valid).reshape(-1, 1)
    lane = lax.broadcasted_iota(jnp.int32, (1, GW), 1) % HD
    same = code == lane
    aq = same.astype(bf16)
    ak = jnp.where((lane < 16) & ~same, -BIG, 0.0).astype(bf16)
    return aq, ak


def phi(x):
    return 0.5 * (1.0 + lax.erf(x * 0.7071067811865476)), jnp.exp(-0.5 * x * x) * 0.3989422804014327


def middle_kernel(groups, split, at_r, tok, *refs):
    ctx_r = refs[:groups]
    cot, vecs, bu = refs[groups : groups + 3]
    refs = refs[groups + 3 :]
    i = pl.program_id(0)
    if split:
        up_parts, down_parts, refs = refs[:8], refs[8:16], refs[16:]
        wu, wd, wo = refs[-3:]
        refs = refs[:-3]

        @pl.when(i == 0)
        def _():
            assemble_quarter_kernel(at_r, *up_parts, wu)
            assemble_half_kernel(split, at_r, *down_parts, wd, wo)

    else:
        wu, wd, wo, refs = *refs[:3], refs[3:]
    out_o, low_o, hid_o, gd_o, gu_o, gb_o, gc_o, vec_o, bup_o, slope = refs
    width = tok.shape[1]
    ff = bu.shape[1]
    step = width
    chunks = ff // step
    bo, g1, s1, bd, g2, s2 = (vecs[j : j + 1, :].astype(f32) for j in range(2, 8))
    ctx = jnp.concatenate([r[...] for r in ctx_r], axis=1)
    pre = tok[...].astype(f32) + nn(ctx, wo[...]) + bo
    mean = lambda v: jnp.mean(v, axis=1, keepdims=True)
    centre = pre - mean(pre)
    r1 = lax.rsqrt(mean(centre * centre) + 1e-05)
    n1 = centre * r1
    normed = n1 * g1 + s1
    low = normed.astype(bf16)
    low_o[...] = low
    acc = normed + bd
    for c in range(chunks):
        cols = slice(c * step, (c + 1) * step)
        hp = nn(low, wu[:, cols]) + bu[:, cols].astype(f32)
        cdf, pdf = phi(hp)
        slope[:, cols] = cdf + hp * pdf
        hid = (hp * cdf).astype(bf16)
        hid_o[:, cols] = hid
        acc = acc + nn(hid, wd[cols, :])
    centre = acc - mean(acc)
    r2 = lax.rsqrt(mean(centre * centre) + 1e-05)
    n2 = centre * r2
    out_o[...] = (n2 * g2 + s2).astype(bf16)
    ct = cot[...].astype(f32)
    e = ct * g2
    gp2 = r2 * (e - mean(e) - n2 * mean(e * n2))
    gd = gp2.astype(bf16)
    gd_o[...] = gd
    acc = gp2
    total = lambda v: jnp.sum(v, axis=0, keepdims=True)

    def put(ref, at, v):
        @pl.when(i == 0)
        def _():
            ref[at] = v

        @pl.when(i > 0)
        def _():
            ref[at] += v

    for c in range(chunks):
        cols = slice(c * step, (c + 1) * step)
        gu = (nt(gd, wd[cols, :]) * slope[:, cols]).astype(bf16)
        gu_o[:, cols] = gu
        put(bup_o, (slice(0, 1), cols), total(gu.astype(f32)))
        acc = acc + nt(gu, wu[:, cols])
    e = acc * g1
    gp1 = r1 * (e - mean(e) - n1 * mean(e * n1))
    gb = gp1.astype(bf16)
    gb_o[...] = gb
    gc_o[...] = nt(gb, wo[...]).astype(bf16)
    for at, v in enumerate((gb.astype(f32), acc * n1, acc, gd.astype(f32), ct * n2, ct)):
        put(vec_o, (slice(at, at + 1), slice(None)), total(v))


def middle(at, tokens, ctx, cot, vecs, bu, weights, split=None, tile=256):
    rows, width = tokens.shape
    ff = bu.shape[1]
    act = pl.BlockSpec((tile, width), lambda i: (i, 0))
    wide = pl.BlockSpec((tile, ff), lambda i: (i, 0))
    whole = lambda a: pl.BlockSpec(a.shape, lambda i: (0,) * a.ndim, pipeline_mode=pl.Buffered(1))
    S = jax.ShapeDtypeStruct
    shapes = [(rows, width), (rows, width), (rows, ff), (rows, width), (rows, ff), (rows, width), (rows, width)]
    scratch = [pltpu.VMEM((tile, ff), f32)]
    if split:
        scratch += [pltpu.VMEM(s, bf16) for s in ((width, ff), (ff, width), (width, width))]
    blocks = [pl.BlockSpec((tile, GW), lambda i: (i, 0)) for _ in ctx]
    return pl.pallas_call(
        functools.partial(middle_kernel, len(ctx), split),
        grid=(rows // tile,),
        in_specs=[SMEM, act] + blocks + [act] + [whole(a) for a in (vecs, bu) + weights],
        out_specs=[act, act, wide, act, wide, act, act, pl.BlockSpec((8, width), lambda i: (0, 0)), pl.BlockSpec((8, ff), lambda i: (0, 0))],
        out_shape=[S(s, bf16) for s in shapes] + [S((8, width), f32), S((8, ff), f32)],
        scratch_shapes=scratch,
        compiler_params=params(),
        cost_estimate=cost(30_000_000_000, 40_000_000),
        name="middle",
    )(at, tokens, *ctx, cot, vecs, bu, *weights)


def grad_down_kernel(groups, at_r, *refs):
    ctx = refs[:groups]
    gb, hid, gd, own_o, other_o, res_s = refs[groups:]
    p = pl.program_id(0)
    turns = ((0, at_r[1]), (1, at_r[0]))
    wide = gd.shape[1] // 2
    tall = hid.shape[1] // 2

    @pl.when(p == 0)
    def _():
        lhs = jnp.concatenate([r[...] for r in ctx], axis=1)
        res_s[...] = tn(lhs, gb[...]).astype(bf16)
        piece = res_s.shape[0] // 8
        half = piece // 2
        for k, s, ref in owners(at_r, own_o, other_o):
            for ab, turn in turns:
                row = pl.multiple_of(s * piece + ab * half, 16)
                for h in range(2):
                    ref[ab, lax.rem(h + turn, 2), k, tall : tall + half] = res_s[pl.ds(row, half), h * wide : (h + 1) * wide]

    @pl.when(p > 0)
    def _():
        res = tn(hid[...], gd[...]).astype(bf16)
        kk = lax.rem(p - 1, 4)
        for ab, turn in turns:
            for h in range(2):
                val = res[ab * tall : (ab + 1) * tall, h * wide : (h + 1) * wide]
                rel = lax.rem(h + turn, 2)
                for ref, cond in ((other_o, p < 5), (own_o, p >= 5)):

                    @pl.when(cond)
                    def _(val=val, rel=rel, ab=ab, ref=ref):
                        ref[ab, rel, kk, 0:tall] = val


def grad_down(at, ctx, gb, hid, gd):
    rows, ff = hid.shape
    width = gd.shape[1]
    piece = ff // 8
    part = (2, 2, 4, (piece + width // 8) // 2, width // 2)

    def owner(p, at_r):
        j = jnp.maximum(p - 1, 0)
        z = lax.rem(at_r[2] + lax.rem(j, 4), 4)
        return 0, 2 * z + jnp.where(j < 4, 1 - at_r[3], at_r[3])

    whole = lambda s: pl.BlockSpec(s, lambda p, at_r: (0,) * len(s))
    return pl.pallas_call(
        functools.partial(grad_down_kernel, len(ctx)),
        grid_spec=pltpu.PrefetchScalarGridSpec(
            num_scalar_prefetch=1,
            grid=(9,),
            in_specs=[whole(c.shape) for c in ctx] + [whole(gb.shape), pl.BlockSpec((rows, piece), owner), whole(gd.shape)],
            out_specs=[whole(part), whole(part)],
            scratch_shapes=[pltpu.VMEM((width, width), bf16)],
        ),
        out_shape=[jax.ShapeDtypeStruct(part, bf16)] * 2,
        compiler_params=params(),
        cost_estimate=cost(9_000_000_000, 14_000_000),
        name="grad_down",
    )(at, *ctx, gb, hid, gd)


def grad_up_kernel(at_r, low, gu, own_o, other_o, turned, res_s):
    j = pl.program_id(0)
    y, x = at_r[0], at_r[1]

    @pl.when(j == 0)
    def _():
        turned[...] = low[...].T

    res_s[...] = nn(turned[...], gu[...]).astype(bf16)
    piece = res_s.shape[0] // 8
    half = piece // 2
    h, l = j // 4, lax.rem(j // 2, 2)
    to = pl.multiple_of(lax.rem(j, 2) * half, 16)
    for k, s, ref in owners(at_r, own_o, other_o):
        for ab, turn, other_turn in ((0, x, y), (1, y, x)):
            row = pl.multiple_of(s * piece + ab * half, 16)
            one, two = lax.rem(h + turn, 2), lax.rem(l + other_turn, 2)
            ref[ab, one, two, k, pl.ds(to, half), :] = res_s[pl.ds(row, half), :]


def grad_up(at, low, gu):
    rows, width = low.shape
    ff = gu.shape[1]
    step = ff // 8
    part = (2, 2, 2, 4, width // 8, ff // 8)
    whole = pl.BlockSpec(part, lambda j: (0, 0, 0, 0, 0, 0))
    return pl.pallas_call(
        grad_up_kernel,
        grid=(8,),
        in_specs=[SMEM, pl.BlockSpec((rows, width), lambda j: (0, 0)), pl.BlockSpec((rows, step), lambda j: (0, j))],
        out_specs=[whole, whole],
        out_shape=[jax.ShapeDtypeStruct(part, bf16)] * 2,
        scratch_shapes=[pltpu.VMEM((width, rows), bf16), pltpu.VMEM((width, step), bf16)],
        compiler_params=params(),
        cost_estimate=cost(9_000_000_000, 14_000_000),
        name="grad_up",
    )(at, low, gu)


AXES = ("rep", "shard")


def pairs(move):
    found = []
    for y in range(2):
        for x in range(2):
            for z in range(4):
                for c in range(2):
                    j, i, k, d = move(y, x, z, c)
                    found.append(((y * 2 + x) * 8 + z * 2 + c, (j * 2 + i) * 8 + k * 2 + d))
    return found


CORE = pairs(lambda y, x, z, c: (y, x, z, 1 - c))
ACROSS = pairs(lambda y, x, z, c: (y, 1 - x, z, c))
ALONG = pairs(lambda y, x, z, c: (1 - y, x, z, c))
SHIFT = [None] + [pairs(lambda y, x, z, c, n=n: (y, x, (z + n) % 4, c)) for n in (1, 2, 3)]


def send(a, where):
    return lax.ppermute(a, AXES, where)


def tie(values, *after):
    flat, tree = jax.tree.flatten(values)
    return jax.tree.unflatten(tree, lax.optimization_barrier(tuple(flat) + tuple(jax.tree.leaves(after)))[: len(flat)])


def place(own, received, at_r, rows, out, base, quarter):
    y, x, z = at_r[0], at_r[1], at_r[2]
    cols = out.shape[1]
    half = rows // 2
    out[pl.ds(pl.multiple_of(base(z), 16), rows), :] = own
    for k in range(1, 4):
        start = base(lax.rem(z - k + 4, 4))
        for ab in range(2):
            at = pl.ds(pl.multiple_of(start + ab * half, 16), half)
            if quarter:
                wide = cols // 4
                for i in range(2):
                    for l in range(2):
                        one, two = (i, l) if ab == 0 else (l, i)
                        col = (lax.rem(x + i, 2) * 2 + lax.rem(y + l, 2)) * wide
                        out[at, pl.ds(pl.multiple_of(col, 128), wide)] = received(ab, one, two, k)
            else:
                wide = cols // 2
                for one in range(2):
                    col = lax.rem((x, y)[ab] + one, 2) * wide
                    out[at, pl.ds(pl.multiple_of(col, 128), wide)] = received(ab, one, 0, k)


def assemble_half_kernel(out_rows, at_r, *refs):
    n = len(out_rows)
    outs = refs[-n:]
    c = at_r[3]
    for turn, (own, ring, far_x, far_y) in ((c, refs[:4]), (1 - c, refs[4:8])):
        off = 0
        total_half = sum(out_rows) // 2
        for out, rows in zip(outs, out_rows):
            half = rows // 2

            def received(ab, one, two, k):
                if one == 0:
                    return ring[k - 1, ab * total_half + off : ab * total_half + off + half, :]
                return (far_x, far_y)[ab][k - 1, off : off + half, :]

            whole = jnp.concatenate([own[off : off + half], own[total_half + off : total_half + off + half]], axis=0)
            place(whole, received, at_r, rows, out, lambda z: (2 * z + turn) * rows, False)
            off += half


def assemble_quarter_kernel(at_r, *refs):
    out = refs[-1]
    c = at_r[3]
    for turn, (own, near_a, near_b, far) in ((c, refs[:4]), (1 - c, refs[4:8])):
        rows = own.shape[0]

        def received(ab, one, two, k):
            if two == 1:
                return far[ab, one, k - 1]
            return (near_a, near_b)[ab][one, k - 1]

        place(own[...], received, at_r, rows, out, lambda z: (2 * z + turn) * rows, True)


def assemble(kernel, at, parts, shapes):
    return pl.pallas_call(
        kernel,
        in_specs=[SMEM] + [VMEM] * len(parts),
        out_specs=[VMEM] * len(shapes),
        out_shape=[jax.ShapeDtypeStruct(s, bf16) for s in shapes],
        compiler_params=params(),
        cost_estimate=cost(0, sum(4 * s[0] * s[1] for s in shapes)),
        name="assemble",
    )(at, *parts)


def halves(w, x, y):
    half, wide = w.shape[0] // 2, w.shape[1] // 2
    a = lax.dynamic_slice(w, (0, x * wide), (half, wide))
    b = lax.dynamic_slice(w, (half, y * wide), (half, wide))
    return jnp.concatenate([a, b], axis=0)


def spread_half(ring, half):
    return send(ring[:, :half], ACROSS), send(ring[:, half : 2 * half], ALONG)


def swap(parts):
    return tuple(send(p, CORE) for p in parts)


def total(*terms):
    out = terms[0].astype(f32)
    for t in terms[1:]:
        out = out + t.astype(f32)
    return out.astype(bf16)


def finish_kernel(kind, at_r, *refs):
    y, x = at_r[0], at_r[1]
    blocks, outs = refs[:4], refs[4:]
    for ab, turn, other_turn in ((0, x, y), (1, y, x)):
        one, two = (blocks[2 * ab + i][...].astype(f32) for i in range(2))
        left = jnp.where(turn == 0, one, two)
        right = jnp.where(turn == 0, two, one)
        both = jnp.concatenate([left, right], axis=1)
        if kind == "ffn":
            off = 0
            for out in outs[:2]:
                half = out.shape[0] // 2
                out[ab * half : (ab + 1) * half, :] = both[off : off + half]
                off += half
            half = outs[2].shape[0] // 2
            eighth = left.shape[1]
            for h, val in ((0, left), (1, right)):
                near, far = val[off : off + 2 * half], val[off + 2 * half : off + 4 * half]
                quarters = jnp.where(other_turn == 0, near, far), jnp.where(other_turn == 0, far, near)
                for i in range(4):
                    row, col = i % 2 * half, (4 * h + i) * eighth
                    outs[2][ab * half : (ab + 1) * half, col : col + eighth] = quarters[i // 2][row : row + half]
        else:
            half = outs[0].shape[0] // 2
            groups = outs[0].shape[1] // (3 * GW)
            for g in range(groups):
                for i in range(3):
                    col = (i * groups + g) * GW
                    outs[0][ab * half : (ab + 1) * half, col : col + GW] = both[g * half : (g + 1) * half, i * GW : (i + 1) * GW]
            if ab == 0:
                small = left[groups * half : groups * half + 16]
                piece = outs[1].shape[1]
                outs[1][...] = small[:2, :piece]
                for i in range(6):
                    outs[2 + i][...] = small[2 + i : 3 + i, :piece]
                outs[8][...] = jnp.concatenate([small[8 + i : 9 + i, :piece] for i in range(4)], axis=1)


def finish(at, kind, blocks, shapes):
    return pl.pallas_call(
        functools.partial(finish_kernel, kind),
        in_specs=[SMEM] + [VMEM] * len(blocks),
        out_specs=[VMEM] * len(shapes),
        out_shape=[jax.ShapeDtypeStruct(s, f32) for s in shapes],
        compiler_params=params(),
        cost_estimate=cost(0, 4_000_000),
        name="finish_" + kind,
    )(at, *blocks)


def pack(vectors, wide):
    block = jnp.concatenate([v.reshape(-1, vectors[1].shape[0]) for v in vectors] + [wide.reshape(4, -1)], axis=0)
    return jnp.pad(block, ((0, 16 - block.shape[0]), (0, 128 - block.shape[1])))


def whole_vectors(every, z, c, piece):
    k = lax.broadcasted_iota(jnp.int32, (2, 4, 8), 1)
    d = lax.broadcasted_iota(jnp.int32, (2, 4, 8), 0)
    s = lax.broadcasted_iota(jnp.int32, (2, 4, 8), 2)
    pick = (s == 2 * ((z - k) % 4) + (c + d) % 2).astype(bf16)
    table = jnp.einsum("dks,dkrl->srl", pick, every, preferred_element_type=f32).astype(bf16)
    table = table[:, :, :piece]
    wide = table[:, 8:12].reshape(1, -1)
    return table.transpose(1, 0, 2).reshape(16, -1), wide


class Sum:
    def __init__(self):
        self.own, self.got = [], []

    def add(self, own, other):
        self.own.append(own)
        self.got.append(send(other, CORE))

    def after(self, *values):
        self.got, self.far, self.parts, self.rest = tie((self.got, self.far, self.parts, self.rest), *values)

    far = parts = ()

    def pair(self, pick, *more):
        found = [total(pick(o), pick(g)) for o, g in zip(self.own, self.got)]
        found = found[0] if len(found) == 1 else jnp.concatenate(found, axis=-2)
        return total(found, *more) if more else found

    def halve(self):
        self.sent = self.pair(lambda a: a[0, 1]), self.pair(lambda a: a[1, 1])
        self.far = send(self.sent[0], ACROSS), send(self.sent[1], ALONG)

    def along_z(self):
        self.mine = [self.near(k) for k in range(4)]
        self.sent = self.mine[1:]
        self.far = ()
        self.parts = [send(self.mine[k], SHIFT[k]) for k in range(1, 4)]

    def joined(self, i):
        one, two, rows = self.sent[i], self.far[i], self.rows
        summed = total(one[:rows], two[:rows])
        return jnp.concatenate([summed, one[rows:], two[rows:]], axis=0)

    rest = ()

    def near(self, k):
        far = jnp.stack([f[k] for f in self.far])
        if self.rest:
            return total(jnp.stack([r[k] for r in self.rest]), far)
        return self.pair(lambda a: a[:, 0, k], far)

    def quarter(self):
        own, got, far = self.own[0], self.got[0], self.far
        part = lambda i, j: total(own[i, 0, j], got[i, 0, j], far[i][j])
        self.sent = part(0, 1), part(1, 1)
        self.rest = part(0, 0), part(1, 0)
        self.far = send(self.sent[0], ALONG), send(self.sent[1], ACROSS)

    def across(self, more=None):
        both = total(self.mine[0], *self.parts)
        rows = both.shape[1]
        if more is not None:
            extra = total(more.mine[0], *more.parts)
            both = jnp.concatenate([both, extra], axis=1)
        self.got = self.parts = ()
        self.sent = both[0], both[1]
        self.far = send(both[0], ALONG), send(both[1], ACROSS)
        self.rows = rows

    def share(self):
        a, b = (self.joined(i) for i in range(2))
        self.sent = a, b
        self.out = a, send(a, ACROSS), b, send(b, ALONG)


def shards_near(
    tokens,
    cotangent,
    qkv_weight,
    query_value_bias,
    out_weight,
    out_bias,
    norm_one_gain,
    norm_one_shift,
    up_weight,
    up_bias,
    down_weight,
    down_bias,
    norm_two_gain,
    norm_two_shift,
    segment_ids,
    valid,
):
    length = segment_ids.shape[1]
    width = tokens.shape[1]
    groups = width // GW
    ff = up_bias.shape[0] * 8
    piece = out_bias.shape[0]
    r, s = lax.axis_index("rep"), lax.axis_index("shard")
    y, x, z, c = r // 2, r % 2, s // 2, s % 2
    at = jnp.stack([y, x, z, c]).astype(jnp.int32)

    half = piece // 2
    block = pack(
        (query_value_bias, out_bias, norm_one_gain, norm_one_shift, down_bias, norm_two_gain, norm_two_shift), up_bias
    )
    lines = lambda n, cols: jnp.pad(block.reshape(n, -1), ((0, 8 - n), (0, cols - 2048 // n)))
    dr = down_weight.shape[0] // 2
    own_q = jnp.concatenate([qkv_weight, lines(1, 3 * width)], axis=0)
    own_d = jnp.concatenate([down_weight[:dr], out_weight[:half], down_weight[dr:], out_weight[half:]], axis=0)
    other_q, other_u, other_d = swap((own_q, up_weight, own_d))
    held = jnp.concatenate([halves(qkv_weight, x, y), lines(2, 3 * width // 2)], axis=0)
    ring = []
    for step in range(3):
        if step == 2:
            held = tie(held, other_q, other_u, other_d)
        held = send(held, SHIFT[1])
        ring.append(held)
    ring_q = jnp.stack(ring)
    far_q = spread_half(ring_q, half)
    first_u = lax.dynamic_slice(up_weight, (0, (2 * x + y) * (ff // 4)), (piece, ff // 4))
    first_u = tie(first_u, held)
    ring_u = [send(first_u, SHIFT[k]) for k in range(1, 4)]
    rest_q = swap(tie((ring_q,) + far_q, ring_u))
    swapped_q = rest_q[0]
    parts_q = (own_q, ring_q) + far_q + (other_q,) + rest_q
    (wqkv,) = assemble(
        functools.partial(assemble_half_kernel, [qkv_weight.shape[0]]), at, parts_q, [(width, 3 * width)]
    )
    blocks = lambda own, ring: jnp.concatenate([own[None, piece : piece + 1, :2048].reshape(1, 16, 128), ring[:, piece : piece + 2, :1024].reshape(3, 16, 128)])
    vecs, bu = whole_vectors(jnp.stack([blocks(own_q, ring_q), blocks(other_q, swapped_q)]), z, c, piece)

    aq, ak = masks(segment_ids, valid)
    ring_u = jnp.stack(tie(ring_u, far_q))
    first_d = tie(halves(own_d, x, y), ring_u)
    d2 = send(first_d, SHIFT[2])
    a, b = ring_u[:, :half], ring_u[:, half:]
    a2, b2 = send(a, ACROSS), send(b, ALONG)
    saved = [attend(0, tie(tokens, a, b, first_d), wqkv, vecs, aq, ak, length)]
    a2, b2, d2, first_d = tie((a2, b2, d2, first_d), saved[0][3])
    a3, b3 = jnp.stack([a, a2]), jnp.stack([b, b2])
    a4, b4 = send(a3, ALONG), send(b3, ACROSS)
    d1, d3 = send(first_d, SHIFT[1]), send(first_d, SHIFT[3])
    other_a = send(a3, CORE)
    saved.append(attend(1, tie(tokens, a3, b3, d2), wqkv, vecs, aq, ak, length))
    a4, b4, other_a, ring_d = tie((a4, b4, other_a, [d1, d2, d3]), saved[1][3])
    ring_d = jnp.stack(ring_d)
    ab4 = jnp.stack([a4, b4])
    far_d = spread_half(ring_d, dr + half)
    other_b, other_ab, other_ring = swap((b3, ab4, ring_d))
    saved.append(attend(2, tie(tokens, ring_d, ab4), wqkv, vecs, aq, ak, length))
    far_d, other_b, other_ab, other_ring = tie((far_d, other_b, other_ab, other_ring), saved[2][3])
    parts_u = (up_weight, a3, b3, ab4, other_u, other_a, other_b, other_ab)
    parts_d = (own_d, ring_d) + far_d + (other_d, other_ring) + swap(far_d)

    ctx = [f[3] for f in saved]
    result, low, hid, gd, gu, gb, gc, vec, bup = middle(
        at, tokens, ctx, cotangent, vecs, bu, parts_u + parts_d, (2 * dr, piece)
    )

    down, up, qkv = Sum(), Sum(), Sum()
    own, other = grad_down(at, ctx, gb, hid, gd)
    down.add(own, other)
    own, other = grad_up(at, *tie((low, gu), other))
    up.add(own, other)
    down.after(other)
    down.halve()
    own, other, dx, db0 = attend_back("first", 0, at, saved[0], tie(gc, down.sent, other), aq, ak, tokens, wqkv, gb, length)
    down.after(dx)
    up.after(dx)
    down.along_z()
    up.halve()
    dx = tie(dx, down.sent, up.sent)
    own, other, dx, db1 = attend_back("second", 1, at, saved[1], gc, aq, ak, tokens, wqkv, dx, length, (own, other))
    two = own, other
    up.after(dx)
    up.quarter()
    wide = bup[0].reshape(8, 4, piece).transpose(1, 0, 2).reshape(4, width)
    table = jnp.concatenate([vec[:6], wide, jnp.zeros((4, width), f32)], axis=0)
    own, other, dx, _ = attend_back(
        "third", 2, at, saved[2], gc, aq, ak, tokens, wqkv, tie(dx, up.sent), length, (db0, db1, table)
    )
    down.after(dx)
    up.after(dx)
    other, first_other = tie((other, two[1]), up.far)
    qkv.add(two[0], first_other)
    qkv.add(own, other)
    up.after(down.parts)
    up.along_z()
    qkv.halve()
    up.after(qkv.far)
    qkv.after(up.parts)
    qkv.along_z()
    down.across(up)
    down.share()
    dwd, dwo, dwu = finish(at, "ffn", down.out, [down_weight.shape, out_weight.shape, up_weight.shape])
    qkv.after(dwd, dwo, dwu)
    qkv.across()
    qkv.share()
    dwq, dqv, *ones, dbu = finish(at, "qkv", qkv.out, [qkv_weight.shape, (2, piece)] + 6 * [(1, piece)] + [(1, 4 * piece)])
    one = lambda i: ones[i - 2].reshape(piece)
    return (
        result,
        dx,
        dwq,
        dqv,
        dwo,
        one(2),
        one(3),
        one(4),
        dwu,
        dbu.reshape(-1),
        dwd,
        one(5),
        one(6),
        one(7),
    )


def spread(args):
    flat = [a.reshape(-1) for a in args]
    packed = jnp.concatenate(flat)
    every = lax.all_gather(packed, "shard", axis=0)
    out, at = [], 0
    for a in args:
        part = every[:, at : at + a.size].reshape((-1,) + a.shape)
        at += a.size
        out.append(jnp.moveaxis(part, 0, -2).reshape(a.shape[:-1] + (-1,)))
    return out


def shards(
    tokens,
    cotangent,
    qkv_weight,
    query_value_bias,
    out_weight,
    out_bias,
    norm_one_gain,
    norm_one_shift,
    up_weight,
    up_bias,
    down_weight,
    down_bias,
    norm_two_gain,
    norm_two_shift,
    segment_ids,
    valid,
):
    length = segment_ids.shape[1]
    width = tokens.shape[1]
    groups = width // GW
    gather = lambda a: lax.all_gather(a, "shard", axis=0, tiled=True)
    *rest, bu = spread(
        (query_value_bias, out_bias, norm_one_gain, norm_one_shift, down_bias, norm_two_gain, norm_two_shift, up_bias)
    )
    vecs = jnp.concatenate([v.reshape(-1, width) for v in rest] + [jnp.zeros((8, width), bf16)], axis=0)
    wqkv, wd, wo, wu = gather(qkv_weight), gather(down_weight), gather(out_weight), gather(up_weight)
    at = jnp.zeros((4,), jnp.int32)
    aq, ak = masks(segment_ids, valid)
    saved = [attend(g, tokens, wqkv, vecs, aq, ak, length) for g in range(groups)]
    ctx = [f[3] for f in saved]
    result, low, hid, gd, gu, gb, gc, vec, bup = middle(at, tokens, ctx, cotangent, vecs, bu[None], (wu, wd, wo))
    dwd = tn(hid, gd).astype(bf16)
    dwu = tn(low, gu).astype(bf16)
    dwo = tn(jnp.concatenate(ctx, axis=1), gb).astype(bf16)
    dx, dws, dbs = gb, [], []
    for g in range(groups):
        dw, dx, db = attend_back("plain", g, at, saved[g], gc, aq, ak, tokens, wqkv, dx, length)
        dws.append(dw)
        dbs.append(db)
    dwq = jnp.concatenate([dw[i] for i in range(3) for dw in dws], axis=1)
    db = jnp.stack(dbs).reshape(groups, 3, GW).transpose(1, 0, 2).reshape(3, width)
    small = jnp.concatenate([db[0], db[2], vec[:6].reshape(-1), bup[0]])
    small = lax.psum(small.reshape(-1, 128), ("rep", "shard")).reshape(-1)

    def owned(a):
        part = lax.psum_scatter(a, "shard", scatter_dimension=0, tiled=True)
        return lax.psum(part, "rep").astype(f32)

    rank = lax.axis_index("shard")
    own = lambda at, size: lax.dynamic_slice(small, (at + rank * size,), (size,))
    piece = out_bias.shape[0]
    vs = [own(width * i, piece) for i in range(8)]
    dbu = own(8 * width, up_bias.shape[0])
    gd_w, gu_w, go_w, gq_w = owned(dwd), owned(dwu), owned(dwo), owned(dwq)
    return result, dx, gq_w, jnp.stack(vs[:2]), go_w, vs[2], vs[3], vs[4], gu_w, dbu, gd_w, vs[5], vs[6], vs[7]


def solution(mesh):
    rows, one = P(("rep", "shard"), None), P("shard")
    mat, two = P("shard", None), P(None, "shard")
    near = mesh.shape["rep"] == 4 and mesh.shape["shard"] == 8
    return jax.shard_map(
        shards_near if near else shards,
        mesh=mesh,
        in_specs=(rows, rows, mat, two, mat, one, one, one, mat, one, mat, one, one, one, rows, rows),
        out_specs=(rows, rows, mat, two, mat, one, one, one, mat, one, mat, one, one, one),
        check_vma=False,
    )
```

```python
import functools

import jax
import jax.numpy as jnp
from jax import lax
from jax.experimental import pallas as pl
from jax.experimental.pallas import tpu as pltpu
from jax.sharding import PartitionSpec as P

HD = 64
GW = 256
SCALE = 0.125 * 1.4426950408889634
BIG = 1e30
VMEM_LIMIT = 60 * 1024 * 1024
bf16 = jnp.bfloat16
f32 = jnp.float32
SMEM = pl.BlockSpec(memory_space=pltpu.SMEM)
VMEM = pl.BlockSpec(memory_space=pltpu.VMEM)


def nn(a, b):
    return lax.dot_general(a, b, (((1,), (0,)), ((), ())), preferred_element_type=f32)


def nt(a, b):
    return lax.dot_general(a, b, (((1,), (1,)), ((), ())), preferred_element_type=f32)


def tn(a, b):
    return lax.dot_general(a, b, (((0,), (0,)), ((), ())), preferred_element_type=f32)


def params(**more):
    return pltpu.CompilerParams(vmem_limit_bytes=VMEM_LIMIT, **more)


def cost(flops, moved):
    return pl.CostEstimate(flops=flops, bytes_accessed=moved, transcendentals=0)


def attend_kernel(tok, wq, wk, wv, vecs, aq, ak, q_o, k_o, v_o, ctx_o, lse_o):
    x = tok[...]
    q = (nn(x, wq[...]) + vecs[0:1, :].astype(f32)).astype(bf16)
    k = nn(x, wk[...]).astype(bf16)
    v = (nn(x, wv[...]) + vecs[1:2, :].astype(f32)).astype(bf16)
    q_o[...] = q
    k_o[...] = k
    v_o[...] = v
    length, width = q.shape
    lane = lax.broadcasted_iota(jnp.int32, (length, width), 1) // HD
    slot = lax.broadcasted_iota(jnp.int32, (length, 128), 1)
    acc = None
    scale = jnp.zeros((length, width), f32)
    stat = jnp.zeros((length, 128), f32)
    for h in range(width // HD):
        mine = lane == h
        qa = jnp.where(mine, q, aq[...])
        ka = jnp.where(mine, k, ak[...])
        va = jnp.where(mine, v, jnp.zeros_like(v))
        t = nt(qa, ka) * SCALE
        m = jnp.max(t, axis=1, keepdims=True)
        p = jnp.exp2(t - m)
        total = jnp.sum(p, axis=1, keepdims=True)
        part = nn(p.astype(bf16), va)
        acc = part if acc is None else acc + part
        scale = jnp.where(mine, 1.0 / total, scale)
        stat = jnp.where(slot == h, m + jnp.log2(total), stat)
    ctx_o[...] = (acc * scale).astype(bf16)
    lse_o[0] = stat.T[:8]


def attend(g, tokens, w, vecs, aq, ak, length):
    rows, width = tokens.shape
    groups = width // GW
    seqs = rows // length
    col = lambda o: pl.BlockSpec((width, GW), lambda b: (0, o * groups + g))
    seq = pl.BlockSpec((length, width), lambda b: (b, 0))
    blk = pl.BlockSpec((length, GW), lambda b: (b, 0))
    act = jax.ShapeDtypeStruct((rows, GW), bf16)
    return pl.pallas_call(
        attend_kernel,
        grid=(seqs,),
        in_specs=[seq, col(0), col(1), col(2), pl.BlockSpec((16, GW), lambda b: (0, g)), blk, blk],
        out_specs=[blk, blk, blk, blk, pl.BlockSpec((1, 8, length), lambda b: (b, 0, 0))],
        out_shape=[act, act, act, act, jax.ShapeDtypeStruct((seqs, 8, length), f32)],
        compiler_params=params(),
        cost_estimate=cost(4_000_000_000, 5_000_000),
        name="attend",
    )(tokens, w, w, w, vecs, aq, ak)


def owners(at_r, own, other):
    for k in range(4):
        z = lax.rem(k + at_r[2], 4)
        for core, ref in ((at_r[3], own), (1 - at_r[3], other)):
            yield k, 2 * z + core, ref


def select_lanes(s, piece, width):
    i = lax.broadcasted_iota(jnp.int32, (128, width), 0)
    j = lax.broadcasted_iota(jnp.int32, (128, width), 1)
    return ((j == s * piece + i) & (i < piece)).astype(f32).astype(bf16)


def attend_back_kernel(mode, at_r, q_r, k_r, v_r, do_r, ctx_r, lse_r, aq, ak, tok, wq, wk, wv, dx_i, *rest):
    b = pl.program_id(0)
    last = b == pl.num_programs(0) - 1
    if mode == "plain":
        dw_o, dx_o, db_o, dw_s = rest
    elif mode == "first":
        own_o, other_o, dx_o, db_o, dw_s = rest
    elif mode == "second":
        _, _, own_o, other_o, dx_o, db_o, dw_s = rest
    else:
        db0, db1, tbl, own_o, other_o, dx_o, db_o, dw_s = rest
    q, k, v, do = q_r[...], k_r[...], v_r[...], do_r[...]
    length, width = q.shape
    lane = lax.broadcasted_iota(jnp.int32, (length, width), 1) // HD
    sel = lax.broadcasted_iota(jnp.int32, (8, width), 1) // HD == lax.broadcasted_iota(jnp.int32, (8, width), 0)
    sel = sel.astype(f32).astype(bf16)
    prod = do.astype(f32) * ctx_r[...].astype(f32)
    hi = prod.astype(bf16)
    lo = (prod - hi.astype(f32)).astype(bf16)
    delta = nt(sel, hi) + nt(sel, lo)
    dq = dk = dv = None
    zero = jnp.zeros_like(q)
    for h in range(width // HD):
        mine = lane == h
        qa = jnp.where(mine, q, aq[...])
        ka = jnp.where(mine, k, ak[...])
        va = jnp.where(mine, v, zero)
        p = jnp.exp2(nt(ka, qa) * SCALE - lse_r[0, h : h + 1, :])
        dp = nt(va, do)
        ds = (p * (dp - delta[h : h + 1, :])).astype(bf16)
        dv_h = nn(p.astype(bf16), jnp.where(mine, do, zero))
        dk_h = nn(ds, jnp.where(mine, q, zero))
        dq_h = tn(ds, jnp.where(mine, k, zero))
        dv = dv_h if dv is None else dv + dv_h
        dk = dk_h if dk is None else dk + dk_h
        dq = dq_h if dq is None else dq + dq_h
    dq = (dq * 0.125).astype(bf16)
    dk = (dk * 0.125).astype(bf16)
    dv = dv.astype(bf16)
    back = jnp.concatenate([dq, dk, dv], axis=1)
    dw = tn(tok[...], back)
    dx = nt(dq, wq[...]) + nt(dk, wk[...]) + nt(dv, wv[...])
    dx_o[...] = (dx_i[...].astype(f32) + dx).astype(dx_o.dtype)
    sums = jnp.sum(back.astype(f32), axis=0, keepdims=True)

    @pl.when(b == 0)
    def _():
        dw_s[...] = dw
        db_o[...] = sums

    @pl.when(b > 0)
    def _():
        dw_s[...] += dw
        db_o[...] += sums

    @pl.when(last)
    def _():
        if mode == "plain":
            for i in range(3):
                dw_o[i] = dw_s[:, i * width : (i + 1) * width].astype(bf16)
            return
        piece = dw_s.shape[0] // 8
        half, wide = piece // 2, dw_s.shape[1] // 2
        for k, s, ref in owners(at_r, own_o, other_o):
            for ab, turn in ((0, at_r[1]), (1, at_r[0])):
                row = pl.multiple_of(s * piece + ab * half, 16)
                for h in range(2):
                    val = dw_s[pl.ds(row, half), h * wide : (h + 1) * wide]
                    ref[ab, lax.rem(h + turn, 2), k, 0:half] = val.astype(bf16)

        if mode == "third":
            sums = [r[...] for r in (db0, db1, db_o)]
            dbq = jnp.concatenate([r[:, :width] for r in sums], axis=1)
            dbv = jnp.concatenate([r[:, 2 * width :] for r in sums], axis=1)
            table = jnp.concatenate([dbq, dbv, tbl[...]], axis=0).astype(bf16)
            extra = jnp.zeros((4, 16, wide), bf16)
            for ab in range(2):
                for h in range(2):
                    own_o[ab, h, :, half : half + 16, :] = extra
                    other_o[ab, h, :, half : half + 16, :] = extra
            for k, s, ref in owners(at_r, own_o, other_o):
                blk = nt(table, select_lanes(s, piece, table.shape[1])).astype(bf16)
                ref[0, at_r[1], k, half : half + 16, 0:128] = blk


def attend_back(mode, g, at, saved, gc, aq, ak, tokens, w, dx, length, extra=()):
    rows, width = tokens.shape
    groups = width // GW
    seqs = rows // length
    half = width // 16
    col = lambda o: pl.BlockSpec((width, GW), lambda b: (0, o * groups + g))
    seq = pl.BlockSpec((length, width), lambda b: (b, 0))
    blk = pl.BlockSpec((length, GW), lambda b: (b, 0))
    whole = lambda s: pl.BlockSpec(s, lambda b: (0,) * len(s))
    S = jax.ShapeDtypeStruct
    tall = {"first": 2 * half, "second": 2 * half, "third": half + 16, "plain": 0}[mode]
    at_row = 1 if mode == "second" else 0
    block = half + 16 if mode == "third" else half
    part = pl.BlockSpec((2, 2, 4, block, 3 * GW // 2), lambda b: (0, 0, 0, at_row, 0))
    if mode == "plain":
        out_specs, out_shape = [whole((3, width, GW))], [S((3, width, GW), bf16)]
    else:
        out_specs, out_shape = [part, part], [S((2, 2, 4, tall, 3 * GW // 2), bf16)] * 2
    out_specs += [seq, whole((1, 3 * GW))]
    out_shape += [S((rows, width), bf16 if mode == "third" or g == groups - 1 else f32), S((1, 3 * GW), f32)]
    in_specs = [SMEM, blk, blk, blk, pl.BlockSpec((length, GW), lambda b: (b, g)), blk]
    in_specs += [pl.BlockSpec((1, 8, length), lambda b: (b, 0, 0)), blk, blk, seq, col(0), col(1), col(2), seq]
    aliases = {}
    if mode == "second":
        in_specs += [pl.BlockSpec(memory_space=pl.ANY)] * 2
        aliases = {len(in_specs) - 2: 0, len(in_specs) - 1: 1}
    elif mode == "third":
        in_specs += [whole(e.shape) for e in extra]
    q, k, v, ctx, lse = saved
    return pl.pallas_call(
        functools.partial(attend_back_kernel, mode),
        grid=(seqs,),
        in_specs=in_specs,
        out_specs=out_specs,
        out_shape=out_shape,
        scratch_shapes=[pltpu.VMEM((width, 3 * GW), f32)],
        input_output_aliases=aliases,
        compiler_params=params(),
        cost_estimate=cost(8_000_000_000, 8_000_000),
        name="attend_back",
    )(at, q, k, v, gc, ctx, lse, aq, ak, tokens, w, w, w, dx, *extra)


def masks(segment_ids, valid):
    code = (segment_ids + 8 * valid).reshape(-1, 1)
    lane = lax.broadcasted_iota(jnp.int32, (1, GW), 1) % HD
    same = code == lane
    aq = same.astype(bf16)
    ak = jnp.where((lane < 16) & ~same, -BIG, 0.0).astype(bf16)
    return aq, ak


def phi(x):
    return 0.5 * (1.0 + lax.erf(x * 0.7071067811865476)), jnp.exp(-0.5 * x * x) * 0.3989422804014327


def middle_kernel(groups, split, at_r, tok, *refs):
    ctx_r = refs[:groups]
    cot, vecs, bu = refs[groups : groups + 3]
    refs = refs[groups + 3 :]
    i = pl.program_id(0)
    if split:
        up_parts, down_parts, refs = refs[:8], refs[8:16], refs[16:]
        wu, wd, wo = refs[-3:]
        refs = refs[:-3]

        @pl.when(i == 0)
        def _():
            assemble_quarter_kernel(at_r, *up_parts, wu)
            assemble_half_kernel(split, at_r, *down_parts, wd, wo)

    else:
        wu, wd, wo, refs = *refs[:3], refs[3:]
    out_o, low_o, hid_o, gd_o, gu_o, gb_o, gc_o, vec_o, bup_o, slope = refs
    width = tok.shape[1]
    ff = bu.shape[1]
    step = width
    chunks = ff // step
    bo, g1, s1, bd, g2, s2 = (vecs[j : j + 1, :].astype(f32) for j in range(2, 8))
    ctx = jnp.concatenate([r[...] for r in ctx_r], axis=1)
    pre = tok[...].astype(f32) + nn(ctx, wo[...]) + bo
    mean = lambda v: jnp.mean(v, axis=1, keepdims=True)
    centre = pre - mean(pre)
    r1 = lax.rsqrt(mean(centre * centre) + 1e-05)
    n1 = centre * r1
    normed = n1 * g1 + s1
    low = normed.astype(bf16)
    low_o[...] = low
    acc = normed + bd
    for c in range(chunks):
        cols = slice(c * step, (c + 1) * step)
        hp = nn(low, wu[:, cols]) + bu[:, cols].astype(f32)
        cdf, pdf = phi(hp)
        slope[:, cols] = cdf + hp * pdf
        hid = (hp * cdf).astype(bf16)
        hid_o[:, cols] = hid
        acc = acc + nn(hid, wd[cols, :])
    centre = acc - mean(acc)
    r2 = lax.rsqrt(mean(centre * centre) + 1e-05)
    n2 = centre * r2
    out_o[...] = (n2 * g2 + s2).astype(bf16)
    ct = cot[...].astype(f32)
    e = ct * g2
    gp2 = r2 * (e - mean(e) - n2 * mean(e * n2))
    gd = gp2.astype(bf16)
    gd_o[...] = gd
    acc = gp2
    total = lambda v: jnp.sum(v, axis=0, keepdims=True)

    def put(ref, at, v):
        @pl.when(i == 0)
        def _():
            ref[at] = v

        @pl.when(i > 0)
        def _():
            ref[at] += v

    for c in range(chunks):
        cols = slice(c * step, (c + 1) * step)
        gu = (nt(gd, wd[cols, :]) * slope[:, cols]).astype(bf16)
        gu_o[:, cols] = gu
        put(bup_o, (slice(0, 1), cols), total(gu.astype(f32)))
        acc = acc + nt(gu, wu[:, cols])
    e = acc * g1
    gp1 = r1 * (e - mean(e) - n1 * mean(e * n1))
    gb = gp1.astype(bf16)
    gb_o[...] = gb
    gc_o[...] = nt(gb, wo[...]).astype(bf16)
    for at, v in enumerate((gb.astype(f32), acc * n1, acc, gd.astype(f32), ct * n2, ct)):
        put(vec_o, (slice(at, at + 1), slice(None)), total(v))


def middle(at, tokens, ctx, cot, vecs, bu, weights, split=None, tile=256):
    rows, width = tokens.shape
    ff = bu.shape[1]
    act = pl.BlockSpec((tile, width), lambda i: (i, 0))
    wide = pl.BlockSpec((tile, ff), lambda i: (i, 0))
    whole = lambda a: pl.BlockSpec(a.shape, lambda i: (0,) * a.ndim, pipeline_mode=pl.Buffered(1))
    S = jax.ShapeDtypeStruct
    shapes = [(rows, width), (rows, width), (rows, ff), (rows, width), (rows, ff), (rows, width), (rows, width)]
    scratch = [pltpu.VMEM((tile, ff), f32)]
    if split:
        scratch += [pltpu.VMEM(s, bf16) for s in ((width, ff), (ff, width), (width, width))]
    blocks = [pl.BlockSpec((tile, GW), lambda i: (i, 0)) for _ in ctx]
    return pl.pallas_call(
        functools.partial(middle_kernel, len(ctx), split),
        grid=(rows // tile,),
        in_specs=[SMEM, act] + blocks + [act] + [whole(a) for a in (vecs, bu) + weights],
        out_specs=[act, act, wide, act, wide, act, act, pl.BlockSpec((8, width), lambda i: (0, 0)), pl.BlockSpec((8, ff), lambda i: (0, 0))],
        out_shape=[S(s, bf16) for s in shapes] + [S((8, width), f32), S((8, ff), f32)],
        scratch_shapes=scratch,
        compiler_params=params(),
        cost_estimate=cost(30_000_000_000, 40_000_000),
        name="middle",
    )(at, tokens, *ctx, cot, vecs, bu, *weights)


def grad_down_kernel(groups, at_r, *refs):
    ctx = refs[:groups]
    gb, hid, gd, own_o, other_o, res_s = refs[groups:]
    p = pl.program_id(0)
    turns = ((0, at_r[1]), (1, at_r[0]))
    wide = gd.shape[1] // 2
    tall = hid.shape[1] // 2

    @pl.when(p == 0)
    def _():
        lhs = jnp.concatenate([r[...] for r in ctx], axis=1)
        res_s[...] = tn(lhs, gb[...]).astype(bf16)
        piece = res_s.shape[0] // 8
        half = piece // 2
        for k, s, ref in owners(at_r, own_o, other_o):
            for ab, turn in turns:
                row = pl.multiple_of(s * piece + ab * half, 16)
                for h in range(2):
                    ref[ab, lax.rem(h + turn, 2), k, tall : tall + half] = res_s[pl.ds(row, half), h * wide : (h + 1) * wide]

    @pl.when(p > 0)
    def _():
        res = tn(hid[...], gd[...]).astype(bf16)
        kk = lax.rem(p - 1, 4)
        for ab, turn in turns:
            for h in range(2):
                val = res[ab * tall : (ab + 1) * tall, h * wide : (h + 1) * wide]
                rel = lax.rem(h + turn, 2)
                for ref, cond in ((other_o, p < 5), (own_o, p >= 5)):

                    @pl.when(cond)
                    def _(val=val, rel=rel, ab=ab, ref=ref):
                        ref[ab, rel, kk, 0:tall] = val


def grad_down(at, ctx, gb, hid, gd):
    rows, ff = hid.shape
    width = gd.shape[1]
    piece = ff // 8
    part = (2, 2, 4, (piece + width // 8) // 2, width // 2)

    def owner(p, at_r):
        j = jnp.maximum(p - 1, 0)
        z = lax.rem(at_r[2] + lax.rem(j, 4), 4)
        return 0, 2 * z + jnp.where(j < 4, 1 - at_r[3], at_r[3])

    whole = lambda s: pl.BlockSpec(s, lambda p, at_r: (0,) * len(s))
    return pl.pallas_call(
        functools.partial(grad_down_kernel, len(ctx)),
        grid_spec=pltpu.PrefetchScalarGridSpec(
            num_scalar_prefetch=1,
            grid=(9,),
            in_specs=[whole(c.shape) for c in ctx] + [whole(gb.shape), pl.BlockSpec((rows, piece), owner), whole(gd.shape)],
            out_specs=[whole(part), whole(part)],
            scratch_shapes=[pltpu.VMEM((width, width), bf16)],
        ),
        out_shape=[jax.ShapeDtypeStruct(part, bf16)] * 2,
        compiler_params=params(),
        cost_estimate=cost(9_000_000_000, 14_000_000),
        name="grad_down",
    )(at, *ctx, gb, hid, gd)


def grad_up_kernel(at_r, low, gu, own_o, other_o, turned, res_s):
    j = pl.program_id(0)
    y, x = at_r[0], at_r[1]

    @pl.when(j == 0)
    def _():
        turned[...] = low[...].T

    res_s[...] = nn(turned[...], gu[...]).astype(bf16)
    piece = res_s.shape[0] // 8
    half = piece // 2
    h, l = j // 4, lax.rem(j // 2, 2)
    to = pl.multiple_of(lax.rem(j, 2) * half, 16)
    for k, s, ref in owners(at_r, own_o, other_o):
        for ab, turn, other_turn in ((0, x, y), (1, y, x)):
            row = pl.multiple_of(s * piece + ab * half, 16)
            one, two = lax.rem(h + turn, 2), lax.rem(l + other_turn, 2)
            ref[ab, one, two, k, pl.ds(to, half), :] = res_s[pl.ds(row, half), :]


def grad_up(at, low, gu):
    rows, width = low.shape
    ff = gu.shape[1]
    step = ff // 8
    part = (2, 2, 2, 4, width // 8, ff // 8)
    whole = pl.BlockSpec(part, lambda j: (0, 0, 0, 0, 0, 0))
    return pl.pallas_call(
        grad_up_kernel,
        grid=(8,),
        in_specs=[SMEM, pl.BlockSpec((rows, width), lambda j: (0, 0)), pl.BlockSpec((rows, step), lambda j: (0, j))],
        out_specs=[whole, whole],
        out_shape=[jax.ShapeDtypeStruct(part, bf16)] * 2,
        scratch_shapes=[pltpu.VMEM((width, rows), bf16), pltpu.VMEM((width, step), bf16)],
        compiler_params=params(),
        cost_estimate=cost(9_000_000_000, 14_000_000),
        name="grad_up",
    )(at, low, gu)


AXES = ("rep", "shard")


def pairs(move):
    found = []
    for y in range(2):
        for x in range(2):
            for z in range(4):
                for c in range(2):
                    j, i, k, d = move(y, x, z, c)
                    found.append(((y * 2 + x) * 8 + z * 2 + c, (j * 2 + i) * 8 + k * 2 + d))
    return found


CORE = pairs(lambda y, x, z, c: (y, x, z, 1 - c))
ACROSS = pairs(lambda y, x, z, c: (y, 1 - x, z, c))
ALONG = pairs(lambda y, x, z, c: (1 - y, x, z, c))
SHIFT = [None] + [pairs(lambda y, x, z, c, n=n: (y, x, (z + n) % 4, c)) for n in (1, 2, 3)]


def send(a, where):
    return lax.ppermute(a, AXES, where)


def tie(values, *after):
    flat, tree = jax.tree.flatten(values)
    return jax.tree.unflatten(tree, lax.optimization_barrier(tuple(flat) + tuple(jax.tree.leaves(after)))[: len(flat)])


def place(own, received, at_r, rows, out, base, quarter):
    y, x, z = at_r[0], at_r[1], at_r[2]
    cols = out.shape[1]
    half = rows // 2
    out[pl.ds(pl.multiple_of(base(z), 16), rows), :] = own
    for k in range(1, 4):
        start = base(lax.rem(z - k + 4, 4))
        for ab in range(2):
            at = pl.ds(pl.multiple_of(start + ab * half, 16), half)
            if quarter:
                wide = cols // 4
                for i in range(2):
                    for l in range(2):
                        one, two = (i, l) if ab == 0 else (l, i)
                        col = (lax.rem(x + i, 2) * 2 + lax.rem(y + l, 2)) * wide
                        out[at, pl.ds(pl.multiple_of(col, 128), wide)] = received(ab, one, two, k)
            else:
                wide = cols // 2
                for one in range(2):
                    col = lax.rem((x, y)[ab] + one, 2) * wide
                    out[at, pl.ds(pl.multiple_of(col, 128), wide)] = received(ab, one, 0, k)


def assemble_half_kernel(out_rows, at_r, *refs):
    n = len(out_rows)
    outs = refs[-n:]
    c = at_r[3]
    for turn, (own, ring, far_x, far_y) in ((c, refs[:4]), (1 - c, refs[4:8])):
        off = 0
        total_half = sum(out_rows) // 2
        for out, rows in zip(outs, out_rows):
            half = rows // 2

            def received(ab, one, two, k):
                if one == 0:
                    return ring[k - 1, ab * total_half + off : ab * total_half + off + half, :]
                return (far_x, far_y)[ab][k - 1, off : off + half, :]

            whole = jnp.concatenate([own[off : off + half], own[total_half + off : total_half + off + half]], axis=0)
            place(whole, received, at_r, rows, out, lambda z: (2 * z + turn) * rows, False)
            off += half


def assemble_quarter_kernel(at_r, *refs):
    out = refs[-1]
    c = at_r[3]
    for turn, (own, near_a, near_b, far) in ((c, refs[:4]), (1 - c, refs[4:8])):
        rows = own.shape[0]

        def received(ab, one, two, k):
            if two == 1:
                return far[ab, one, k - 1]
            return (near_a, near_b)[ab][one, k - 1]

        place(own[...], received, at_r, rows, out, lambda z: (2 * z + turn) * rows, True)


def assemble(kernel, at, parts, shapes):
    return pl.pallas_call(
        kernel,
        in_specs=[SMEM] + [VMEM] * len(parts),
        out_specs=[VMEM] * len(shapes),
        out_shape=[jax.ShapeDtypeStruct(s, bf16) for s in shapes],
        compiler_params=params(),
        cost_estimate=cost(0, sum(4 * s[0] * s[1] for s in shapes)),
        name="assemble",
    )(at, *parts)


def halves(w, x, y):
    half, wide = w.shape[0] // 2, w.shape[1] // 2
    a = lax.dynamic_slice(w, (0, x * wide), (half, wide))
    b = lax.dynamic_slice(w, (half, y * wide), (half, wide))
    return jnp.concatenate([a, b], axis=0)


def spread_half(ring, half):
    return send(ring[:, :half], ACROSS), send(ring[:, half : 2 * half], ALONG)


def swap(parts):
    return tuple(send(p, CORE) for p in parts)


def total(*terms):
    out = terms[0].astype(f32)
    for t in terms[1:]:
        out = out + t.astype(f32)
    return out.astype(bf16)


def finish_kernel(kind, at_r, *refs):
    y, x = at_r[0], at_r[1]
    blocks, outs = refs[:4], refs[4:]
    for ab, turn, other_turn in ((0, x, y), (1, y, x)):
        one, two = (blocks[2 * ab + i][...].astype(f32) for i in range(2))
        left = jnp.where(turn == 0, one, two)
        right = jnp.where(turn == 0, two, one)
        both = jnp.concatenate([left, right], axis=1)
        if kind == "ffn":
            off = 0
            for out in outs[:2]:
                half = out.shape[0] // 2
                out[ab * half : (ab + 1) * half, :] = both[off : off + half]
                off += half
            half = outs[2].shape[0] // 2
            eighth = left.shape[1]
            for h, val in ((0, left), (1, right)):
                near, far = val[off : off + 2 * half], val[off + 2 * half : off + 4 * half]
                quarters = jnp.where(other_turn == 0, near, far), jnp.where(other_turn == 0, far, near)
                for i in range(4):
                    row, col = i % 2 * half, (4 * h + i) * eighth
                    outs[2][ab * half : (ab + 1) * half, col : col + eighth] = quarters[i // 2][row : row + half]
        else:
            half = outs[0].shape[0] // 2
            groups = outs[0].shape[1] // (3 * GW)
            for g in range(groups):
                for i in range(3):
                    col = (i * groups + g) * GW
                    outs[0][ab * half : (ab + 1) * half, col : col + GW] = both[g * half : (g + 1) * half, i * GW : (i + 1) * GW]
            if ab == 0:
                small = left[groups * half : groups * half + 16]
                piece = outs[1].shape[1]
                outs[1][...] = small[:2, :piece]
                for i in range(6):
                    outs[2 + i][...] = small[2 + i : 3 + i, :piece]
                outs[8][...] = jnp.concatenate([small[8 + i : 9 + i, :piece] for i in range(4)], axis=1)


def finish(at, kind, blocks, shapes):
    return pl.pallas_call(
        functools.partial(finish_kernel, kind),
        in_specs=[SMEM] + [VMEM] * len(blocks),
        out_specs=[VMEM] * len(shapes),
        out_shape=[jax.ShapeDtypeStruct(s, f32) for s in shapes],
        compiler_params=params(),
        cost_estimate=cost(0, 4_000_000),
        name="finish_" + kind,
    )(at, *blocks)


def pack(vectors, wide):
    block = jnp.concatenate([v.reshape(-1, vectors[1].shape[0]) for v in vectors] + [wide.reshape(4, -1)], axis=0)
    return jnp.pad(block, ((0, 16 - block.shape[0]), (0, 128 - block.shape[1])))


def whole_vectors(every, z, c, piece):
    k = lax.broadcasted_iota(jnp.int32, (2, 4, 8), 1)
    d = lax.broadcasted_iota(jnp.int32, (2, 4, 8), 0)
    s = lax.broadcasted_iota(jnp.int32, (2, 4, 8), 2)
    pick = (s == 2 * ((z - k) % 4) + (c + d) % 2).astype(bf16)
    table = jnp.einsum("dks,dkrl->srl", pick, every, preferred_element_type=f32).astype(bf16)
    table = table[:, :, :piece]
    wide = table[:, 8:12].reshape(1, -1)
    return table.transpose(1, 0, 2).reshape(16, -1), wide


class Sum:
    def __init__(self):
        self.own, self.got = [], []

    def add(self, own, other):
        self.own.append(own)
        self.got.append(send(other, CORE))

    def after(self, *values):
        self.got, self.far, self.parts, self.rest = tie((self.got, self.far, self.parts, self.rest), *values)

    far = parts = ()

    def pair(self, pick, *more):
        found = [total(pick(o), pick(g)) for o, g in zip(self.own, self.got)]
        found = found[0] if len(found) == 1 else jnp.concatenate(found, axis=-2)
        return total(found, *more) if more else found

    def halve(self):
        self.sent = self.pair(lambda a: a[0, 1]), self.pair(lambda a: a[1, 1])
        self.far = send(self.sent[0], ACROSS), send(self.sent[1], ALONG)

    def along_z(self):
        self.mine = [jnp.stack([self.near(i, k) for i in range(2)]) for k in range(4)]
        self.sent = self.mine[1:]
        self.far = ()
        self.parts = [send(self.mine[k], SHIFT[k]) for k in range(1, 4)]

    def joined(self, i):
        one, two, rows = self.sent[i], self.far[i], self.rows
        summed = total(one[:rows], two[:rows])
        return jnp.concatenate([summed, one[rows:], two[rows:]], axis=0)

    rest = ()

    def near(self, i, k):
        if self.rest:
            return total(self.rest[i][k], self.far[i][k])
        terms = []
        at = 0
        for o, g in zip(self.own, self.got):
            rows = o.shape[3]
            terms.append(total(o[i, 0, k], g[i, 0, k], self.far[i][k, at : at + rows]))
            at += rows
        return terms[0] if len(terms) == 1 else jnp.concatenate(terms, axis=0)

    def quarter(self):
        own, got, far = self.own[0], self.got[0], self.far
        part = lambda i, j: total(own[i, 0, j], got[i, 0, j], far[i][j])
        self.sent = part(0, 1), part(1, 1)
        self.rest = part(0, 0), part(1, 0)
        self.far = send(self.sent[0], ALONG), send(self.sent[1], ACROSS)

    def across(self, more=None):
        both = total(self.mine[0], *self.parts)
        rows = both.shape[1]
        if more is not None:
            extra = total(more.mine[0], *more.parts)
            both = jnp.concatenate([both, extra], axis=1)
        self.got = self.parts = ()
        self.sent = both[0], both[1]
        self.far = send(both[0], ALONG), send(both[1], ACROSS)
        self.rows = rows

    def share(self):
        a, b = (self.joined(i) for i in range(2))
        self.sent = a, b
        self.out = a, send(a, ACROSS), b, send(b, ALONG)


def shards_near(
    tokens,
    cotangent,
    qkv_weight,
    query_value_bias,
    out_weight,
    out_bias,
    norm_one_gain,
    norm_one_shift,
    up_weight,
    up_bias,
    down_weight,
    down_bias,
    norm_two_gain,
    norm_two_shift,
    segment_ids,
    valid,
):
    length = segment_ids.shape[1]
    width = tokens.shape[1]
    groups = width // GW
    ff = up_bias.shape[0] * 8
    piece = out_bias.shape[0]
    r, s = lax.axis_index("rep"), lax.axis_index("shard")
    y, x, z, c = r // 2, r % 2, s // 2, s % 2
    at = jnp.stack([y, x, z, c]).astype(jnp.int32)

    half = piece // 2
    block = pack(
        (query_value_bias, out_bias, norm_one_gain, norm_one_shift, down_bias, norm_two_gain, norm_two_shift), up_bias
    )
    lines = lambda n, cols: jnp.pad(block.reshape(n, -1), ((0, 8 - n), (0, cols - 2048 // n)))
    dr = down_weight.shape[0] // 2
    own_q = jnp.concatenate([qkv_weight, lines(1, 3 * width)], axis=0)
    own_d = jnp.concatenate([down_weight[:dr], out_weight[:half], down_weight[dr:], out_weight[half:]], axis=0)
    other_q, other_u, other_d = swap((own_q, up_weight, own_d))
    held = jnp.concatenate([halves(qkv_weight, x, y), lines(2, 3 * width // 2)], axis=0)
    ring = []
    for step in range(3):
        if step == 2:
            held = tie(held, other_q, other_u, other_d)
        held = send(held, SHIFT[1])
        ring.append(held)
    ring_q = jnp.stack(ring)
    far_q = spread_half(ring_q, half)
    first_u = lax.dynamic_slice(up_weight, (0, (2 * x + y) * (ff // 4)), (piece, ff // 4))
    first_u = tie(first_u, held)
    ring_u = [send(first_u, SHIFT[k]) for k in range(1, 4)]
    rest_q = swap(tie((ring_q,) + far_q, ring_u))
    swapped_q = rest_q[0]
    parts_q = (own_q, ring_q) + far_q + (other_q,) + rest_q
    (wqkv,) = assemble(
        functools.partial(assemble_half_kernel, [qkv_weight.shape[0]]), at, parts_q, [(width, 3 * width)]
    )
    blocks = lambda own, ring: jnp.concatenate([own[None, piece : piece + 1, :2048].reshape(1, 16, 128), ring[:, piece : piece + 2, :1024].reshape(3, 16, 128)])
    vecs, bu = whole_vectors(jnp.stack([blocks(own_q, ring_q), blocks(other_q, swapped_q)]), z, c, piece)

    aq, ak = masks(segment_ids, valid)
    ring_u = jnp.stack(tie(ring_u, far_q))
    first_d = tie(halves(own_d, x, y), ring_u)
    d2 = send(first_d, SHIFT[2])
    a, b = ring_u[:, :half], ring_u[:, half:]
    a2, b2 = send(a, ACROSS), send(b, ALONG)
    saved = [attend(0, tie(tokens, a, b, first_d), wqkv, vecs, aq, ak, length)]
    a2, b2, d2, first_d = tie((a2, b2, d2, first_d), saved[0][3])
    a3, b3 = jnp.stack([a, a2]), jnp.stack([b, b2])
    a4, b4 = send(a3, ALONG), send(b3, ACROSS)
    d1, d3 = send(first_d, SHIFT[1]), send(first_d, SHIFT[3])
    other_a = send(a3, CORE)
    saved.append(attend(1, tie(tokens, a3, b3, d2), wqkv, vecs, aq, ak, length))
    a4, b4, other_a, ring_d = tie((a4, b4, other_a, [d1, d2, d3]), saved[1][3])
    ring_d = jnp.stack(ring_d)
    ab4 = jnp.stack([a4, b4])
    far_d = spread_half(ring_d, dr + half)
    other_b, other_ab, other_ring = swap((b3, ab4, ring_d))
    saved.append(attend(2, tie(tokens, ring_d, ab4), wqkv, vecs, aq, ak, length))
    far_d, other_b, other_ab, other_ring = tie((far_d, other_b, other_ab, other_ring), saved[2][3])
    parts_u = (up_weight, a3, b3, ab4, other_u, other_a, other_b, other_ab)
    parts_d = (own_d, ring_d) + far_d + (other_d, other_ring) + swap(far_d)

    ctx = [f[3] for f in saved]
    result, low, hid, gd, gu, gb, gc, vec, bup = middle(
        at, tokens, ctx, cotangent, vecs, bu, parts_u + parts_d, (2 * dr, piece)
    )

    down, up, qkv = Sum(), Sum(), Sum()
    own, other = grad_down(at, ctx, gb, hid, gd)
    down.add(own, other)
    own, other = grad_up(at, *tie((low, gu), other))
    up.add(own, other)
    down.after(other)
    down.halve()
    own, other, dx, db0 = attend_back("first", 0, at, saved[0], tie(gc, down.sent, other), aq, ak, tokens, wqkv, gb, length)
    down.after(dx)
    up.after(dx)
    down.along_z()
    up.halve()
    dx = tie(dx, down.sent, up.sent)
    own, other, dx, db1 = attend_back("second", 1, at, saved[1], gc, aq, ak, tokens, wqkv, dx, length, (own, other))
    two = own, other
    up.after(dx)
    up.quarter()
    wide = bup[0].reshape(8, 4, piece).transpose(1, 0, 2).reshape(4, width)
    table = jnp.concatenate([vec[:6], wide, jnp.zeros((4, width), f32)], axis=0)
    own, other, dx, _ = attend_back(
        "third", 2, at, saved[2], gc, aq, ak, tokens, wqkv, tie(dx, up.sent), length, (db0, db1, table)
    )
    down.after(dx)
    up.after(dx)
    other, first_other = tie((other, two[1]), up.far)
    qkv.add(two[0], first_other)
    qkv.add(own, other)
    up.after(down.parts)
    up.along_z()
    qkv.halve()
    up.after(qkv.far)
    qkv.after(up.parts)
    qkv.along_z()
    down.across(up)
    down.share()
    dwd, dwo, dwu = finish(at, "ffn", down.out, [down_weight.shape, out_weight.shape, up_weight.shape])
    qkv.after(dwd, dwo, dwu)
    qkv.across()
    qkv.share()
    dwq, dqv, *ones, dbu = finish(at, "qkv", qkv.out, [qkv_weight.shape, (2, piece)] + 6 * [(1, piece)] + [(1, 4 * piece)])
    one = lambda i: ones[i - 2].reshape(piece)
    return (
        result,
        dx,
        dwq,
        dqv,
        dwo,
        one(2),
        one(3),
        one(4),
        dwu,
        dbu.reshape(-1),
        dwd,
        one(5),
        one(6),
        one(7),
    )


def spread(args):
    flat = [a.reshape(-1) for a in args]
    packed = jnp.concatenate(flat)
    every = lax.all_gather(packed, "shard", axis=0)
    out, at = [], 0
    for a in args:
        part = every[:, at : at + a.size].reshape((-1,) + a.shape)
        at += a.size
        out.append(jnp.moveaxis(part, 0, -2).reshape(a.shape[:-1] + (-1,)))
    return out


def shards(
    tokens,
    cotangent,
    qkv_weight,
    query_value_bias,
    out_weight,
    out_bias,
    norm_one_gain,
    norm_one_shift,
    up_weight,
    up_bias,
    down_weight,
    down_bias,
    norm_two_gain,
    norm_two_shift,
    segment_ids,
    valid,
):
    length = segment_ids.shape[1]
    width = tokens.shape[1]
    groups = width // GW
    gather = lambda a: lax.all_gather(a, "shard", axis=0, tiled=True)
    *rest, bu = spread(
        (query_value_bias, out_bias, norm_one_gain, norm_one_shift, down_bias, norm_two_gain, norm_two_shift, up_bias)
    )
    vecs = jnp.concatenate([v.reshape(-1, width) for v in rest] + [jnp.zeros((8, width), bf16)], axis=0)
    wqkv, wd, wo, wu = gather(qkv_weight), gather(down_weight), gather(out_weight), gather(up_weight)
    at = jnp.zeros((4,), jnp.int32)
    aq, ak = masks(segment_ids, valid)
    saved = [attend(g, tokens, wqkv, vecs, aq, ak, length) for g in range(groups)]
    ctx = [f[3] for f in saved]
    result, low, hid, gd, gu, gb, gc, vec, bup = middle(at, tokens, ctx, cotangent, vecs, bu[None], (wu, wd, wo))
    dwd = tn(hid, gd).astype(bf16)
    dwu = tn(low, gu).astype(bf16)
    dwo = tn(jnp.concatenate(ctx, axis=1), gb).astype(bf16)
    dx, dws, dbs = gb, [], []
    for g in range(groups):
        dw, dx, db = attend_back("plain", g, at, saved[g], gc, aq, ak, tokens, wqkv, dx, length)
        dws.append(dw)
        dbs.append(db)
    dwq = jnp.concatenate([dw[i] for i in range(3) for dw in dws], axis=1)
    db = jnp.stack(dbs).reshape(groups, 3, GW).transpose(1, 0, 2).reshape(3, width)
    small = jnp.concatenate([db[0], db[2], vec[:6].reshape(-1), bup[0]])
    small = lax.psum(small.reshape(-1, 128), ("rep", "shard")).reshape(-1)

    def owned(a):
        part = lax.psum_scatter(a, "shard", scatter_dimension=0, tiled=True)
        return lax.psum(part, "rep").astype(f32)

    rank = lax.axis_index("shard")
    own = lambda at, size: lax.dynamic_slice(small, (at + rank * size,), (size,))
    piece = out_bias.shape[0]
    vs = [own(width * i, piece) for i in range(8)]
    dbu = own(8 * width, up_bias.shape[0])
    gd_w, gu_w, go_w, gq_w = owned(dwd), owned(dwu), owned(dwo), owned(dwq)
    return result, dx, gq_w, jnp.stack(vs[:2]), go_w, vs[2], vs[3], vs[4], gu_w, dbu, gd_w, vs[5], vs[6], vs[7]


def solution(mesh):
    rows, one = P(("rep", "shard"), None), P("shard")
    mat, two = P("shard", None), P(None, "shard")
    near = mesh.shape["rep"] == 4 and mesh.shape["shard"] == 8
    return jax.shard_map(
        shards_near if near else shards,
        mesh=mesh,
        in_specs=(rows, rows, mat, two, mat, one, one, one, mat, one, mat, one, one, one, rows, rows),
        out_specs=(rows, rows, mat, two, mat, one, one, one, mat, one, mat, one, one, one),
        check_vma=False,
    )
```

```python
import functools

import jax
import jax.numpy as jnp
from jax import lax
from jax.experimental import pallas as pl
from jax.experimental.pallas import tpu as pltpu
from jax.sharding import PartitionSpec as P

HD = 64
GW = 256
SCALE = 0.125 * 1.4426950408889634
BIG = 1e30
VMEM_LIMIT = 60 * 1024 * 1024
bf16 = jnp.bfloat16
f32 = jnp.float32
SMEM = pl.BlockSpec(memory_space=pltpu.SMEM)
VMEM = pl.BlockSpec(memory_space=pltpu.VMEM)


def nn(a, b):
    return lax.dot_general(a, b, (((1,), (0,)), ((), ())), preferred_element_type=f32)


def nt(a, b):
    return lax.dot_general(a, b, (((1,), (1,)), ((), ())), preferred_element_type=f32)


def tn(a, b):
    return lax.dot_general(a, b, (((0,), (0,)), ((), ())), preferred_element_type=f32)


def params(**more):
    return pltpu.CompilerParams(vmem_limit_bytes=VMEM_LIMIT, **more)


def cost(flops, moved):
    return pl.CostEstimate(flops=flops, bytes_accessed=moved, transcendentals=0)


def attend_kernel(tok, wq, wk, wv, vecs, aq, ak, q_o, k_o, v_o, ctx_o, lse_o):
    x = tok[...]
    q = (nn(x, wq[...]) + vecs[0:1, :].astype(f32)).astype(bf16)
    k = nn(x, wk[...]).astype(bf16)
    v = (nn(x, wv[...]) + vecs[1:2, :].astype(f32)).astype(bf16)
    q_o[...] = q
    k_o[...] = k
    v_o[...] = v
    length, width = q.shape
    lane = lax.broadcasted_iota(jnp.int32, (length, width), 1) // HD
    slot = lax.broadcasted_iota(jnp.int32, (length, 128), 1)

    def head(h, state):
        acc, scale, stat = state
        mine = lane == h
        qa = jnp.where(mine, q, aq[...])
        ka = jnp.where(mine, k, ak[...])
        va = jnp.where(mine, v, jnp.zeros_like(v))
        t = nt(qa, ka) * SCALE
        m = jnp.max(t, axis=1, keepdims=True)
        p = jnp.exp2(t - m)
        total = jnp.sum(p, axis=1, keepdims=True)
        acc = acc + nn(p.astype(bf16), va)
        return acc, jnp.where(mine, 1.0 / total, scale), jnp.where(slot == h, m + jnp.log2(total), stat)

    zero = jnp.zeros((length, width), f32)
    acc, scale, stat = lax.fori_loop(0, width // HD, head, (zero, zero, jnp.zeros((length, 128), f32)))
    ctx_o[...] = (acc * scale).astype(bf16)
    lse_o[0] = stat.T[:8]


def attend(g, tokens, w, vecs, aq, ak, length):
    rows, width = tokens.shape
    groups = width // GW
    seqs = rows // length
    col = lambda o: pl.BlockSpec((width, GW), lambda b: (0, o * groups + g))
    seq = pl.BlockSpec((length, width), lambda b: (b, 0))
    blk = pl.BlockSpec((length, GW), lambda b: (b, 0))
    act = jax.ShapeDtypeStruct((rows, GW), bf16)
    return pl.pallas_call(
        attend_kernel,
        grid=(seqs,),
        in_specs=[seq, col(0), col(1), col(2), pl.BlockSpec((16, GW), lambda b: (0, g)), blk, blk],
        out_specs=[blk, blk, blk, blk, pl.BlockSpec((1, 8, length), lambda b: (b, 0, 0))],
        out_shape=[act, act, act, act, jax.ShapeDtypeStruct((seqs, 8, length), f32)],
        compiler_params=params(),
        cost_estimate=cost(4_000_000_000, 5_000_000),
        name="attend",
    )(tokens, w, w, w, vecs, aq, ak)


def owners(at_r, own, other):
    for k in range(4):
        z = lax.rem(k + at_r[2], 4)
        for core, ref in ((at_r[3], own), (1 - at_r[3], other)):
            yield k, 2 * z + core, ref


def select_lanes(s, piece, width):
    i = lax.broadcasted_iota(jnp.int32, (128, width), 0)
    j = lax.broadcasted_iota(jnp.int32, (128, width), 1)
    return ((j == s * piece + i) & (i < piece)).astype(f32).astype(bf16)


def attend_back_kernel(mode, at_r, q_r, k_r, v_r, do_r, ctx_r, lse_r, aq, ak, tok, wq, wk, wv, dx_i, *rest):
    b = pl.program_id(0)
    last = b == pl.num_programs(0) - 1
    if mode == "plain":
        dw_o, dx_o, db_o, dw_s, delta_s = rest
    elif mode == "first":
        own_o, other_o, dx_o, db_o, dw_s, delta_s = rest
    elif mode == "second":
        _, _, own_o, other_o, dx_o, db_o, dw_s, delta_s = rest
    else:
        db0, db1, tbl, own_o, other_o, dx_o, db_o, dw_s, delta_s = rest
    q, k, v, do = q_r[...], k_r[...], v_r[...], do_r[...]
    length, width = q.shape
    lane = lax.broadcasted_iota(jnp.int32, (length, width), 1) // HD
    sel = lax.broadcasted_iota(jnp.int32, (8, width), 1) // HD == lax.broadcasted_iota(jnp.int32, (8, width), 0)
    sel = sel.astype(f32).astype(bf16)
    prod = do.astype(f32) * ctx_r[...].astype(f32)
    hi = prod.astype(bf16)
    lo = (prod - hi.astype(f32)).astype(bf16)
    delta_s[...] = nt(sel, hi) + nt(sel, lo)
    zero = jnp.zeros_like(q)

    def head(h, state):
        dq, dk, dv = state
        mine = lane == h
        qa = jnp.where(mine, q, aq[...])
        ka = jnp.where(mine, k, ak[...])
        va = jnp.where(mine, v, zero)
        p = jnp.exp2(nt(ka, qa) * SCALE - lse_r[0, pl.ds(h, 1), :])
        dp = nt(va, do)
        ds = (p * (dp - delta_s[pl.ds(h, 1), :])).astype(bf16)
        dv = dv + nn(p.astype(bf16), jnp.where(mine, do, zero))
        dk = dk + nn(ds, jnp.where(mine, q, zero))
        dq = dq + tn(ds, jnp.where(mine, k, zero))
        return dq, dk, dv

    dq, dk, dv = lax.fori_loop(0, width // HD, head, (jnp.zeros((length, width), f32),) * 3)
    dq = (dq * 0.125).astype(bf16)
    dk = (dk * 0.125).astype(bf16)
    dv = dv.astype(bf16)
    back = jnp.concatenate([dq, dk, dv], axis=1)
    dw = tn(tok[...], back)
    dx = nt(dq, wq[...]) + nt(dk, wk[...]) + nt(dv, wv[...])
    dx_o[...] = (dx_i[...].astype(f32) + dx).astype(dx_o.dtype)
    sums = jnp.sum(back.astype(f32), axis=0, keepdims=True)

    @pl.when(b == 0)
    def _():
        dw_s[...] = dw
        db_o[...] = sums

    @pl.when(b > 0)
    def _():
        dw_s[...] += dw
        db_o[...] += sums

    @pl.when(last)
    def _():
        if mode == "plain":
            for i in range(3):
                dw_o[i] = dw_s[:, i * width : (i + 1) * width].astype(bf16)
            return
        piece = dw_s.shape[0] // 8
        half, wide = piece // 2, dw_s.shape[1] // 2
        for k, s, ref in owners(at_r, own_o, other_o):
            for ab, turn in ((0, at_r[1]), (1, at_r[0])):
                row = pl.multiple_of(s * piece + ab * half, 16)
                for h in range(2):
                    val = dw_s[pl.ds(row, half), h * wide : (h + 1) * wide]
                    ref[ab, lax.rem(h + turn, 2), k, 0:half] = val.astype(bf16)

        if mode == "third":
            sums = [r[...] for r in (db0, db1, db_o)]
            dbq = jnp.concatenate([r[:, :width] for r in sums], axis=1)
            dbv = jnp.concatenate([r[:, 2 * width :] for r in sums], axis=1)
            table = jnp.concatenate([dbq, dbv, tbl[...]], axis=0).astype(bf16)
            extra = jnp.zeros((4, 16, wide), bf16)
            for ab in range(2):
                for h in range(2):
                    own_o[ab, h, :, half : half + 16, :] = extra
                    other_o[ab, h, :, half : half + 16, :] = extra
            for k, s, ref in owners(at_r, own_o, other_o):
                blk = nt(table, select_lanes(s, piece, table.shape[1])).astype(bf16)
                ref[0, at_r[1], k, half : half + 16, 0:128] = blk


def attend_back(mode, g, at, saved, gc, aq, ak, tokens, w, dx, length, extra=()):
    rows, width = tokens.shape
    groups = width // GW
    seqs = rows // length
    half = width // 16
    col = lambda o: pl.BlockSpec((width, GW), lambda b: (0, o * groups + g))
    seq = pl.BlockSpec((length, width), lambda b: (b, 0))
    blk = pl.BlockSpec((length, GW), lambda b: (b, 0))
    whole = lambda s: pl.BlockSpec(s, lambda b: (0,) * len(s))
    S = jax.ShapeDtypeStruct
    tall = {"first": 2 * half, "second": 2 * half, "third": half + 16, "plain": 0}[mode]
    at_row = 1 if mode == "second" else 0
    block = half + 16 if mode == "third" else half
    part = pl.BlockSpec((2, 2, 4, block, 3 * GW // 2), lambda b: (0, 0, 0, at_row, 0))
    if mode == "plain":
        out_specs, out_shape = [whole((3, width, GW))], [S((3, width, GW), bf16)]
    else:
        out_specs, out_shape = [part, part], [S((2, 2, 4, tall, 3 * GW // 2), bf16)] * 2
    out_specs += [seq, whole((1, 3 * GW))]
    out_shape += [S((rows, width), bf16 if mode == "third" or g == groups - 1 else f32), S((1, 3 * GW), f32)]
    in_specs = [SMEM, blk, blk, blk, pl.BlockSpec((length, GW), lambda b: (b, g)), blk]
    in_specs += [pl.BlockSpec((1, 8, length), lambda b: (b, 0, 0)), blk, blk, seq, col(0), col(1), col(2), seq]
    aliases = {}
    if mode == "second":
        in_specs += [pl.BlockSpec(memory_space=pl.ANY)] * 2
        aliases = {len(in_specs) - 2: 0, len(in_specs) - 1: 1}
    elif mode == "third":
        in_specs += [whole(e.shape) for e in extra]
    q, k, v, ctx, lse = saved
    return pl.pallas_call(
        functools.partial(attend_back_kernel, mode),
        grid=(seqs,),
        in_specs=in_specs,
        out_specs=out_specs,
        out_shape=out_shape,
        scratch_shapes=[pltpu.VMEM((width, 3 * GW), f32), pltpu.VMEM((8, length), f32)],
        input_output_aliases=aliases,
        compiler_params=params(),
        cost_estimate=cost(8_000_000_000, 8_000_000),
        name="attend_back",
    )(at, q, k, v, gc, ctx, lse, aq, ak, tokens, w, w, w, dx, *extra)


def masks(segment_ids, valid):
    code = (segment_ids + 8 * valid).reshape(-1, 1)
    lane = lax.broadcasted_iota(jnp.int32, (1, GW), 1) % HD
    same = code == lane
    aq = same.astype(bf16)
    ak = jnp.where((lane < 16) & ~same, -BIG, 0.0).astype(bf16)
    return aq, ak


def phi(x):
    return 0.5 * (1.0 + lax.erf(x * 0.7071067811865476)), jnp.exp(-0.5 * x * x) * 0.3989422804014327


def middle_kernel(groups, split, at_r, tok, *refs):
    ctx_r = refs[:groups]
    cot, vecs, bu = refs[groups : groups + 3]
    refs = refs[groups + 3 :]
    i = pl.program_id(0)
    if split:
        up_parts, down_parts, refs = refs[:8], refs[8:16], refs[16:]
        wu, wd, wo = refs[-3:]
        refs = refs[:-3]

        @pl.when(i == 0)
        def _():
            assemble_quarter_kernel(at_r, *up_parts, wu)
            assemble_half_kernel(split, at_r, *down_parts, wd, wo)

    else:
        wu, wd, wo, refs = *refs[:3], refs[3:]
    out_o, low_o, hid_o, gd_o, gu_o, gb_o, gc_o, vec_o, bup_o, slope = refs
    width = tok.shape[1]
    ff = bu.shape[1]
    step = width
    chunks = ff // step
    bo, g1, s1, bd, g2, s2 = (vecs[j : j + 1, :].astype(f32) for j in range(2, 8))
    ctx = jnp.concatenate([r[...] for r in ctx_r], axis=1)
    pre = tok[...].astype(f32) + nn(ctx, wo[...]) + bo
    mean = lambda v: jnp.mean(v, axis=1, keepdims=True)
    centre = pre - mean(pre)
    r1 = lax.rsqrt(mean(centre * centre) + 1e-05)
    n1 = centre * r1
    normed = n1 * g1 + s1
    low = normed.astype(bf16)
    low_o[...] = low

    def forward(c, acc):
        cols = pl.ds(pl.multiple_of(c * step, 128), step)
        hp = nn(low, wu[:, cols]) + bu[:, cols].astype(f32)
        cdf, pdf = phi(hp)
        slope[:, cols] = cdf + hp * pdf
        hid = (hp * cdf).astype(bf16)
        hid_o[:, cols] = hid
        return acc + nn(hid, wd[cols, :])

    acc = lax.fori_loop(0, chunks, forward, normed + bd)
    centre = acc - mean(acc)
    r2 = lax.rsqrt(mean(centre * centre) + 1e-05)
    n2 = centre * r2
    out_o[...] = (n2 * g2 + s2).astype(bf16)
    ct = cot[...].astype(f32)
    e = ct * g2
    gp2 = r2 * (e - mean(e) - n2 * mean(e * n2))
    gd = gp2.astype(bf16)
    gd_o[...] = gd
    acc = gp2
    total = lambda v: jnp.sum(v, axis=0, keepdims=True)

    def put(ref, at, v):
        @pl.when(i == 0)
        def _():
            ref[at] = v

        @pl.when(i > 0)
        def _():
            ref[at] += v

    def backward(c, acc):
        cols = pl.ds(pl.multiple_of(c * step, 128), step)
        gu = (nt(gd, wd[cols, :]) * slope[:, cols]).astype(bf16)
        gu_o[:, cols] = gu
        put(bup_o, (slice(0, 1), cols), total(gu.astype(f32)))
        return acc + nt(gu, wu[:, cols])

    acc = lax.fori_loop(0, chunks, backward, acc)
    e = acc * g1
    gp1 = r1 * (e - mean(e) - n1 * mean(e * n1))
    gb = gp1.astype(bf16)
    gb_o[...] = gb
    gc_o[...] = nt(gb, wo[...]).astype(bf16)
    for at, v in enumerate((gb.astype(f32), acc * n1, acc, gd.astype(f32), ct * n2, ct)):
        put(vec_o, (slice(at, at + 1), slice(None)), total(v))


def middle(at, tokens, ctx, cot, vecs, bu, weights, split=None, tile=256):
    rows, width = tokens.shape
    ff = bu.shape[1]
    act = pl.BlockSpec((tile, width), lambda i: (i, 0))
    wide = pl.BlockSpec((tile, ff), lambda i: (i, 0))
    whole = lambda a: pl.BlockSpec(a.shape, lambda i: (0,) * a.ndim, pipeline_mode=pl.Buffered(1))
    S = jax.ShapeDtypeStruct
    shapes = [(rows, width), (rows, width), (rows, ff), (rows, width), (rows, ff), (rows, width), (rows, width)]
    scratch = [pltpu.VMEM((tile, ff), f32)]
    if split:
        scratch += [pltpu.VMEM(s, bf16) for s in ((width, ff), (ff, width), (width, width))]
    blocks = [pl.BlockSpec((tile, GW), lambda i: (i, 0)) for _ in ctx]
    return pl.pallas_call(
        functools.partial(middle_kernel, len(ctx), split),
        grid=(rows // tile,),
        in_specs=[SMEM, act] + blocks + [act] + [whole(a) for a in (vecs, bu) + weights],
        out_specs=[act, act, wide, act, wide, act, act, pl.BlockSpec((8, width), lambda i: (0, 0)), pl.BlockSpec((8, ff), lambda i: (0, 0))],
        out_shape=[S(s, bf16) for s in shapes] + [S((8, width), f32), S((8, ff), f32)],
        scratch_shapes=scratch,
        compiler_params=params(),
        cost_estimate=cost(30_000_000_000, 40_000_000),
        name="middle",
    )(at, tokens, *ctx, cot, vecs, bu, *weights)


def grad_down_kernel(groups, at_r, *refs):
    ctx = refs[:groups]
    gb, hid, gd, own_o, other_o, res_s = refs[groups:]
    p = pl.program_id(0)
    turns = ((0, at_r[1]), (1, at_r[0]))
    wide = gd.shape[1] // 2
    tall = hid.shape[1] // 2

    @pl.when(p == 0)
    def _():
        lhs = jnp.concatenate([r[...] for r in ctx], axis=1)
        res_s[...] = tn(lhs, gb[...]).astype(bf16)
        piece = res_s.shape[0] // 8
        half = piece // 2
        for k, s, ref in owners(at_r, own_o, other_o):
            for ab, turn in turns:
                row = pl.multiple_of(s * piece + ab * half, 16)
                for h in range(2):
                    ref[ab, lax.rem(h + turn, 2), k, tall : tall + half] = res_s[pl.ds(row, half), h * wide : (h + 1) * wide]

    @pl.when(p > 0)
    def _():
        res = tn(hid[...], gd[...]).astype(bf16)
        kk = lax.rem(p - 1, 4)
        for ab, turn in turns:
            for h in range(2):
                val = res[ab * tall : (ab + 1) * tall, h * wide : (h + 1) * wide]
                rel = lax.rem(h + turn, 2)
                for ref, cond in ((other_o, p < 5), (own_o, p >= 5)):

                    @pl.when(cond)
                    def _(val=val, rel=rel, ab=ab, ref=ref):
                        ref[ab, rel, kk, 0:tall] = val


def grad_down(at, ctx, gb, hid, gd):
    rows, ff = hid.shape
    width = gd.shape[1]
    piece = ff // 8
    part = (2, 2, 4, (piece + width // 8) // 2, width // 2)

    def owner(p, at_r):
        j = jnp.maximum(p - 1, 0)
        z = lax.rem(at_r[2] + lax.rem(j, 4), 4)
        return 0, 2 * z + jnp.where(j < 4, 1 - at_r[3], at_r[3])

    whole = lambda s: pl.BlockSpec(s, lambda p, at_r: (0,) * len(s))
    return pl.pallas_call(
        functools.partial(grad_down_kernel, len(ctx)),
        grid_spec=pltpu.PrefetchScalarGridSpec(
            num_scalar_prefetch=1,
            grid=(9,),
            in_specs=[whole(c.shape) for c in ctx] + [whole(gb.shape), pl.BlockSpec((rows, piece), owner), whole(gd.shape)],
            out_specs=[whole(part), whole(part)],
            scratch_shapes=[pltpu.VMEM((width, width), bf16)],
        ),
        out_shape=[jax.ShapeDtypeStruct(part, bf16)] * 2,
        compiler_params=params(),
        cost_estimate=cost(9_000_000_000, 14_000_000),
        name="grad_down",
    )(at, *ctx, gb, hid, gd)


def grad_up_kernel(at_r, low, gu, own_o, other_o, turned, res_s):
    j = pl.program_id(0)
    y, x = at_r[0], at_r[1]

    @pl.when(j == 0)
    def _():
        turned[...] = low[...].T

    res_s[...] = nn(turned[...], gu[...]).astype(bf16)
    piece = res_s.shape[0] // 8
    half = piece // 2
    h, l = j // 4, lax.rem(j // 2, 2)
    to = pl.multiple_of(lax.rem(j, 2) * half, 16)
    for k, s, ref in owners(at_r, own_o, other_o):
        for ab, turn, other_turn in ((0, x, y), (1, y, x)):
            row = pl.multiple_of(s * piece + ab * half, 16)
            one, two = lax.rem(h + turn, 2), lax.rem(l + other_turn, 2)
            ref[ab, one, two, k, pl.ds(to, half), :] = res_s[pl.ds(row, half), :]


def grad_up(at, low, gu):
    rows, width = low.shape
    ff = gu.shape[1]
    step = ff // 8
    part = (2, 2, 2, 4, width // 8, ff // 8)
    whole = pl.BlockSpec(part, lambda j: (0, 0, 0, 0, 0, 0))
    return pl.pallas_call(
        grad_up_kernel,
        grid=(8,),
        in_specs=[SMEM, pl.BlockSpec((rows, width), lambda j: (0, 0)), pl.BlockSpec((rows, step), lambda j: (0, j))],
        out_specs=[whole, whole],
        out_shape=[jax.ShapeDtypeStruct(part, bf16)] * 2,
        scratch_shapes=[pltpu.VMEM((width, rows), bf16), pltpu.VMEM((width, step), bf16)],
        compiler_params=params(),
        cost_estimate=cost(9_000_000_000, 14_000_000),
        name="grad_up",
    )(at, low, gu)


AXES = ("rep", "shard")


def pairs(move):
    found = []
    for y in range(2):
        for x in range(2):
            for z in range(4):
                for c in range(2):
                    j, i, k, d = move(y, x, z, c)
                    found.append(((y * 2 + x) * 8 + z * 2 + c, (j * 2 + i) * 8 + k * 2 + d))
    return found


CORE = pairs(lambda y, x, z, c: (y, x, z, 1 - c))
ACROSS = pairs(lambda y, x, z, c: (y, 1 - x, z, c))
ALONG = pairs(lambda y, x, z, c: (1 - y, x, z, c))
SHIFT = [None] + [pairs(lambda y, x, z, c, n=n: (y, x, (z + n) % 4, c)) for n in (1, 2, 3)]


def send(a, where):
    return lax.ppermute(a, AXES, where)


def tie(values, *after):
    flat, tree = jax.tree.flatten(values)
    return jax.tree.unflatten(tree, lax.optimization_barrier(tuple(flat) + tuple(jax.tree.leaves(after)))[: len(flat)])


def place(own, received, at_r, rows, out, base, quarter):
    y, x, z = at_r[0], at_r[1], at_r[2]
    cols = out.shape[1]
    half = rows // 2
    out[pl.ds(pl.multiple_of(base(z), 16), rows), :] = own
    for k in range(1, 4):
        start = base(lax.rem(z - k + 4, 4))
        for ab in range(2):
            at = pl.ds(pl.multiple_of(start + ab * half, 16), half)
            if quarter:
                wide = cols // 4
                for i in range(2):
                    for l in range(2):
                        one, two = (i, l) if ab == 0 else (l, i)
                        col = (lax.rem(x + i, 2) * 2 + lax.rem(y + l, 2)) * wide
                        out[at, pl.ds(pl.multiple_of(col, 128), wide)] = received(ab, one, two, k)
            else:
                wide = cols // 2
                for one in range(2):
                    col = lax.rem((x, y)[ab] + one, 2) * wide
                    out[at, pl.ds(pl.multiple_of(col, 128), wide)] = received(ab, one, 0, k)


def assemble_half_kernel(out_rows, at_r, *refs):
    n = len(out_rows)
    outs = refs[-n:]
    c = at_r[3]
    for turn, (own, ring, far_x, far_y) in ((c, refs[:4]), (1 - c, refs[4:8])):
        off = 0
        total_half = sum(out_rows) // 2
        for out, rows in zip(outs, out_rows):
            half = rows // 2

            def received(ab, one, two, k):
                if one == 0:
                    return ring[k - 1, ab * total_half + off : ab * total_half + off + half, :]
                return (far_x, far_y)[ab][k - 1, off : off + half, :]

            whole = jnp.concatenate([own[off : off + half], own[total_half + off : total_half + off + half]], axis=0)
            place(whole, received, at_r, rows, out, lambda z: (2 * z + turn) * rows, False)
            off += half


def assemble_quarter_kernel(at_r, *refs):
    out = refs[-1]
    c = at_r[3]
    for turn, (own, near_a, near_b, far) in ((c, refs[:4]), (1 - c, refs[4:8])):
        rows = own.shape[0]

        def received(ab, one, two, k):
            if two == 1:
                return far[ab, one, k - 1]
            return (near_a, near_b)[ab][one, k - 1]

        place(own[...], received, at_r, rows, out, lambda z: (2 * z + turn) * rows, True)


def assemble(kernel, at, parts, shapes):
    return pl.pallas_call(
        kernel,
        in_specs=[SMEM] + [VMEM] * len(parts),
        out_specs=[VMEM] * len(shapes),
        out_shape=[jax.ShapeDtypeStruct(s, bf16) for s in shapes],
        compiler_params=params(),
        cost_estimate=cost(0, sum(4 * s[0] * s[1] for s in shapes)),
        name="assemble",
    )(at, *parts)


def halves(w, x, y):
    half, wide = w.shape[0] // 2, w.shape[1] // 2
    a = lax.dynamic_slice(w, (0, x * wide), (half, wide))
    b = lax.dynamic_slice(w, (half, y * wide), (half, wide))
    return jnp.concatenate([a, b], axis=0)


def spread_half(ring, half):
    return send(ring[:, :half], ACROSS), send(ring[:, half : 2 * half], ALONG)


def swap(parts):
    return tuple(send(p, CORE) for p in parts)


def total(*terms):
    out = terms[0].astype(f32)
    for t in terms[1:]:
        out = out + t.astype(f32)
    return out.astype(bf16)


def finish_kernel(kind, at_r, *refs):
    y, x = at_r[0], at_r[1]
    blocks, outs = refs[:4], refs[4:]
    for ab, turn, other_turn in ((0, x, y), (1, y, x)):
        one, two = (blocks[2 * ab + i][...].astype(f32) for i in range(2))
        left = jnp.where(turn == 0, one, two)
        right = jnp.where(turn == 0, two, one)
        both = jnp.concatenate([left, right], axis=1)
        if kind == "ffn":
            off = 0
            for out in outs[:2]:
                half = out.shape[0] // 2
                out[ab * half : (ab + 1) * half, :] = both[off : off + half]
                off += half
            half = outs[2].shape[0] // 2
            eighth = left.shape[1]
            for h, val in ((0, left), (1, right)):
                near, far = val[off : off + 2 * half], val[off + 2 * half : off + 4 * half]
                quarters = jnp.where(other_turn == 0, near, far), jnp.where(other_turn == 0, far, near)
                for i in range(4):
                    row, col = i % 2 * half, (4 * h + i) * eighth
                    outs[2][ab * half : (ab + 1) * half, col : col + eighth] = quarters[i // 2][row : row + half]
        else:
            half = outs[0].shape[0] // 2
            groups = outs[0].shape[1] // (3 * GW)
            for g in range(groups):
                for i in range(3):
                    col = (i * groups + g) * GW
                    outs[0][ab * half : (ab + 1) * half, col : col + GW] = both[g * half : (g + 1) * half, i * GW : (i + 1) * GW]
            if ab == 0:
                small = left[groups * half : groups * half + 16]
                piece = outs[1].shape[1]
                outs[1][...] = small[:2, :piece]
                for i in range(6):
                    outs[2 + i][...] = small[2 + i : 3 + i, :piece]
                outs[8][...] = jnp.concatenate([small[8 + i : 9 + i, :piece] for i in range(4)], axis=1)


def finish(at, kind, blocks, shapes):
    return pl.pallas_call(
        functools.partial(finish_kernel, kind),
        in_specs=[SMEM] + [VMEM] * len(blocks),
        out_specs=[VMEM] * len(shapes),
        out_shape=[jax.ShapeDtypeStruct(s, f32) for s in shapes],
        compiler_params=params(),
        cost_estimate=cost(0, 4_000_000),
        name="finish_" + kind,
    )(at, *blocks)


def pack(vectors, wide):
    block = jnp.concatenate([v.reshape(-1, vectors[1].shape[0]) for v in vectors] + [wide.reshape(4, -1)], axis=0)
    return jnp.pad(block, ((0, 16 - block.shape[0]), (0, 128 - block.shape[1])))


def whole_vectors(every, z, c, piece):
    k = lax.broadcasted_iota(jnp.int32, (2, 4, 8), 1)
    d = lax.broadcasted_iota(jnp.int32, (2, 4, 8), 0)
    s = lax.broadcasted_iota(jnp.int32, (2, 4, 8), 2)
    pick = (s == 2 * ((z - k) % 4) + (c + d) % 2).astype(bf16)
    table = jnp.einsum("dks,dkrl->srl", pick, every, preferred_element_type=f32).astype(bf16)
    table = table[:, :, :piece]
    wide = table[:, 8:12].reshape(1, -1)
    return table.transpose(1, 0, 2).reshape(16, -1), wide


class Sum:
    def __init__(self):
        self.own, self.got = [], []

    def add(self, own, other):
        self.own.append(own)
        self.got.append(send(other, CORE))

    def after(self, *values):
        self.got, self.far, self.parts, self.rest = tie((self.got, self.far, self.parts, self.rest), *values)

    far = parts = ()

    def pair(self, pick, *more):
        found = [total(pick(o), pick(g)) for o, g in zip(self.own, self.got)]
        found = found[0] if len(found) == 1 else jnp.concatenate(found, axis=-2)
        return total(found, *more) if more else found

    def halve(self):
        self.sent = self.pair(lambda a: a[0, 1]), self.pair(lambda a: a[1, 1])
        self.far = send(self.sent[0], ACROSS), send(self.sent[1], ALONG)

    def along_z(self):
        self.mine = [jnp.stack([self.near(i, k) for i in range(2)]) for k in range(4)]
        self.sent = self.mine[1:]
        self.far = ()
        self.parts = [send(self.mine[k], SHIFT[k]) for k in range(1, 4)]

    def joined(self, i):
        one, two, rows = self.sent[i], self.far[i], self.rows
        summed = total(one[:rows], two[:rows])
        return jnp.concatenate([summed, one[rows:], two[rows:]], axis=0)

    rest = ()

    def near(self, i, k):
        if self.rest:
            return total(self.rest[i][k], self.far[i][k])
        terms = []
        at = 0
        for o, g in zip(self.own, self.got):
            rows = o.shape[3]
            terms.append(total(o[i, 0, k], g[i, 0, k], self.far[i][k, at : at + rows]))
            at += rows
        return terms[0] if len(terms) == 1 else jnp.concatenate(terms, axis=0)

    def quarter(self):
        own, got, far = self.own[0], self.got[0], self.far
        part = lambda i, j: total(own[i, 0, j], got[i, 0, j], far[i][j])
        self.sent = part(0, 1), part(1, 1)
        self.rest = part(0, 0), part(1, 0)
        self.far = send(self.sent[0], ALONG), send(self.sent[1], ACROSS)

    def across(self, more=None):
        both = total(self.mine[0], *self.parts)
        rows = both.shape[1]
        if more is not None:
            extra = total(more.mine[0], *more.parts)
            both = jnp.concatenate([both, extra], axis=1)
        self.got = self.parts = ()
        self.sent = both[0], both[1]
        self.far = send(both[0], ALONG), send(both[1], ACROSS)
        self.rows = rows

    def share(self):
        a, b = (self.joined(i) for i in range(2))
        self.sent = a, b
        self.out = a, send(a, ACROSS), b, send(b, ALONG)


def shards_near(
    tokens,
    cotangent,
    qkv_weight,
    query_value_bias,
    out_weight,
    out_bias,
    norm_one_gain,
    norm_one_shift,
    up_weight,
    up_bias,
    down_weight,
    down_bias,
    norm_two_gain,
    norm_two_shift,
    segment_ids,
    valid,
):
    length = segment_ids.shape[1]
    width = tokens.shape[1]
    groups = width // GW
    ff = up_bias.shape[0] * 8
    piece = out_bias.shape[0]
    r, s = lax.axis_index("rep"), lax.axis_index("shard")
    y, x, z, c = r // 2, r % 2, s // 2, s % 2
    at = jnp.stack([y, x, z, c]).astype(jnp.int32)

    half = piece // 2
    block = pack(
        (query_value_bias, out_bias, norm_one_gain, norm_one_shift, down_bias, norm_two_gain, norm_two_shift), up_bias
    )
    lines = lambda n, cols: jnp.pad(block.reshape(n, -1), ((0, 8 - n), (0, cols - 2048 // n)))
    dr = down_weight.shape[0] // 2
    own_q = jnp.concatenate([qkv_weight, lines(1, 3 * width)], axis=0)
    own_d = jnp.concatenate([down_weight[:dr], out_weight[:half], down_weight[dr:], out_weight[half:]], axis=0)
    other_q, other_u, other_d = swap((own_q, up_weight, own_d))
    held = jnp.concatenate([halves(qkv_weight, x, y), lines(2, 3 * width // 2)], axis=0)
    ring = []
    for step in range(3):
        if step == 2:
            held = tie(held, other_q, other_u, other_d)
        held = send(held, SHIFT[1])
        ring.append(held)
    ring_q = jnp.stack(ring)
    far_q = spread_half(ring_q, half)
    first_u = lax.dynamic_slice(up_weight, (0, (2 * x + y) * (ff // 4)), (piece, ff // 4))
    first_u = tie(first_u, held)
    ring_u = [send(first_u, SHIFT[k]) for k in range(1, 4)]
    rest_q = swap(tie((ring_q,) + far_q, ring_u))
    swapped_q = rest_q[0]
    parts_q = (own_q, ring_q) + far_q + (other_q,) + rest_q
    (wqkv,) = assemble(
        functools.partial(assemble_half_kernel, [qkv_weight.shape[0]]), at, parts_q, [(width, 3 * width)]
    )
    blocks = lambda own, ring: jnp.concatenate([own[None, piece : piece + 1, :2048].reshape(1, 16, 128), ring[:, piece : piece + 2, :1024].reshape(3, 16, 128)])
    vecs, bu = whole_vectors(jnp.stack([blocks(own_q, ring_q), blocks(other_q, swapped_q)]), z, c, piece)

    aq, ak = masks(segment_ids, valid)
    ring_u = jnp.stack(tie(ring_u, far_q))
    first_d = tie(halves(own_d, x, y), ring_u)
    d2 = send(first_d, SHIFT[2])
    a, b = ring_u[:, :half], ring_u[:, half:]
    a2, b2 = send(a, ACROSS), send(b, ALONG)
    saved = [attend(0, tie(tokens, a, b, first_d), wqkv, vecs, aq, ak, length)]
    a2, b2, d2, first_d = tie((a2, b2, d2, first_d), saved[0][3])
    a3, b3 = jnp.stack([a, a2]), jnp.stack([b, b2])
    a4, b4 = send(a3, ALONG), send(b3, ACROSS)
    d1, d3 = send(first_d, SHIFT[1]), send(first_d, SHIFT[3])
    other_a = send(a3, CORE)
    saved.append(attend(1, tie(tokens, a3, b3, d2), wqkv, vecs, aq, ak, length))
    a4, b4, other_a, ring_d = tie((a4, b4, other_a, [d1, d2, d3]), saved[1][3])
    ring_d = jnp.stack(ring_d)
    ab4 = jnp.stack([a4, b4])
    far_d = spread_half(ring_d, dr + half)
    other_b, other_ab, other_ring = swap((b3, ab4, ring_d))
    saved.append(attend(2, tie(tokens, ring_d, ab4), wqkv, vecs, aq, ak, length))
    far_d, other_b, other_ab, other_ring = tie((far_d, other_b, other_ab, other_ring), saved[2][3])
    parts_u = (up_weight, a3, b3, ab4, other_u, other_a, other_b, other_ab)
    parts_d = (own_d, ring_d) + far_d + (other_d, other_ring) + swap(far_d)

    ctx = [f[3] for f in saved]
    result, low, hid, gd, gu, gb, gc, vec, bup = middle(
        at, tokens, ctx, cotangent, vecs, bu, parts_u + parts_d, (2 * dr, piece)
    )

    down, up, qkv = Sum(), Sum(), Sum()
    own, other = grad_down(at, ctx, gb, hid, gd)
    down.add(own, other)
    own, other = grad_up(at, *tie((low, gu), other))
    up.add(own, other)
    down.after(other)
    down.halve()
    own, other, dx, db0 = attend_back("first", 0, at, saved[0], tie(gc, down.sent, other), aq, ak, tokens, wqkv, gb, length)
    down.after(dx)
    up.after(dx)
    down.along_z()
    up.halve()
    dx = tie(dx, down.sent, up.sent)
    own, other, dx, db1 = attend_back("second", 1, at, saved[1], gc, aq, ak, tokens, wqkv, dx, length, (own, other))
    two = own, other
    up.after(dx)
    up.quarter()
    wide = bup[0].reshape(8, 4, piece).transpose(1, 0, 2).reshape(4, width)
    table = jnp.concatenate([vec[:6], wide, jnp.zeros((4, width), f32)], axis=0)
    own, other, dx, _ = attend_back(
        "third", 2, at, saved[2], gc, aq, ak, tokens, wqkv, tie(dx, up.sent), length, (db0, db1, table)
    )
    down.after(dx)
    up.after(dx)
    other, first_other = tie((other, two[1]), up.far)
    qkv.add(two[0], first_other)
    qkv.add(own, other)
    up.after(down.parts)
    up.along_z()
    qkv.halve()
    up.after(qkv.far)
    qkv.after(up.parts)
    qkv.along_z()
    down.across(up)
    down.share()
    dwd, dwo, dwu = finish(at, "ffn", down.out, [down_weight.shape, out_weight.shape, up_weight.shape])
    qkv.after(dwd, dwo, dwu)
    qkv.across()
    qkv.share()
    dwq, dqv, *ones, dbu = finish(at, "qkv", qkv.out, [qkv_weight.shape, (2, piece)] + 6 * [(1, piece)] + [(1, 4 * piece)])
    one = lambda i: ones[i - 2].reshape(piece)
    return (
        result,
        dx,
        dwq,
        dqv,
        dwo,
        one(2),
        one(3),
        one(4),
        dwu,
        dbu.reshape(-1),
        dwd,
        one(5),
        one(6),
        one(7),
    )


def spread(args):
    flat = [a.reshape(-1) for a in args]
    packed = jnp.concatenate(flat)
    every = lax.all_gather(packed, "shard", axis=0)
    out, at = [], 0
    for a in args:
        part = every[:, at : at + a.size].reshape((-1,) + a.shape)
        at += a.size
        out.append(jnp.moveaxis(part, 0, -2).reshape(a.shape[:-1] + (-1,)))
    return out


def shards(
    tokens,
    cotangent,
    qkv_weight,
    query_value_bias,
    out_weight,
    out_bias,
    norm_one_gain,
    norm_one_shift,
    up_weight,
    up_bias,
    down_weight,
    down_bias,
    norm_two_gain,
    norm_two_shift,
    segment_ids,
    valid,
):
    length = segment_ids.shape[1]
    width = tokens.shape[1]
    groups = width // GW
    gather = lambda a: lax.all_gather(a, "shard", axis=0, tiled=True)
    *rest, bu = spread(
        (query_value_bias, out_bias, norm_one_gain, norm_one_shift, down_bias, norm_two_gain, norm_two_shift, up_bias)
    )
    vecs = jnp.concatenate([v.reshape(-1, width) for v in rest] + [jnp.zeros((8, width), bf16)], axis=0)
    wqkv, wd, wo, wu = gather(qkv_weight), gather(down_weight), gather(out_weight), gather(up_weight)
    at = jnp.zeros((4,), jnp.int32)
    aq, ak = masks(segment_ids, valid)
    saved = [attend(g, tokens, wqkv, vecs, aq, ak, length) for g in range(groups)]
    ctx = [f[3] for f in saved]
    result, low, hid, gd, gu, gb, gc, vec, bup = middle(at, tokens, ctx, cotangent, vecs, bu[None], (wu, wd, wo))
    dwd = tn(hid, gd).astype(bf16)
    dwu = tn(low, gu).astype(bf16)
    dwo = tn(jnp.concatenate(ctx, axis=1), gb).astype(bf16)
    dx, dws, dbs = gb, [], []
    for g in range(groups):
        dw, dx, db = attend_back("plain", g, at, saved[g], gc, aq, ak, tokens, wqkv, dx, length)
        dws.append(dw)
        dbs.append(db)
    dwq = jnp.concatenate([dw[i] for i in range(3) for dw in dws], axis=1)
    db = jnp.stack(dbs).reshape(groups, 3, GW).transpose(1, 0, 2).reshape(3, width)
    small = jnp.concatenate([db[0], db[2], vec[:6].reshape(-1), bup[0]])
    small = lax.psum(small.reshape(-1, 128), ("rep", "shard")).reshape(-1)

    def owned(a):
        part = lax.psum_scatter(a, "shard", scatter_dimension=0, tiled=True)
        return lax.psum(part, "rep").astype(f32)

    rank = lax.axis_index("shard")
    own = lambda at, size: lax.dynamic_slice(small, (at + rank * size,), (size,))
    piece = out_bias.shape[0]
    vs = [own(width * i, piece) for i in range(8)]
    dbu = own(8 * width, up_bias.shape[0])
    gd_w, gu_w, go_w, gq_w = owned(dwd), owned(dwu), owned(dwo), owned(dwq)
    return result, dx, gq_w, jnp.stack(vs[:2]), go_w, vs[2], vs[3], vs[4], gu_w, dbu, gd_w, vs[5], vs[6], vs[7]


def solution(mesh):
    rows, one = P(("rep", "shard"), None), P("shard")
    mat, two = P("shard", None), P(None, "shard")
    near = mesh.shape["rep"] == 4 and mesh.shape["shard"] == 8
    return jax.shard_map(
        shards_near if near else shards,
        mesh=mesh,
        in_specs=(rows, rows, mat, two, mat, one, one, one, mat, one, mat, one, one, one, rows, rows),
        out_specs=(rows, rows, mat, two, mat, one, one, one, mat, one, mat, one, one, one),
        check_vma=False,
    )
```
